32 devices in a mesh: groups: 2 (over y), tile: 4 (over z), image: 4 (over x, core).
Axes of the slice: x: 2, y: 2, z: 4, core: 2. Of those that a mesh axis runs over, the one named last changes fastest.
Arguments:
- images: bfloat16 [8, 16, 64, 256], P(('groups', 'image'), 'tile'), parts along dimension 0, may hold values from -12 to 12
- cotangent: bfloat16 [8, 16, 64, 256], P(('groups', 'image'), 'tile'), parts along dimension 0, may hold values from -12 to 12
- timesteps: int32 [8], P(('groups', 'image')), parts along dimension 0, may hold values from 0 to 999
- class_ids: int32 [8], P(('groups', 'image')), parts along dimension 0, may hold values from 0 to 999
- norm_gain: float32 [256], replicated, may hold values from 0.25 to 1.75
- norm_bias: float32 [256], replicated, may hold values from -3 to 3
- conv_first: bfloat16 [3, 3, 256, 256], replicated, may hold values from -0.125 to 0.125
- conv_second: bfloat16 [3, 3, 256, 256], replicated, may hold values from -0.125 to 0.125
- time_weight: bfloat16 [256, 1024], P(None, 'tile'), may hold values from -0.375 to 0.375
- time_bias: float32 [1024], P('tile'), may hold values from -3 to 3
- class_table: bfloat16 [1000, 1024], P(None, 'tile'), may hold values from -5 to 5
- adaptive_weight: bfloat16 [1024, 512], P('tile'), may hold values from -0.1875 to 0.1875
- adaptive_bias: float32 [512], replicated, may hold values from -2 to 2
Outputs:
- branch: bfloat16 [8, 16, 64, 256], P(('groups', 'image'), 'tile'), parts along dimension 0
- input_grad: bfloat16 [8, 16, 64, 256], P(('groups', 'image'), 'tile'), parts along dimension 0
- grad_adaptive_weight: float32 [2048, 512], P(('groups', 'tile')), parts along dimension 0
- grad_adaptive_bias: float32 [1024], P('groups'), parts along dimension 0
The draws below stay inside these ranges and needn't reach their ends.
There are 2 independent parts, one for each index of `groups`. The reference program is written for one: setup_inputs(seed, part) draws one part's arguments, and reference() takes and returns one part's arrays. A program takes and returns all parts, laid end to end along the dimension named above; an argument that names none is the same for every part. Nothing has to cross between parts.
All inputs are finite; a program needn't handle non-finite values.
Results may differ from the reference program's by a relative error of at most 0.013.
Values may be sent and summed in bfloat16 or wider, within the bound.
A program may use at most 64 MiB of HBM per device.

```python
import math
import jax
import jax.numpy as jnp
from jax import lax

C = 256
EMB = 1024
FREQ = 256
CLASSES = 1000
GN_GROUPS = 32
COLS = 64
IMAGES = 4
H = 16


def scaled_field(key, offset_tag):
    folded = jax.random.fold_in(key, offset_tag)
    sample_key, row_key, chan_key = jax.random.split(folded, 3)
    extent = (IMAGES, H, COLS, C)
    sample = jnp.clip(jax.random.normal(sample_key, extent, jnp.float32), -4.0, 4.0)
    rising = 3.0 ** (jnp.arange(H, dtype=jnp.float32) / (H - 1))
    row_scale = rising[None, :] * jnp.exp(jax.random.uniform(row_key, (IMAGES, H), jnp.float32, 0.0, math.log(3.3))) / math.sqrt(10.0)
    chan_scale = jnp.exp(jax.random.uniform(chan_key, (IMAGES, C), jnp.float32, math.log(0.316), math.log(3.16)))
    return jnp.clip(sample * row_scale[:, :, None, None] * chan_scale[:, None, None, :], -12.0, 12.0)


def draw_images(key, part):
    return scaled_field(key, 11).astype(jnp.bfloat16)


def draw_cotangent(key, part):
    return scaled_field(key, 23).astype(jnp.bfloat16)


def with_ends(result, stream_key, smallest, top_value):
    spot = [jax.random.randint(jax.random.fold_in(stream_key, axis), (), 0, length) for axis, length in enumerate(result.shape)]
    main_axis = result.shape.index(max(result.shape))
    next_to = spot[:main_axis] + [(spot[main_axis] + 1) % result.shape[main_axis]] + spot[main_axis + 1:]
    return result.at[tuple(spot)].set(smallest).at[tuple(next_to)].set(top_value)


def steps_of(key, dims, cuts, least, top_value):
    def one(position, shards_of):
        heights = jax.random.uniform(jax.random.fold_in(jax.random.fold_in(key, 6), position), (shards_of,), jnp.float32, least / len(cuts), top_value / len(cuts))
        return jnp.repeat(jnp.exp(heights), dims[position] // shards_of).reshape((-1,) + (1,) * (len(dims) - position - 1))

    level = one(*cuts[0])
    for cut in cuts[1:]:
        level = level * one(*cut)
    return level


def gaussian(key, shape, width, bound, pieces=(), kind=jnp.bfloat16):
    entries = width * jax.random.normal(key, shape, jnp.float32)
    if pieces:
        entries = entries * steps_of(key, shape, pieces, -0.22, 0.18)
    return jnp.clip(entries, -bound, bound).astype(kind)


def setup_inputs(seed: int = 0, part: int = 0) -> dict:
    seeds = jax.random.split(jax.random.key(seed), 14)
    part_keys = jax.random.split(jax.random.fold_in(seeds[13], part), 14)
    images = draw_images(jax.random.fold_in(jax.random.fold_in(seeds[13], part), 71), part)
    cotangent = draw_cotangent(jax.random.fold_in(jax.random.fold_in(seeds[13], part), 71), part)
    timesteps = with_ends(jax.random.randint(part_keys[2], (IMAGES,), 0, 1000), jax.random.fold_in(part_keys[2], 1), 0, 999).astype(jnp.int32)
    class_ids = with_ends(jax.random.randint(part_keys[3], (IMAGES,), 0, CLASSES), jax.random.fold_in(part_keys[3], 1), 0, CLASSES - 1).astype(jnp.int32)
    norm_gain = jnp.clip(1.0 + 0.15 * jax.random.normal(seeds[4], (C,), jnp.float32), 0.25, 1.75)
    norm_bias = gaussian(seeds[5], (C,), 0.5, 3.0, (), jnp.float32)
    conv_first = gaussian(seeds[6], (3, 3, C, C), (9 * C) ** -0.5, 0.125)
    conv_second = gaussian(seeds[7], (3, 3, C, C), (9 * C) ** -0.5, 0.125)
    time_weight = gaussian(seeds[8], (FREQ, EMB), FREQ ** -0.5, 0.375, ((1, 4),))
    time_bias = gaussian(seeds[9], (EMB,), 0.5, 3.0, ((0, 4),), jnp.float32)
    class_table = gaussian(seeds[10], (CLASSES, EMB), 1.0, 5.0, ((1, 4),))
    adaptive_weight = gaussian(seeds[11], (EMB, 2 * C), EMB ** -0.5, 0.1875, ((0, 4),))
    adaptive_bias = gaussian(seeds[12], (2 * C,), 0.3, 2.0, (), jnp.float32)
    return {"images": images, "cotangent": cotangent, "timesteps": timesteps, "class_ids": class_ids, "norm_gain": norm_gain, "norm_bias": norm_bias, "conv_first": conv_first, "conv_second": conv_second, "time_weight": time_weight, "time_bias": time_bias, "class_table": class_table, "adaptive_weight": adaptive_weight, "adaptive_bias": adaptive_bias}


EPSILON = 1e-05

def rounded(values):
    return lax.optimization_barrier(values.astype(jnp.bfloat16)).astype(jnp.float32)

def conv_same(values, kernel):
    return lax.conv_general_dilated(values[None], kernel.astype(jnp.float32), (1, 1), 'SAME', dimension_numbers=('NHWC', 'HWIO', 'NHWC'), precision=lax.Precision.HIGHEST)[0]

def group_mean(values):
    per_group = values.reshape(-1, GN_GROUPS, C // GN_GROUPS).mean(axis=(0, 2))
    return jnp.repeat(per_group, C // GN_GROUPS)

def normalize(values):
    centred = values - group_mean(values)
    inverse = lax.rsqrt(group_mean(centred * centred) + EPSILON)
    return (centred * inverse, inverse)

def norm_backward(grad_norm, normed, inverse):
    return inverse * (grad_norm - group_mean(grad_norm) - normed * group_mean(grad_norm * normed))

def silu_grad(pre_values):
    sigma = jax.nn.sigmoid(pre_values)
    return sigma * (1.0 + pre_values * (1.0 - sigma))

def reference(images, cotangent, timesteps, class_ids, norm_gain, norm_bias, conv_first, conv_second, time_weight, time_bias, class_table, adaptive_weight, adaptive_bias):
    half_freq = FREQ // 2
    frequencies = jnp.exp(-math.log(10000.0) * jnp.arange(half_freq, dtype=jnp.float32) / half_freq)
    angles = timesteps.astype(jnp.float32)[:, None] * frequencies[None]
    sinusoid = jnp.concatenate([jnp.cos(angles), jnp.sin(angles)], axis=1)
    hidden = jnp.dot(sinusoid, time_weight.astype(jnp.float32), precision=lax.Precision.HIGHEST) + time_bias.astype(jnp.float32)
    onehot = (class_ids[:, None] == jnp.arange(CLASSES, dtype=jnp.int32)[None]).astype(jnp.float32)
    embedding = jax.nn.silu(hidden) + jnp.dot(onehot, class_table.astype(jnp.float32), precision=lax.Precision.HIGHEST)
    activated = jax.nn.silu(embedding)
    modulation = jnp.dot(activated, adaptive_weight.astype(jnp.float32), precision=lax.Precision.HIGHEST) + adaptive_bias.astype(jnp.float32)
    flipped_first = jnp.flip(conv_first, (0, 1)).transpose(0, 1, 3, 2)
    flipped_second = jnp.flip(conv_second, (0, 1)).transpose(0, 1, 3, 2)
    gain = norm_gain.astype(jnp.float32)
    bias_term = norm_bias.astype(jnp.float32)

    def one_image(inputs):
        picture, grad_out, modul_row = inputs
        normed_first, inverse_first = normalize(picture.astype(jnp.float32))
        pre_first = normed_first * gain + bias_term
        active_first = rounded(jax.nn.silu(pre_first))
        hidden_first = rounded(conv_same(active_first, conv_first))
        normed_second, inverse_second = normalize(hidden_first)
        factor = 1.0 + modul_row[:C]
        pre_second = normed_second * factor + modul_row[C:]
        active_second = rounded(jax.nn.silu(pre_second))
        branch = conv_same(active_second, conv_second).astype(jnp.bfloat16)
        grad_active = conv_same(grad_out.astype(jnp.float32), flipped_second)
        grad_pre = grad_active * silu_grad(pre_second)
        grad_scale = lax.optimization_barrier(jnp.sum(grad_pre * normed_second, axis=(0, 1)))
        grad_shift = lax.optimization_barrier(jnp.sum(grad_pre, axis=(0, 1)))
        grad_hidden = rounded(norm_backward(grad_pre * factor, normed_second, inverse_second))
        grad_active_first = conv_same(grad_hidden, flipped_first)
        grad_first = grad_active_first * silu_grad(pre_first) * gain
        input_grad = norm_backward(grad_first, normed_first, inverse_first).astype(jnp.bfloat16)
        return (branch, input_grad, jnp.concatenate([grad_scale, grad_shift]))
    branch, input_grad, pairs = lax.map(one_image, (images, cotangent, modulation))
    grad_weight = jnp.dot(activated.T, pairs, precision=lax.Precision.HIGHEST)
    grad_bias = lax.optimization_barrier(jnp.sum(pairs, axis=0))
    return (branch, input_grad, grad_weight, grad_bias)
```

```python
import functools
import math

import jax
import jax.numpy as jnp
from jax import lax
from jax.experimental import pallas as pl
from jax.experimental.pallas import tpu as pltpu
from jax.sharding import PartitionSpec as P

GN_GROUPS = 32
EPSILON = 1e-05
MESH = pl.DeviceIdType.MESH
F32 = jnp.float32
BF16 = jnp.bfloat16
GRANT = 24 << 20
REACH = 2
HIGHEST = lax.Precision.HIGHEST


def group_spread(values, width):
    count = values.shape[-1]
    lane = lax.broadcasted_iota(jnp.int32, values.shape, values.ndim - 1)
    step = 1
    while step < width:
        up = pltpu.roll(values, step, values.ndim - 1)
        down = pltpu.roll(values, count - step, values.ndim - 1)
        values = values + jnp.where((lane & step) != 0, up, down)
        step *= 2
    return values


def silu_slope(pre, sigma):
    return sigma * (1.0 + pre * (1.0 - sigma))


def column_sums(first, second):
    return jnp.concatenate(
        [jnp.sum(first, axis=0, keepdims=True), jnp.sum(second, axis=0, keepdims=True)], axis=0
    )


def kernel(
    n, m,
    steps_hbm, ids_hbm, gain_hbm, bias_hbm, tbias_hbm, abias_hbm,
    images_hbm, cot_hbm, first_hbm, second_hbm, tweight_hbm, table_hbm, aweight_hbm,
    branch, igrad, wgrad, bgrad,
    images, cot, first, second, tweight, table, aweight,
    gain_ref, bias_ref, tbias_ref, abias_ref, steps_ref, ids_ref,
    wide_first, wide_cot, wide_second, wide_hidden,
    hidden, gact, nsecond, gpre, nfirst, slope,
    slots, acts, pairs,
    load_sem, halo_send, halo_recv, send_sem, recv_sem,
    act_send, act_recv, pair_send, pair_recv,
):
    me = lax.axis_index("tile")
    mine = lax.axis_index("image")
    rows, cols, channels = images_hbm.shape[1:]
    width = channels // GN_GROUPS
    cells = float(rows * cols * n * width)
    own = rows * cols
    rim = cols
    above, below = me > 0, me < n - 1

    loads = [
        pltpu.make_async_copy(source, target, load_sem.at[k])
        for k, (source, target) in enumerate(
            [
                (images_hbm.at[0], images.at[pl.ds(REACH, rows)]),
                (cot_hbm.at[0], cot.at[pl.ds(REACH, rows)]),
                (tweight_hbm, tweight),
                (table_hbm, table),
                (aweight_hbm, aweight),
                (first_hbm, first),
                (second_hbm, second),
                (gain_hbm, gain_ref),
                (bias_hbm, bias_ref),
                (tbias_hbm, tbias_ref),
                (abias_hbm, abias_ref),
                (steps_hbm, steps_ref),
                (ids_hbm, ids_ref),
            ]
        )
    ]
    loads[0].start()
    barrier = pltpu.get_barrier_semaphore()
    for k in range(1, n):
        pl.semaphore_signal(
            barrier, inc=1, device_id={"tile": lax.rem(me + k, n)}, device_id_type=MESH
        )
    for k in range(1, m):
        pl.semaphore_signal(
            barrier, inc=1, device_id={"image": lax.rem(mine + k, m)}, device_id_type=MESH
        )
    for load in loads[1:]:
        load.start()

    def tile_copy(stage, k, arriving):
        peer = lax.rem(me + k, n)
        slot = lax.rem(me + n - k, n) if arriving else me
        return pltpu.make_async_remote_copy(
            src_ref=slots.at[stage, slot],
            dst_ref=slots.at[stage, slot],
            send_sem=send_sem.at[stage, k],
            recv_sem=recv_sem.at[stage, k],
            device_id={"tile": peer},
            device_id_type=MESH,
        )

    def share(stage, value):
        slots[stage, me] = value
        for k in range(1, n):
            tile_copy(stage, k, False).start()

    def total(stage):
        for k in range(1, n):
            tile_copy(stage, k, True).wait_recv()
        summed = slots[stage, 0]
        for k in range(1, n):
            summed = summed + slots[stage, k]
        return summed

    def image_copy(buffer, sends, receives, k, arriving):
        peer = lax.rem(mine + k, m)
        slot = lax.rem(mine + m - k, m) if arriving else mine
        return pltpu.make_async_remote_copy(
            src_ref=buffer.at[slot],
            dst_ref=buffer.at[slot],
            send_sem=sends.at[k],
            recv_sem=receives.at[k],
            device_id={"image": peer},
            device_id_type=MESH,
        )

    def halo_copy(which, buffer, up):
        source = pl.ds(REACH, REACH) if up else pl.ds(rows, REACH)
        target = pl.ds(rows + REACH, REACH) if up else pl.ds(0, REACH)
        return pltpu.make_async_remote_copy(
            src_ref=buffer.at[source],
            dst_ref=buffer.at[target],
            send_sem=halo_send.at[which, int(up)],
            recv_sem=halo_recv.at[which, int(up)],
            device_id={"tile": me - 1 if up else me + 1},
            device_id_type=MESH,
        )

    def flat(buffer, start, count):
        return buffer[pl.ds(start, count)].reshape(count * cols, channels).astype(F32)

    def widen(wide, start, values):
        count = values.shape[0]
        column = lax.rem(lax.broadcasted_iota(jnp.int32, values.shape, 0), cols)
        before = jnp.where(column == 0, 0.0, pltpu.roll(values, 1, 0))
        after = jnp.where(column == cols - 1, 0.0, pltpu.roll(values, count - 1, 0))
        at = pl.ds(start * cols, count)
        wide[at, 0:channels] = before.astype(BF16)
        wide[at, channels : 2 * channels] = values.astype(BF16)
        wide[at, 2 * channels : 3 * channels] = after.astype(BF16)

    def conv(wide, start, count, weight):
        summed = None
        for i in range(3):
            product = jnp.dot(
                wide[pl.ds((start + i) * cols, count * cols), :],
                weight[i].reshape(3 * channels, channels),
                preferred_element_type=F32,
            )
            summed = product if summed is None else summed + product
        return summed

    def conv_back(wide, start, count, weight):
        summed = None
        for i in range(3):
            for j in range(3):
                product = lax.dot_general(
                    wide[pl.ds((start + i) * cols, count * cols), j * channels : (j + 1) * channels],
                    weight[2 - i, 2 - j],
                    (((1,), (1,)), ((), ())),
                    preferred_element_type=F32,
                )
                summed = product if summed is None else summed + product
        return summed

    def moments(summed):
        spread = group_spread(summed, width) / cells
        centre = spread[0:1]
        variance = jnp.maximum(spread[1:2] - centre * centre, 0.0)
        return centre, lax.rsqrt(variance + EPSILON)

    loads[0].wait()
    values = flat(images, REACH, rows)
    sums = column_sums(values, values * values)
    pl.semaphore_wait(barrier, n - 1 + m - 1)
    share(0, sums)
    def halo_start(which, buffer):

        @pl.when(above)
        def _():
            halo_copy(which, buffer, True).start()

        @pl.when(below)
        def _():
            halo_copy(which, buffer, False).start()

        @pl.when(jnp.logical_not(above))
        def _():
            buffer[pl.ds(0, REACH)] = jnp.zeros((REACH, cols, channels), BF16)

        @pl.when(jnp.logical_not(below))
        def _():
            buffer[pl.ds(rows + REACH, REACH)] = jnp.zeros((REACH, cols, channels), BF16)

    halo_start(0, images)

    for k in (2, 3, 4, 7, 8, 9, 10, 11, 12):
        loads[k].wait()
    half = tweight.shape[0] // 2
    index = lax.broadcasted_iota(jnp.int32, (half, 1), 0).astype(F32)
    angles = steps_ref[0, 0].astype(F32) * jnp.exp(-math.log(10000.0) * index / half)
    pre_time = (
        jnp.sum(jnp.cos(angles) * tweight[0:half].astype(F32), axis=0, keepdims=True)
        + jnp.sum(jnp.sin(angles) * tweight[half:].astype(F32), axis=0, keepdims=True)
        + tbias_ref[...]
    )
    entry = lax.broadcasted_iota(jnp.int32, table.shape, 0) == ids_ref[0, 0]
    picked = jnp.sum(jnp.where(entry, table[...].astype(F32), 0.0), axis=0, keepdims=True)
    embedding = pre_time * jax.nn.sigmoid(pre_time) + picked
    activated = embedding * jax.nn.sigmoid(embedding)
    acts[mine] = activated
    for k in range(1, m):
        image_copy(acts, act_send, act_recv, k, False).start()
    partial = jnp.dot(
        jnp.broadcast_to(activated, (8, activated.shape[1])),
        aweight[...].astype(F32),
        precision=HIGHEST,
        preferred_element_type=F32,
    )[0:1]
    share(1, jnp.concatenate([partial[:, :channels], partial[:, channels:]], axis=0))

    loads[1].wait()
    halo_start(1, cot)

    gain, bias = gain_ref[...], bias_ref[...]
    centre, inverse_first = moments(total(0))

    def first_activation(normed):
        pre = normed * gain + bias
        return pre, jax.nn.sigmoid(pre)

    values = (flat(images, REACH, rows) - centre) * inverse_first
    pre, sigma = first_activation(values)
    widen(wide_first, REACH, pre * sigma)

    def halo_wait(which, buffer):
        @pl.when(below)
        def _():
            halo_copy(which, buffer, True).wait_recv()

        @pl.when(above)
        def _():
            halo_copy(which, buffer, False).wait_recv()

    halo_wait(0, images)
    for start, inside in ((0, above), (rows + REACH, below)):
        rim_values = (flat(images, start, REACH) - centre) * inverse_first
        rim_pre, rim_sigma = first_activation(rim_values)
        widen(wide_first, start, jnp.where(inside, rim_pre * rim_sigma, 0.0))
    loads[5].wait()
    centre_rows = conv(wide_first, 1, rows, first).astype(BF16).astype(F32)
    share(2, column_sums(centre_rows, centre_rows * centre_rows))
    hidden[pl.ds(rim, own)] = centre_rows

    for row in (0, rows + 1):
        hidden[pl.ds(row * cols, cols)] = conv(wide_first, row, 1, first).astype(BF16).astype(F32)
    halo_wait(1, cot)
    widen(wide_cot, 0, flat(cot, 0, rows + 2 * REACH))
    loads[6].wait()
    gact[...] = conv_back(wide_cot, 0, rows + 2, second)
    values = (flat(images, REACH, rows) - centre) * inverse_first
    pre, sigma = first_activation(values)
    nfirst[...] = values
    slope[...] = silu_slope(pre, sigma) * gain

    modulation = total(1)
    factor = 1.0 + (modulation[0:1] + abias_ref[:, :channels])
    shift = modulation[1:2] + abias_ref[:, channels:]
    centre, inverse_second = moments(total(2))
    for start, count, inside in ((1, rows, None), (0, 1, above), (rows + 1, 1, below)):
        at = pl.ds(start * cols, count * cols)
        normed = (hidden[at] - centre) * inverse_second
        pre = normed * factor + shift
        sigma = jax.nn.sigmoid(pre)
        back = gact[at] * silu_slope(pre, sigma)
        if inside is None:
            share(3, column_sums(back * normed, back))
        active = pre * sigma
        if inside is not None:
            active = jnp.where(inside, active, 0.0)
        widen(wide_second, start, active)
        nsecond[at] = normed
        gpre[at] = back

    branch[0] = conv(wide_second, 0, rows, second).astype(BF16).reshape(rows, cols, channels)

    sums = total(3)
    spread = group_spread(sums * factor, width) / cells
    paired_mean, plain_mean = spread[0:1], spread[1:2]
    for start, count, inside in ((1, rows, None), (0, 1, above), (rows + 1, 1, below)):
        at = pl.ds(start * cols, count * cols)
        back = inverse_second * (gpre[at] * factor - plain_mean - nsecond[at] * paired_mean)
        if inside is not None:
            back = jnp.where(inside, back, 0.0)
        widen(wide_hidden, start, back)
    pairs[mine] = sums
    for k in range(1, m):
        image_copy(pairs, pair_send, pair_recv, k, False).start()
    back = conv_back(wide_hidden, 0, rows, first) * slope[...]
    normed = nfirst[...]
    share(4, column_sums(back, back * normed))

    for k in range(1, m):
        image_copy(acts, act_send, act_recv, k, True).wait_recv()
        image_copy(pairs, pair_send, pair_recv, k, True).wait_recv()
    extra = (-m) % 8

    def stacked(pieces):
        if extra:
            pieces = pieces + [jnp.zeros((extra, pieces[0].shape[1]), F32)]
        return jnp.concatenate(pieces, axis=0)

    left = stacked([acts[k] for k in range(m)])
    for part in range(2):
        right = stacked([pairs[k][part : part + 1] for k in range(m)])
        columns = slice(part * channels, (part + 1) * channels)
        wgrad[:, columns] = lax.dot_general(
            left, right, (((0,), (0,)), ((), ())), precision=HIGHEST, preferred_element_type=F32
        )
        bgrad[:, columns] = jnp.sum(right, axis=0, keepdims=True)

    spread = group_spread(total(4), width) / cells
    result = inverse_first * (back - spread[0:1] - normed * spread[1:2])
    igrad[0] = result.astype(BF16).reshape(rows, cols, channels)

    for stage in range(5):
        for k in range(1, n):
            tile_copy(stage, k, False).wait_send()
    for k in range(1, m):
        image_copy(acts, act_send, act_recv, k, False).wait_send()
        image_copy(pairs, pair_send, pair_recv, k, False).wait_send()
    for which, buffer in enumerate((images, cot)):

        @pl.when(above)
        def _():
            halo_copy(which, buffer, True).wait_send()

        @pl.when(below)
        def _():
            halo_copy(which, buffer, False).wait_send()

def finish(*refs):
    count = (len(refs) - 1) // 2
    sem = refs[-1]
    copies = [
        pltpu.make_async_copy(refs[k], refs[count + k], sem.at[k]) for k in range(count)
    ]
    for copy in copies:
        copy.start()
    for copy in copies:
        copy.wait()


def body(
    n, m,
    images, cotangent, timesteps, class_ids, norm_gain, norm_bias, conv_first, conv_second,
    time_weight, time_bias, class_table, adaptive_weight, adaptive_bias,
):
    count, rows, cols, channels = images.shape
    assert count == 1 and rows >= REACH
    emb = time_weight.shape[1]
    vmem = pl.BlockSpec(memory_space=pltpu.VMEM)
    anywhere = pl.BlockSpec(memory_space=pl.ANY)
    padded = rows + 2 * REACH
    own, more, most = rows * cols, (rows + 2) * cols, padded * cols
    dma = pltpu.SemaphoreType.DMA
    results = pl.pallas_call(
        functools.partial(kernel, n, m),
        out_shape=(
            jax.ShapeDtypeStruct(images.shape, BF16),
            jax.ShapeDtypeStruct(images.shape, BF16),
            jax.ShapeDtypeStruct((emb, 2 * channels), F32),
            jax.ShapeDtypeStruct((1, 2 * channels), F32),
        ),
        in_specs=[anywhere] * 2 + [pl.BlockSpec(memory_space=pltpu.HBM)] * 11,
        out_specs=(vmem,) * 4,
        scratch_shapes=[
            pltpu.VMEM((padded, cols, channels), BF16),
            pltpu.VMEM((padded, cols, channels), BF16),
            pltpu.VMEM(conv_first.shape, BF16),
            pltpu.VMEM(conv_second.shape, BF16),
            pltpu.VMEM(time_weight.shape, BF16),
            pltpu.VMEM(class_table.shape, BF16),
            pltpu.VMEM(adaptive_weight.shape, BF16),
            pltpu.VMEM((1, channels), F32),
            pltpu.VMEM((1, channels), F32),
            pltpu.VMEM((1, emb), F32),
            pltpu.VMEM((1, 2 * channels), F32),
            pltpu.SMEM((1, 1), jnp.int32),
            pltpu.SMEM((1, 1), jnp.int32),
            pltpu.VMEM((most, 3 * channels), BF16),
            pltpu.VMEM((most, 3 * channels), BF16),
            pltpu.VMEM((more, 3 * channels), BF16),
            pltpu.VMEM((more, 3 * channels), BF16),
            pltpu.VMEM((more, channels), F32),
            pltpu.VMEM((more, channels), F32),
            pltpu.VMEM((more, channels), F32),
            pltpu.VMEM((more, channels), F32),
            pltpu.VMEM((own, channels), F32),
            pltpu.VMEM((own, channels), F32),
            pltpu.VMEM((5, n, 2, channels), F32),
            pltpu.VMEM((m, 1, emb), F32),
            pltpu.VMEM((m, 2, channels), F32),
            dma((13,)),
            dma((2, 2)),
            dma((2, 2)),
            dma((5, n)),
            dma((5, n)),
            dma((m,)),
            dma((m,)),
            dma((m,)),
            dma((m,)),
        ],
        compiler_params=pltpu.CompilerParams(
            collective_id=0, has_side_effects=True, vmem_limit_bytes=GRANT
        ),
    )(
        timesteps[None], class_ids[None],
        *(
            pltpu.with_memory_space_constraint(operand, pltpu.HBM)
            for operand in (
                norm_gain[None], norm_bias[None], time_bias[None],
                adaptive_bias[None], images, cotangent, conv_first, conv_second, time_weight,
                class_table, adaptive_weight,
            )
        )
    )
    branch, igrad, wgrad, bgrad = pl.pallas_call(
        finish,
        out_shape=tuple(jax.ShapeDtypeStruct(r.shape, r.dtype) for r in results),
        in_specs=[anywhere] * 4,
        out_specs=(anywhere,) * 4,
        scratch_shapes=[dma((4,))],
        compiler_params=pltpu.CompilerParams(vmem_limit_bytes=GRANT),
    )(*results)
    return branch, igrad, wgrad, bgrad[0]


def solution(mesh):
    return jax.shard_map(
        functools.partial(body, mesh.shape["tile"], mesh.shape["image"]),
        mesh=mesh,
        in_specs=(
            P(("groups", "image"), "tile", None, None),
            P(("groups", "image"), "tile", None, None),
            P(("groups", "image")),
            P(("groups", "image")),
            P(),
            P(),
            P(),
            P(),
            P(None, "tile"),
            P("tile"),
            P(None, "tile"),
            P("tile", None),
            P(),
        ),
        out_specs=(
            P(("groups", "image"), "tile", None, None),
            P(("groups", "image"), "tile", None, None),
            P(("groups", "tile"), None),
            P("groups"),
        ),
        check_vma=False,
    )
```

```python
import functools
import math

import jax
import jax.numpy as jnp
from jax import lax
from jax.experimental import pallas as pl
from jax.experimental.pallas import tpu as pltpu
from jax.sharding import PartitionSpec as P

GN_GROUPS = 32
EPSILON = 1e-05
MESH = pl.DeviceIdType.MESH
F32 = jnp.float32
BF16 = jnp.bfloat16
GRANT = 24 << 20
REACH = 2
HIGHEST = lax.Precision.HIGHEST


def group_spread(values, width):
    count = values.shape[-1]
    lane = lax.broadcasted_iota(jnp.int32, values.shape, values.ndim - 1)
    step = 1
    while step < width:
        up = pltpu.roll(values, step, values.ndim - 1)
        down = pltpu.roll(values, count - step, values.ndim - 1)
        values = values + jnp.where((lane & step) != 0, up, down)
        step *= 2
    return values


def silu_slope(pre, sigma):
    return sigma * (1.0 + pre * (1.0 - sigma))


def column_sums(first, second):
    return jnp.concatenate(
        [jnp.sum(first, axis=0, keepdims=True), jnp.sum(second, axis=0, keepdims=True)], axis=0
    )


def kernel(
    n, m,
    steps_ref, ids_ref, gain_hbm, bias_hbm, tbias_hbm, abias_hbm,
    images_hbm, cot_hbm, first_hbm, second_hbm, tweight_hbm, table_hbm, aweight_hbm,
    branch, igrad, wgrad, bgrad,
    images, cot, first, second, tweight, table, aweight,
    gain_ref, bias_ref, tbias_ref, abias_ref,
    wide_first, wide_cot, wide_second, wide_hidden,
    wide_scaled, wide_plain, tall, table_of,
    hidden, gact, nsecond, gpre, nfirst, slope,
    slots, acts, pairs, maps,
    load_sem, halo_send, halo_recv, send_sem, recv_sem,
    act_send, act_recv, pair_send, pair_recv, map_send, map_recv,
):
    me = lax.axis_index("tile")
    mine = lax.axis_index("image")
    rows, cols, channels = images_hbm.shape[1:]
    width = channels // GN_GROUPS
    cells = float(rows * cols * n * width)
    own = rows * cols
    rim = cols
    above, below = me > 0, me < n - 1

    loads = [
        pltpu.make_async_copy(source, target, load_sem.at[k])
        for k, (source, target) in enumerate(
            [
                (images_hbm.at[0], images.at[pl.ds(REACH, rows)]),
                (cot_hbm.at[0], cot.at[pl.ds(REACH, rows)]),
                (tweight_hbm, tweight),
                (table_hbm, table),
                (aweight_hbm, aweight),
                (first_hbm, first),
                (second_hbm, second),
                (gain_hbm, gain_ref),
                (bias_hbm, bias_ref),
                (tbias_hbm, tbias_ref),
                (abias_hbm, abias_ref),
            ]
        )
    ]
    for load in loads:
        load.start()

    barrier = pltpu.get_barrier_semaphore()
    for k in range(1, n):
        pl.semaphore_signal(
            barrier, inc=1, device_id={"tile": lax.rem(me + k, n)}, device_id_type=MESH
        )
    for k in range(1, m):
        pl.semaphore_signal(
            barrier, inc=1, device_id={"image": lax.rem(mine + k, m)}, device_id_type=MESH
        )

    def tile_copy(stage, k, arriving):
        peer = lax.rem(me + k, n)
        slot = lax.rem(me + n - k, n) if arriving else me
        return pltpu.make_async_remote_copy(
            src_ref=slots.at[stage, slot],
            dst_ref=slots.at[stage, slot],
            send_sem=send_sem.at[stage, k],
            recv_sem=recv_sem.at[stage, k],
            device_id={"tile": peer},
            device_id_type=MESH,
        )

    def map_copy(k, arriving):
        slot = lax.rem(me + n - k, n) if arriving else me
        return pltpu.make_async_remote_copy(
            src_ref=maps.at[slot],
            dst_ref=maps.at[slot],
            send_sem=map_send.at[k],
            recv_sem=map_recv.at[k],
            device_id={"tile": lax.rem(me + k, n)},
            device_id_type=MESH,
        )

    def pair_copy(k, step, arriving):
        slot = lax.rem(me + n - k, n) if arriving else me
        image = lax.rem(mine + m - step, m) if arriving else mine
        return pltpu.make_async_remote_copy(
            src_ref=pairs.at[image, slot],
            dst_ref=pairs.at[image, slot],
            send_sem=pair_send.at[k, step],
            recv_sem=pair_recv.at[k, step],
            device_id={"tile": lax.rem(me + k, n), "image": lax.rem(mine + step, m)},
            device_id_type=MESH,
        )

    others = [(k, step) for step in range(m) for k in range(n) if k or step]

    def share(stage, value):
        slots[stage, me] = value
        for k in range(1, n):
            tile_copy(stage, k, False).start()

    def total(stage):
        for k in range(1, n):
            tile_copy(stage, k, True).wait_recv()
        summed = slots[stage, 0]
        for k in range(1, n):
            summed = summed + slots[stage, k]
        return summed

    def image_copy(buffer, sends, receives, k, arriving):
        peer = lax.rem(mine + k, m)
        slot = lax.rem(mine + m - k, m) if arriving else mine
        return pltpu.make_async_remote_copy(
            src_ref=buffer.at[slot],
            dst_ref=buffer.at[slot],
            send_sem=sends.at[k],
            recv_sem=receives.at[k],
            device_id={"image": peer},
            device_id_type=MESH,
        )

    def halo_copy(which, buffer, up):
        source = pl.ds(REACH, REACH) if up else pl.ds(rows, REACH)
        target = pl.ds(rows + REACH, REACH) if up else pl.ds(0, REACH)
        return pltpu.make_async_remote_copy(
            src_ref=buffer.at[source],
            dst_ref=buffer.at[target],
            send_sem=halo_send.at[which, int(up)],
            recv_sem=halo_recv.at[which, int(up)],
            device_id={"tile": me - 1 if up else me + 1},
            device_id_type=MESH,
        )

    def flat(buffer, start, count):
        return buffer[pl.ds(start, count)].reshape(count * cols, channels).astype(F32)

    def widen(wide, start, values):
        count = values.shape[0]
        column = lax.rem(lax.broadcasted_iota(jnp.int32, values.shape, 0), cols)
        before = jnp.where(column == 0, 0.0, pltpu.roll(values, 1, 0))
        after = jnp.where(column == cols - 1, 0.0, pltpu.roll(values, count - 1, 0))
        at = pl.ds(start * cols, count)
        wide[at, 0:channels] = before.astype(BF16)
        wide[at, channels : 2 * channels] = values.astype(BF16)
        wide[at, 2 * channels : 3 * channels] = after.astype(BF16)

    def conv(wide, start, count, weight):
        summed = None
        for i in range(3):
            product = jnp.dot(
                wide[pl.ds((start + i) * cols, count * cols), :],
                weight[i].reshape(3 * channels, channels),
                preferred_element_type=F32,
            )
            summed = product if summed is None else summed + product
        return summed

    def conv_back(wide, start, count, weight):
        summed = None
        for i in range(3):
            for j in range(3):
                product = lax.dot_general(
                    wide[pl.ds((start + i) * cols, count * cols), j * channels : (j + 1) * channels],
                    weight[2 - i, 2 - j],
                    (((1,), (1,)), ((), ())),
                    preferred_element_type=F32,
                )
                summed = product if summed is None else summed + product
        return summed

    def pieces(values):
        parts = []
        for _ in range(3):
            part = values.astype(BF16)
            parts.append(part)
            values = values - part.astype(F32)
        return parts

    def moments(summed):
        spread = group_spread(summed, width) / cells
        centre = spread[0:1]
        variance = jnp.maximum(spread[1:2] - centre * centre, 0.0)
        return centre, lax.rsqrt(variance + EPSILON)

    loads[0].wait()
    values = flat(images, REACH, rows)
    sums = column_sums(values, values * values)
    pl.semaphore_wait(barrier, n - 1 + m - 1)
    share(0, sums)
    def halo_start(which, buffer):

        @pl.when(above)
        def _():
            halo_copy(which, buffer, True).start()

        @pl.when(below)
        def _():
            halo_copy(which, buffer, False).start()

        @pl.when(jnp.logical_not(above))
        def _():
            buffer[pl.ds(0, REACH)] = jnp.zeros((REACH, cols, channels), BF16)

        @pl.when(jnp.logical_not(below))
        def _():
            buffer[pl.ds(rows + REACH, REACH)] = jnp.zeros((REACH, cols, channels), BF16)

    halo_start(0, images)

    for k in (2, 3, 4, 7, 8, 9, 10):
        loads[k].wait()
    half = tweight.shape[0] // 2
    index = lax.broadcasted_iota(jnp.int32, (half, 1), 0).astype(F32)
    angles = steps_ref[0].astype(F32) * jnp.exp(-math.log(10000.0) * index / half)
    pre_time = (
        jnp.sum(jnp.cos(angles) * tweight[0:half].astype(F32), axis=0, keepdims=True)
        + jnp.sum(jnp.sin(angles) * tweight[half:].astype(F32), axis=0, keepdims=True)
        + tbias_ref[...]
    )
    entry = lax.broadcasted_iota(jnp.int32, table.shape, 0) == ids_ref[0]
    picked = jnp.sum(jnp.where(entry, table[...].astype(F32), 0.0), axis=0, keepdims=True)
    embedding = pre_time * jax.nn.sigmoid(pre_time) + picked
    activated = embedding * jax.nn.sigmoid(embedding)
    acts[mine] = activated
    for k in range(1, m):
        image_copy(acts, act_send, act_recv, k, False).start()
    partial = jnp.dot(
        jnp.broadcast_to(activated, (8, activated.shape[1])),
        aweight[...].astype(F32),
        precision=HIGHEST,
        preferred_element_type=F32,
    )[0:1]
    share(1, jnp.concatenate([partial[:, :channels], partial[:, channels:]], axis=0))

    loads[1].wait()
    halo_start(1, cot)

    gain, bias = gain_ref[...], bias_ref[...]
    centre, inverse_first = moments(total(0))

    def first_activation(normed):
        pre = normed * gain + bias
        return pre, jax.nn.sigmoid(pre)

    values = (flat(images, REACH, rows) - centre) * inverse_first
    pre, sigma = first_activation(values)
    widen(wide_first, REACH, pre * sigma)

    def halo_wait(which, buffer):
        @pl.when(below)
        def _():
            halo_copy(which, buffer, True).wait_recv()

        @pl.when(above)
        def _():
            halo_copy(which, buffer, False).wait_recv()

    halo_wait(0, images)
    for start, inside in ((0, above), (rows + REACH, below)):
        rim_values = (flat(images, start, REACH) - centre) * inverse_first
        rim_pre, rim_sigma = first_activation(rim_values)
        widen(wide_first, start, jnp.where(inside, rim_pre * rim_sigma, 0.0))
    loads[5].wait()
    centre_rows = conv(wide_first, 1, rows, first).astype(BF16).astype(F32)
    share(2, column_sums(centre_rows, centre_rows * centre_rows))
    hidden[pl.ds(rim, own)] = centre_rows

    for row in (0, rows + 1):
        hidden[pl.ds(row * cols, cols)] = conv(wide_first, row, 1, first).astype(BF16).astype(F32)

    values = (flat(images, REACH, rows) - centre) * inverse_first
    pre, sigma = first_activation(values)
    nfirst[...] = values
    steep = silu_slope(pre, sigma) * gain
    slope[...] = steep
    edges = []
    for part, lines in enumerate((steep, steep * values)):
        lines = lines.astype(BF16).astype(F32)
        tall[pl.ds(part * channels, channels), :] = lines.T.astype(BF16)
        by_row = [lines[p * cols : (p + 1) * cols] for p in range(rows)]
        full = [jnp.sum(line, axis=0, keepdims=True) for line in by_row]
        kept = [
            [total_row - line[0:1] for total_row, line in zip(full, by_row)],
            full,
            [total_row - line[cols - 1 : cols] for total_row, line in zip(full, by_row)],
        ]
        grid = []
        for i in range(3):
            for j in range(3):
                entry = functools.reduce(jnp.add, kept[j])
                if i == 0:
                    entry = entry - jnp.where(above, 0.0, kept[j][0])
                elif i == 2:
                    entry = entry - jnp.where(below, 0.0, kept[j][rows - 1])
                grid.append(entry)
        edges.append(grid)
    for start, count, inside in ((1, rows, None), (0, 1, above), (rows + 1, 1, below)):
        lines = hidden[pl.ds(start * cols, count * cols)]
        if inside is not None:
            lines = jnp.where(inside, lines, 0.0)
        widen(wide_plain, start, lines)
    same = (
        lax.broadcasted_iota(jnp.int32, (GN_GROUPS, channels), 1) // width
        == lax.broadcasted_iota(jnp.int32, (GN_GROUPS, channels), 0)
    )
    products, constants = [None, None], None
    for i in range(3):
        for j in range(3):
            taps = first[2 - i, 2 - j]
            wide_taps = taps.astype(F32)
            near = wide_plain[pl.ds(i * cols, own), j * channels : (j + 1) * channels]
            for part in range(2):
                product = wide_taps * jnp.dot(
                    tall[pl.ds(part * channels, channels), :], near, preferred_element_type=F32
                )
                products[part] = product if i + j == 0 else products[part] + product
            spread_rows = [
                jnp.where(same, piece.astype(F32), 0.0)
                for part in range(2)
                for piece in pieces(edges[part][3 * i + j])
            ]
            product = jnp.dot(
                jnp.concatenate(spread_rows, axis=0).astype(BF16), taps, preferred_element_type=F32
            )
            constants = product if i + j == 0 else constants + product
    blocks = [
        jnp.sum(product.reshape(GN_GROUPS, width, channels), axis=1) for product in products
    ] + [
        sum(constants[(3 * part + q) * GN_GROUPS : (3 * part + q + 1) * GN_GROUPS] for q in range(3))
        for part in range(2)
    ]
    columns_of = [pieces(block) for block in blocks]
    gathered = None
    for quarter in range(4):
        row = lax.broadcasted_iota(jnp.int32, (channels, 4 * GN_GROUPS), 0)
        lane = lax.broadcasted_iota(jnp.int32, (channels, 4 * GN_GROUPS), 1)
        chosen = jnp.where(row // width + quarter * GN_GROUPS == lane, 1.0, 0.0).astype(BF16)
        product = jnp.dot(
            jnp.concatenate(columns_of[quarter], axis=0), chosen, preferred_element_type=F32
        )
        gathered = product if gathered is None else gathered + product
    maps[me] = sum(gathered[q * GN_GROUPS : (q + 1) * GN_GROUPS] for q in range(3))
    for k in range(1, n):
        map_copy(k, False).start()

    halo_wait(1, cot)
    widen(wide_cot, 0, flat(cot, 0, rows + 2 * REACH))
    loads[6].wait()
    gact[...] = conv_back(wide_cot, 0, rows + 2, second)

    modulation = total(1)
    factor = 1.0 + (modulation[0:1] + abias_ref[:, :channels])
    shift = modulation[1:2] + abias_ref[:, channels:]
    centre, inverse_second = moments(total(2))
    for start, count, inside in ((1, rows, None), (0, 1, above), (rows + 1, 1, below)):
        at = pl.ds(start * cols, count * cols)
        normed = (hidden[at] - centre) * inverse_second
        pre = normed * factor + shift
        sigma = jax.nn.sigmoid(pre)
        back = gact[at] * silu_slope(pre, sigma)
        if inside is None:
            pairs[mine, me] = column_sums(back * normed, back)
            for k, step in others:
                pair_copy(k, step, False).start()
        active = pre * sigma
        back = back * (factor * inverse_second)
        if inside is not None:
            active = jnp.where(inside, active, 0.0)
            back = jnp.where(inside, back, 0.0)
        widen(wide_scaled, start, back)
        widen(wide_second, start, active)
        nsecond[at] = normed
        gpre[at] = back

    early = conv_back(wide_scaled, 0, rows, first) * slope[...]
    share(3, column_sums(early, early * nfirst[...]))

    branch[0] = conv(wide_second, 0, rows, second).astype(BF16).reshape(rows, cols, channels)

    for k in range(1, n):
        map_copy(k, True).wait_recv()
    summed = maps[0]
    for k in range(1, n):
        summed = summed + maps[k]
    lanes = 4 * GN_GROUPS
    spread_of = jnp.where(same, 1.0, 0.0)
    for q, piece in enumerate(pieces(summed)):
        table_of[pl.ds(q * lanes, lanes), :] = lax.dot_general(
            piece.astype(F32), spread_of, (((0,), (0,)), ((), ())), preferred_element_type=F32
        ).astype(BF16)

    for k in range(1, n):
        pair_copy(k, 0, True).wait_recv()

    def whole(image):
        summed = pairs[image, 0]
        for k in range(1, n):
            summed = summed + pairs[image, k]
        return summed

    spread = group_spread(whole(mine) * factor, width) / cells
    paired_mean, plain_mean = inverse_second * spread[0:1], inverse_second * spread[1:2]
    for start, count, inside in ((1, rows, None), (0, 1, above), (rows + 1, 1, below)):
        at = pl.ds(start * cols, count * cols)
        back = gpre[at] - plain_mean - nsecond[at] * paired_mean
        if inside is not None:
            back = jnp.where(inside, back, 0.0)
        widen(wide_hidden, start, back)

    tilt = paired_mean * inverse_second
    level = plain_mean - tilt * centre
    row = lax.broadcasted_iota(jnp.int32, (channels, lanes), 0)
    lane = lax.broadcasted_iota(jnp.int32, (channels, lanes), 1)
    chosen = jnp.where(lax.rem(lane, GN_GROUPS) * width == row, 1.0, 0.0).astype(BF16)
    short = [piece.astype(F32) for piece in pieces(level) + pieces(tilt)]
    short = jnp.concatenate(short + [jnp.zeros((2, channels), F32)], axis=0).astype(BF16)
    short = jnp.dot(short, chosen, preferred_element_type=F32)
    quarter = lax.broadcasted_iota(jnp.int32, (1, lanes), 1) // GN_GROUPS
    nothing = jnp.zeros((1, lanes), F32)
    left = []
    for part in range(2):
        mixed = [
            jnp.where(quarter == part, short[3 + q : 4 + q], jnp.where(quarter == part + 2, short[q : q + 1], 0.0))
            for q in range(3)
        ]
        left += [
            jnp.concatenate([mixed[q]] * (3 - q) + [nothing] * q, axis=1) for q in range(3)
        ]
    left = jnp.concatenate(left + [jnp.zeros((2, 3 * lanes), F32)], axis=0).astype(BF16)
    moved = jnp.dot(left, table_of[...], preferred_element_type=F32)
    moved = jnp.concatenate(
        [jnp.sum(moved[3 * part : 3 * part + 3], axis=0, keepdims=True) for part in range(2)], axis=0
    )

    back = conv_back(wide_hidden, 0, rows, first) * slope[...]
    spread = (group_spread(total(3), width) - moved) / cells
    result = inverse_first * (back - spread[0:1] - nfirst[...] * spread[1:2])
    igrad[0] = result.astype(BF16).reshape(rows, cols, channels)

    for k in range(1, m):
        image_copy(acts, act_send, act_recv, k, True).wait_recv()
    for k, step in others:
        if step:
            pair_copy(k, step, True).wait_recv()
    sums = [whole(k) for k in range(m)]
    extra = (-6 * m) % 16

    def stacked(parts):
        if extra:
            parts = parts + [jnp.zeros((extra, parts[0].shape[1]), F32)]
        return jnp.concatenate(parts, axis=0).astype(BF16)

    thirds = [[piece.astype(F32) for piece in pieces(acts[k])] for k in range(m)]
    left = stacked([thirds[k][q] for q in (0, 0, 1, 0, 1, 2) for k in range(m)])
    for part in range(2):
        lines = [value[part : part + 1] for value in sums]
        thirds = [[piece.astype(F32) for piece in pieces(line)] for line in lines]
        right = stacked([thirds[k][q] for q in (0, 1, 0, 2, 1, 0) for k in range(m)])
        columns = slice(part * channels, (part + 1) * channels)
        wgrad[:, columns] = lax.dot_general(
            left, right, (((0,), (0,)), ((), ())), preferred_element_type=F32
        )
        bgrad[:, columns] = functools.reduce(jnp.add, lines)

    for stage in range(4):
        for k in range(1, n):
            tile_copy(stage, k, False).wait_send()
    for k in range(1, n):
        map_copy(k, False).wait_send()
    for k in range(1, m):
        image_copy(acts, act_send, act_recv, k, False).wait_send()
    for k, step in others:
        pair_copy(k, step, False).wait_send()
    for which, buffer in enumerate((images, cot)):

        @pl.when(above)
        def _():
            halo_copy(which, buffer, True).wait_send()

        @pl.when(below)
        def _():
            halo_copy(which, buffer, False).wait_send()

def finish(*refs):
    count = (len(refs) - 1) // 2
    sem = refs[-1]
    copies = [
        pltpu.make_async_copy(refs[k], refs[count + k], sem.at[k]) for k in range(count)
    ]
    for copy in copies:
        copy.start()
    for copy in copies:
        copy.wait()


def body(
    n, m,
    images, cotangent, timesteps, class_ids, norm_gain, norm_bias, conv_first, conv_second,
    time_weight, time_bias, class_table, adaptive_weight, adaptive_bias,
):
    count, rows, cols, channels = images.shape
    assert count == 1 and rows >= REACH
    emb = time_weight.shape[1]
    vmem = pl.BlockSpec(memory_space=pltpu.VMEM)
    anywhere = pl.BlockSpec(memory_space=pl.ANY)
    padded = rows + 2 * REACH
    own, more, most = rows * cols, (rows + 2) * cols, padded * cols
    dma = pltpu.SemaphoreType.DMA
    results = pl.pallas_call(
        functools.partial(kernel, n, m),
        out_shape=(
            jax.ShapeDtypeStruct(images.shape, BF16),
            jax.ShapeDtypeStruct(images.shape, BF16),
            jax.ShapeDtypeStruct((emb, 2 * channels), F32),
            jax.ShapeDtypeStruct((1, 2 * channels), F32),
        ),
        in_specs=[pl.BlockSpec(memory_space=pltpu.SMEM)] * 2
        + [pl.BlockSpec(memory_space=pltpu.HBM)] * 11,
        out_specs=(vmem,) * 4,
        scratch_shapes=[
            pltpu.VMEM((padded, cols, channels), BF16),
            pltpu.VMEM((padded, cols, channels), BF16),
            pltpu.VMEM(conv_first.shape, BF16),
            pltpu.VMEM(conv_second.shape, BF16),
            pltpu.VMEM(time_weight.shape, BF16),
            pltpu.VMEM(class_table.shape, BF16),
            pltpu.VMEM(adaptive_weight.shape, BF16),
            pltpu.VMEM((1, channels), F32),
            pltpu.VMEM((1, channels), F32),
            pltpu.VMEM((1, emb), F32),
            pltpu.VMEM((1, 2 * channels), F32),
            pltpu.VMEM((most, 3 * channels), BF16),
            pltpu.VMEM((most, 3 * channels), BF16),
            pltpu.VMEM((more, 3 * channels), BF16),
            pltpu.VMEM((more, 3 * channels), BF16),
            pltpu.VMEM((more, 3 * channels), BF16),
            pltpu.VMEM((more, 3 * channels), BF16),
            pltpu.VMEM((2 * channels, own), BF16),
            pltpu.VMEM((12 * GN_GROUPS, channels), BF16),
            pltpu.VMEM((more, channels), F32),
            pltpu.VMEM((more, channels), F32),
            pltpu.VMEM((more, channels), F32),
            pltpu.VMEM((more, channels), F32),
            pltpu.VMEM((own, channels), F32),
            pltpu.VMEM((own, channels), F32),
            pltpu.VMEM((4, n, 2, channels), F32),
            pltpu.VMEM((m, 1, emb), F32),
            pltpu.VMEM((m, n, 2, channels), F32),
            pltpu.VMEM((n, GN_GROUPS, 4 * GN_GROUPS), F32),
            dma((11,)),
            dma((2, 2)),
            dma((2, 2)),
            dma((4, n)),
            dma((4, n)),
            dma((m,)),
            dma((m,)),
            dma((n, m)),
            dma((n, m)),
            dma((n,)),
            dma((n,)),
        ],
        compiler_params=pltpu.CompilerParams(
            collective_id=0, has_side_effects=True, vmem_limit_bytes=GRANT
        ),
    )(
        timesteps, class_ids,
        *(
            pltpu.with_memory_space_constraint(operand, pltpu.HBM)
            for operand in (
                norm_gain[None], norm_bias[None], time_bias[None],
                adaptive_bias[None], images, cotangent, conv_first, conv_second, time_weight,
                class_table, adaptive_weight,
            )
        )
    )
    branch, igrad, wgrad, bgrad = pl.pallas_call(
        finish,
        out_shape=tuple(jax.ShapeDtypeStruct(r.shape, r.dtype) for r in results),
        in_specs=[anywhere] * 4,
        out_specs=(anywhere,) * 4,
        scratch_shapes=[dma((4,))],
        compiler_params=pltpu.CompilerParams(vmem_limit_bytes=GRANT),
    )(*results)
    return branch, igrad, wgrad, bgrad[0]


def solution(mesh):
    return jax.shard_map(
        functools.partial(body, mesh.shape["tile"], mesh.shape["image"]),
        mesh=mesh,
        in_specs=(
            P(("groups", "image"), "tile", None, None),
            P(("groups", "image"), "tile", None, None),
            P(("groups", "image")),
            P(("groups", "image")),
            P(),
            P(),
            P(),
            P(),
            P(None, "tile"),
            P("tile"),
            P(None, "tile"),
            P("tile", None),
            P(),
        ),
        out_specs=(
            P(("groups", "image"), "tile", None, None),
            P(("groups", "image"), "tile", None, None),
            P(("groups", "tile"), None),
            P("groups"),
        ),
        check_vma=False,
    )
```

```python
import functools
import math

import jax
import jax.numpy as jnp
from jax import lax
from jax.experimental import pallas as pl
from jax.experimental.pallas import tpu as pltpu
from jax.sharding import PartitionSpec as P

GN_GROUPS = 32
EPSILON = 1e-05
MESH = pl.DeviceIdType.MESH
F32 = jnp.float32
BF16 = jnp.bfloat16
GRANT = 24 << 20
REACH = 2
PARTS = 2
SPARE = 128
HIGHEST = lax.Precision.HIGHEST


def group_spread(values, width):
    count = values.shape[-1]
    lane = lax.broadcasted_iota(jnp.int32, values.shape, values.ndim - 1)
    step = 1
    while step < width:
        up = pltpu.roll(values, step, values.ndim - 1)
        down = pltpu.roll(values, count - step, values.ndim - 1)
        values = values + jnp.where((lane & step) != 0, up, down)
        step *= 2
    return values


def silu_slope(pre, sigma):
    return sigma * (1.0 + pre * (1.0 - sigma))


def column_sums(first, second):
    return jnp.concatenate(
        [jnp.sum(first, axis=0, keepdims=True), jnp.sum(second, axis=0, keepdims=True)], axis=0
    )


def kernel(
    n, m,
    steps_ref, ids_ref, gain_hbm, bias_hbm, tbias_hbm, abias_hbm,
    images_hbm, cot_hbm, first_hbm, second_hbm, tweight_hbm, table_hbm, aweight_hbm,
    branch, igrad, left_out, right_out, bgrad,
    images, cot, first, second, tweight, table, aweight,
    gain_ref, bias_ref, tbias_ref, abias_ref,
    wide_first, wide_cot, wide_second, wide_hidden,
    wide_scaled, wide_plain, tall, table_of,
    hidden, gact, nsecond, gpre, nfirst, slope,
    slots, acts, pairs, maps, spare,
    load_sem, halo_send, halo_recv, send_sem, slot_recv, act_recv, pair_recv, map_recv,
):
    me = lax.axis_index("tile")
    mine = lax.axis_index("image")
    rows, cols, channels = images_hbm.shape[1:]
    width = channels // GN_GROUPS
    cells = float(rows * cols * n * width)
    own = rows * cols
    above, below = me > 0, me < n - 1

    def load(source, target, k):
        return pltpu.make_async_copy(source, target, load_sem.at[k])

    loads = [
        load(images_hbm.at[0], images.at[pl.ds(REACH, rows)], 0),
        load(cot_hbm.at[0], cot.at[pl.ds(REACH, rows)], 1),
        load(tweight_hbm, tweight, 2),
        load(table_hbm, table, 3),
        load(aweight_hbm, aweight, 4),
        load(first_hbm, first, 5),
        load(second_hbm, second, 6),
        load(gain_hbm, gain_ref, 7),
        load(bias_hbm, bias_ref, 8),
        load(tbias_hbm, tbias_ref, 9),
        load(abias_hbm, abias_ref, 10),
    ]
    loads[0].start()
    barrier = pltpu.get_barrier_semaphore()
    for k in reversed(range(1, n)):
        pl.semaphore_signal(
            barrier, inc=1, device_id={"tile": lax.rem(me + k, n)}, device_id_type=MESH
        )
    for k in range(1, m):
        pl.semaphore_signal(
            barrier, inc=1, device_id={"image": lax.rem(mine + k, m)}, device_id_type=MESH
        )
    for k in (7, 8, 5, 2, 3, 4, 9, 10, 1, 6):
        loads[k].start()

    def remote(buffer, slot, receive, device):
        return pltpu.make_async_remote_copy(
            src_ref=buffer.at[slot],
            dst_ref=buffer.at[slot],
            send_sem=send_sem.at[0],
            recv_sem=receive,
            device_id=device,
            device_id_type=MESH,
        )

    def settle(lines, receive):
        while lines:
            part = min(lines, spare.shape[0])
            block = spare.at[pl.ds(0, part)]
            copy = pltpu.make_async_remote_copy(
                src_ref=block,
                dst_ref=block,
                send_sem=send_sem.at[0],
                recv_sem=send_sem.at[0] if receive is None else receive,
                device_id={"tile": lax.rem(me + 1, n)},
                device_id_type=MESH,
            )
            if receive is None:
                copy.wait_send()
            else:
                copy.wait_recv()
            lines -= part

    def tile_peer(k):
        return {"tile": lax.rem(me + k, n)}

    def share(stage, value):
        slots[stage, me] = value
        for k in range(1, n):
            remote(slots.at[stage], me, slot_recv.at[stage], tile_peer(k)).start()

    def total(stage):
        settle(2 * (n - 1), slot_recv.at[stage])
        summed = slots[stage, 0]
        for k in range(1, n):
            summed = summed + slots[stage, k]
        return summed

    HALOS = ((REACH, rows + REACH, rows + REACH - 1, REACH - 1, 1),
             (REACH + 1, rows + REACH + 1, rows + REACH - 2, REACH - 2, 1),
             (REACH, rows + REACH, rows, 0, REACH))

    def halo_copy(which, buffer, up):
        up_from, up_to, down_from, down_to, count = HALOS[which]
        source, target = (up_from, up_to) if up else (down_from, down_to)
        return pltpu.make_async_remote_copy(
            src_ref=buffer.at[pl.ds(source, count)],
            dst_ref=buffer.at[pl.ds(target, count)],
            send_sem=halo_send.at[which, int(up)],
            recv_sem=halo_recv.at[which, int(up)],
            device_id={"tile": me - 1 if up else me + 1},
            device_id_type=MESH,
        )

    def halo_start(which, buffer):
        _, low, _, high, count = HALOS[which]

        @pl.when(above)
        def _():
            halo_copy(which, buffer, True).start()

        @pl.when(below)
        def _():
            halo_copy(which, buffer, False).start()

        @pl.when(jnp.logical_not(above))
        def _():
            buffer[pl.ds(high, count)] = jnp.zeros((count, cols, channels), BF16)

        @pl.when(jnp.logical_not(below))
        def _():
            buffer[pl.ds(low, count)] = jnp.zeros((count, cols, channels), BF16)

    def halo_wait(which, buffer):
        @pl.when(below)
        def _():
            halo_copy(which, buffer, True).wait_recv()

        @pl.when(above)
        def _():
            halo_copy(which, buffer, False).wait_recv()

    column = lax.broadcasted_iota(jnp.int32, (cols, channels), 0)

    def widen(wide, row, values):
        before = jnp.where(column == 0, 0.0, pltpu.roll(values, 1, 0))
        after = jnp.where(column == cols - 1, 0.0, pltpu.roll(values, cols - 1, 0))
        at = pl.ds(row * cols, cols)
        wide[at, 0:channels] = before.astype(BF16)
        wide[at, channels : 2 * channels] = values.astype(BF16)
        wide[at, 2 * channels : 3 * channels] = after.astype(BF16)

    def conv(wide, starts, count, weight):
        summed = None
        for i in range(3):
            lines = [wide[pl.ds((start + i) * cols, count * cols), :] for start in starts]
            product = jnp.dot(
                lines[0] if len(lines) == 1 else jnp.concatenate(lines, axis=0),
                weight[i].reshape(3 * channels, channels),
                preferred_element_type=F32,
            )
            summed = product if summed is None else summed + product
        return summed

    def conv_back(wide, start, count, weight):
        summed = None
        for i in range(3):
            for j in range(3):
                product = lax.dot_general(
                    wide[pl.ds((start + i) * cols, count * cols), j * channels : (j + 1) * channels],
                    weight[2 - i, 2 - j],
                    (((1,), (1,)), ((), ())),
                    preferred_element_type=F32,
                )
                summed = product if summed is None else summed + product
        return summed

    def pieces(values):
        parts = []
        for _ in range(3):
            part = values.astype(BF16)
            parts.append(part)
            values = values - part.astype(F32)
        return parts

    def moments(summed):
        spread = group_spread(summed, width) / cells
        centre = spread[0:1]
        variance = jnp.maximum(spread[1:2] - centre * centre, 0.0)
        return centre, lax.rsqrt(variance + EPSILON)

    def add_up(parts):
        return functools.reduce(jnp.add, parts)

    loads[0].wait()
    sums = []
    for p in range(rows):
        line = images[REACH + p].astype(F32)
        sums.append(column_sums(line, line * line))
    sums = add_up(sums)
    pl.semaphore_wait(barrier, n - 1 + m - 1)
    share(0, sums)
    halo_start(0, images)
    halo_start(1, images)

    for k in (2, 3, 4, 7, 8, 9, 10):
        loads[k].wait()
    half = tweight.shape[0] // 2
    index = lax.broadcasted_iota(jnp.int32, (half, 1), 0).astype(F32)
    angles = steps_ref[0].astype(F32) * jnp.exp(-math.log(10000.0) * index / half)
    pre_time = (
        jnp.sum(jnp.cos(angles) * tweight[0:half].astype(F32), axis=0, keepdims=True)
        + jnp.sum(jnp.sin(angles) * tweight[half:].astype(F32), axis=0, keepdims=True)
        + tbias_ref[...]
    )
    entry = lax.broadcasted_iota(jnp.int32, table.shape, 0) == ids_ref[0]
    picked = jnp.sum(jnp.where(entry, table[...].astype(F32), 0.0), axis=0, keepdims=True)
    embedding = pre_time * jax.nn.sigmoid(pre_time) + picked
    activated = embedding * jax.nn.sigmoid(embedding)
    acts[mine] = activated
    for k in range(1, m):
        remote(acts, mine, act_recv.at[0], {"image": lax.rem(mine + k, m)}).start()
    partial = jnp.dot(
        jnp.broadcast_to(activated, (8, activated.shape[1])),
        aweight[...].astype(F32),
        precision=HIGHEST,
        preferred_element_type=F32,
    )[0:1]
    share(1, jnp.concatenate([partial[:, :channels], partial[:, channels:]], axis=0))

    loads[1].wait()
    halo_start(2, cot)
    for p in range(rows):
        widen(wide_cot, REACH + p, cot[REACH + p].astype(F32))

    loads[5].wait()
    halo_wait(0, images)
    gain, bias = gain_ref[...], bias_ref[...]
    centre, inverse_first = moments(total(0))
    stretch = 0.5 * inverse_first * gain
    offset = 0.5 * bias - centre * stretch

    def first_row(row, inside):
        lean = images[row].astype(F32) * stretch + offset
        value = lean * (1.0 + jnp.tanh(lean))
        if inside is not None:
            value = jnp.where(inside, value, 0.0)
        widen(wide_first, row, value)

    first_row(REACH - 1, above)
    for p in range(rows):
        first_row(REACH + p, None)
    first_row(rows + REACH, below)
    centre_rows = conv(wide_first, (1,), rows, first).astype(BF16).astype(F32)
    share(2, column_sums(centre_rows, centre_rows * centre_rows))
    hidden[pl.ds(cols, own)] = centre_rows

    halo_wait(1, images)
    first_row(0, above)
    first_row(rows + 2 * REACH - 1, below)
    outer = conv(wide_first, (0, rows + 1), 1, first).astype(BF16).astype(F32)
    hidden[pl.ds(0, cols)] = outer[0:cols]
    hidden[pl.ds((rows + 1) * cols, cols)] = outer[cols : 2 * cols]

    whole_rows, first_cells, last_cells = [[], []], [[], []], [[], []]
    for p in range(rows):
        at = pl.ds(p * cols, cols)
        line = images[REACH + p].astype(F32)
        lean = line * stretch + offset
        bend = jnp.tanh(lean)
        steep = (0.5 * gain) * ((1.0 + bend) * (1.0 + lean * (1.0 - bend)))
        line = (line - centre) * inverse_first
        nfirst[at] = line
        slope[at] = steep
        for part, lines in enumerate((steep, steep * line)):
            lines = lines.astype(BF16).astype(F32)
            gact[at if part == 0 else pl.ds((rows + p) * cols, cols)] = lines
            whole_rows[part].append(jnp.sum(lines, axis=0, keepdims=True))
            first_cells[part].append(lines[0:1])
            last_cells[part].append(lines[cols - 1 : cols])
    edges = []
    for part in range(2):
        tall[pl.ds(part * channels, channels), :] = gact[pl.ds(part * own, own)].T.astype(BF16)
        kept = [
            [a - b for a, b in zip(whole_rows[part], first_cells[part])],
            whole_rows[part],
            [a - b for a, b in zip(whole_rows[part], last_cells[part])],
        ]
        grid = []
        for i in range(3):
            for j in range(3):
                value = add_up(kept[j])
                if i == 0:
                    value = value - jnp.where(above, 0.0, kept[j][0])
                elif i == 2:
                    value = value - jnp.where(below, 0.0, kept[j][rows - 1])
                grid.append(value)
        edges.append(grid)
    for row in range(rows + 2):
        lines = hidden[pl.ds(row * cols, cols)]
        if row == 0:
            lines = jnp.where(above, lines, 0.0)
        elif row == rows + 1:
            lines = jnp.where(below, lines, 0.0)
        widen(wide_plain, row, lines)
    same = (
        lax.broadcasted_iota(jnp.int32, (GN_GROUPS, channels), 1) // width
        == lax.broadcasted_iota(jnp.int32, (GN_GROUPS, channels), 0)
    )
    products, constants = [None, None], None
    for i in range(3):
        for j in range(3):
            taps = first[2 - i, 2 - j]
            wide_taps = taps.astype(F32)
            near = wide_plain[pl.ds(i * cols, own), j * channels : (j + 1) * channels]
            for part in range(2):
                product = wide_taps * jnp.dot(
                    tall[pl.ds(part * channels, channels), :], near, preferred_element_type=F32
                )
                products[part] = product if i + j == 0 else products[part] + product
            spread_rows = [
                jnp.where(same, piece.astype(F32), 0.0)
                for part in range(2)
                for piece in pieces(edges[part][3 * i + j])
            ]
            product = jnp.dot(
                jnp.concatenate(spread_rows, axis=0).astype(BF16), taps, preferred_element_type=F32
            )
            constants = product if i + j == 0 else constants + product
    blocks = [
        jnp.sum(product.reshape(GN_GROUPS, width, channels), axis=1) for product in products
    ] + [
        add_up(
            [constants[(3 * part + q) * GN_GROUPS : (3 * part + q + 1) * GN_GROUPS] for q in range(3)]
        )
        for part in range(2)
    ]
    columns_of = [pieces(block) for block in blocks]
    lanes = 4 * GN_GROUPS
    gathered = None
    for quarter in range(4):
        row = lax.broadcasted_iota(jnp.int32, (channels, lanes), 0)
        lane = lax.broadcasted_iota(jnp.int32, (channels, lanes), 1)
        chosen = jnp.where(row // width + quarter * GN_GROUPS == lane, 1.0, 0.0).astype(BF16)
        product = jnp.dot(
            jnp.concatenate(columns_of[quarter], axis=0), chosen, preferred_element_type=F32
        )
        gathered = product if gathered is None else gathered + product
    maps[me] = add_up([gathered[q * GN_GROUPS : (q + 1) * GN_GROUPS] for q in range(3)])
    for k in range(1, n):
        remote(maps, me, map_recv.at[0], tile_peer(k)).start()

    halo_wait(2, cot)
    for row in (0, 1, rows + REACH, rows + REACH + 1):
        widen(wide_cot, row, cot[row].astype(F32))
    loads[6].wait()
    gact[pl.ds(0, (rows + 2) * cols)] = conv_back(wide_cot, 0, rows + 2, second)

    modulation = total(1)
    factor = 1.0 + (modulation[0:1] + abias_ref[:, :channels])
    shift = modulation[1:2] + abias_ref[:, channels:]
    centre, inverse_second = moments(total(2))

    def second_row(row):
        at = pl.ds(row * cols, cols)
        normed = (hidden[at] - centre) * inverse_second
        lean = normed * (0.5 * factor) + 0.5 * shift
        bend = jnp.tanh(lean)
        rise = 1.0 + bend
        back = gact[at] * (0.5 * rise * (1.0 + lean * (1.0 - bend)))
        nsecond[at] = normed
        gact[at] = lean * rise
        gpre[at] = back
        return column_sums(back * normed, back)

    pairs[mine, me] = add_up([second_row(1 + p) for p in range(rows)])
    others = [(k, step) for step in range(m) for k in range(n) if k or step]
    for k, step in others:
        remote(
            pairs.at[mine], me, pair_recv.at[min(step, 1)],
            {"tile": lax.rem(me + k, n), "image": lax.rem(mine + step, m)},
        ).start()

    scale = factor * inverse_second
    second_row(0)
    second_row(rows + 1)

    def masked(row, values):
        if row == 0:
            return jnp.where(above, values, 0.0)
        if row == rows + 1:
            return jnp.where(below, values, 0.0)
        return values

    for row in range(rows + 2):
        at = pl.ds(row * cols, cols)
        back = gpre[at] * scale
        gpre[at] = back
        widen(wide_scaled, row, masked(row, back))
    gradient = conv_back(wide_scaled, 0, rows, first)
    sums = []
    for p in range(rows):
        at = pl.ds(p * cols, cols)
        early = gradient[p * cols : (p + 1) * cols] * slope[at]
        sums.append(column_sums(early, early * nfirst[at]))
    share(3, add_up(sums))

    for row in range(rows + 2):
        widen(wide_second, row, masked(row, gact[pl.ds(row * cols, cols)]))
    branch[0] = conv(wide_second, (0,), rows, second).astype(BF16).reshape(rows, cols, channels)

    settle(maps.shape[1] * maps.shape[2] // channels * (n - 1), map_recv.at[0])
    summed = add_up([maps[k] for k in range(n)])
    spread_of = jnp.where(same, 1.0, 0.0)
    for q, piece in enumerate(pieces(summed)):
        table_of[pl.ds(q * lanes, lanes), :] = lax.dot_general(
            piece.astype(F32), spread_of, (((0,), (0,)), ((), ())), preferred_element_type=F32
        ).astype(BF16)

    settle((m - 1) * acts.shape[2] // channels, act_recv.at[0])
    extra = (-6 * m) % 16

    def stacked(parts):
        if extra:
            parts = parts + [jnp.zeros((extra, parts[0].shape[1]), F32)]
        return jnp.concatenate(parts, axis=0).astype(BF16)

    thirds = [[piece.astype(F32) for piece in pieces(acts[k])] for k in range(m)]
    left_out[...] = stacked([thirds[k][q] for q in (0, 0, 1, 0, 1, 2) for k in range(m)])

    settle(2 * (n - 1), pair_recv.at[0])

    def whole(image):
        return add_up([pairs[image, k] for k in range(n)])

    spread = group_spread(whole(mine) * factor, width) / cells
    paired_mean, plain_mean = inverse_second * spread[0:1], inverse_second * spread[1:2]
    for row in range(rows + 2):
        at = pl.ds(row * cols, cols)
        back = gpre[at] - plain_mean - nsecond[at] * paired_mean
        widen(wide_hidden, row, masked(row, back))

    tilt = paired_mean * inverse_second
    level = plain_mean - tilt * centre
    row = lax.broadcasted_iota(jnp.int32, (channels, lanes), 0)
    lane = lax.broadcasted_iota(jnp.int32, (channels, lanes), 1)
    chosen = jnp.where(lax.rem(lane, GN_GROUPS) * width == row, 1.0, 0.0).astype(BF16)
    short = [piece.astype(F32) for piece in pieces(level) + pieces(tilt)]
    short = jnp.concatenate(short + [jnp.zeros((2, channels), F32)], axis=0).astype(BF16)
    short = jnp.dot(short, chosen, preferred_element_type=F32)
    quarter = lax.broadcasted_iota(jnp.int32, (1, lanes), 1) // GN_GROUPS
    nothing = jnp.zeros((1, lanes), F32)
    left = []
    for part in range(2):
        mixed = [
            jnp.where(quarter == part, short[3 + q : 4 + q], jnp.where(quarter == part + 2, short[q : q + 1], 0.0))
            for q in range(3)
        ]
        left += [
            jnp.concatenate([mixed[q]] * (3 - q) + [nothing] * q, axis=1) for q in range(3)
        ]
    left = jnp.concatenate(left + [jnp.zeros((2, 3 * lanes), F32)], axis=0).astype(BF16)
    moved = jnp.dot(left, table_of[...], preferred_element_type=F32)
    moved = jnp.concatenate(
        [jnp.sum(moved[3 * part : 3 * part + 3], axis=0, keepdims=True) for part in range(2)], axis=0
    )

    gradient = conv_back(wide_hidden, 0, rows, first)

    settle(2 * n * (m - 1), pair_recv.at[1])
    sums = [whole(k) for k in range(m)]
    for part in range(2):
        lines = [value[part : part + 1] for value in sums]
        thirds = [[piece.astype(F32) for piece in pieces(line)] for line in lines]
        columns = slice(part * channels, (part + 1) * channels)
        right_out[:, columns] = stacked([thirds[k][q] for q in (0, 1, 0, 2, 1, 0) for k in range(m)])
        bgrad[:, columns] = add_up(lines)

    spread = (group_spread(total(3), width) - moved) / cells
    for p in range(rows):
        at = pl.ds(p * cols, cols)
        back = gradient[p * cols : (p + 1) * cols] * slope[at]
        result = inverse_first * (back - spread[0:1] - nfirst[at] * spread[1:2])
        igrad[0, p] = result.astype(BF16)

    lines = 2 * (4 * (n - 1) + len(others)) + (m - 1) * acts.shape[2] // channels
    lines += maps.shape[1] * maps.shape[2] // channels * (n - 1)
    settle(lines, None)
    for which, buffer in enumerate((images, images, cot)):

        @pl.when(above)
        def _():
            halo_copy(which, buffer, True).wait_send()

        @pl.when(below)
        def _():
            halo_copy(which, buffer, False).wait_send()


def finish(branch, igrad, left, right, bgrad, branch_out, igrad_out, wgrad_out, bgrad_out, wgrad, sem):
    copies = [
        pltpu.make_async_copy(source, target, sem.at[k])
        for k, (source, target) in enumerate(
            [(igrad, igrad_out), (branch, branch_out), (bgrad, bgrad_out)]
        )
    ]
    for copy in copies:
        copy.start()
    height = wgrad.shape[0] // PARTS
    for k in range(PARTS):
        at = pl.ds(k * height, height)
        wgrad[at] = lax.dot_general(
            left[:, k * height : (k + 1) * height], right[...],
            (((0,), (0,)), ((), ())), preferred_element_type=F32,
        )
        copy = pltpu.make_async_copy(wgrad.at[at], wgrad_out.at[at], sem.at[3 + k])
        copy.start()
        copies.append(copy)
    for copy in copies:
        copy.wait()


def body(
    n, m,
    images, cotangent, timesteps, class_ids, norm_gain, norm_bias, conv_first, conv_second,
    time_weight, time_bias, class_table, adaptive_weight, adaptive_bias,
):
    count, rows, cols, channels = images.shape
    assert count == 1 and rows >= REACH
    emb = time_weight.shape[1]
    vmem = pl.BlockSpec(memory_space=pltpu.VMEM)
    anywhere = pl.BlockSpec(memory_space=pl.ANY)
    padded = rows + 2 * REACH
    stack = 6 * m + (-6 * m) % 16
    own, more, most = rows * cols, (rows + 2) * cols, padded * cols
    dma = pltpu.SemaphoreType.DMA
    results = pl.pallas_call(
        functools.partial(kernel, n, m),
        out_shape=(
            jax.ShapeDtypeStruct(images.shape, BF16),
            jax.ShapeDtypeStruct(images.shape, BF16),
            jax.ShapeDtypeStruct((stack, emb), BF16),
            jax.ShapeDtypeStruct((stack, 2 * channels), BF16),
            jax.ShapeDtypeStruct((1, 2 * channels), F32),
        ),
        in_specs=[pl.BlockSpec(memory_space=pltpu.SMEM)] * 2
        + [pl.BlockSpec(memory_space=pltpu.HBM)] * 11,
        out_specs=(vmem,) * 5,
        scratch_shapes=[
            pltpu.VMEM((padded, cols, channels), BF16),
            pltpu.VMEM((padded, cols, channels), BF16),
            pltpu.VMEM(conv_first.shape, BF16),
            pltpu.VMEM(conv_second.shape, BF16),
            pltpu.VMEM(time_weight.shape, BF16),
            pltpu.VMEM(class_table.shape, BF16),
            pltpu.VMEM(adaptive_weight.shape, BF16),
            pltpu.VMEM((1, channels), F32),
            pltpu.VMEM((1, channels), F32),
            pltpu.VMEM((1, emb), F32),
            pltpu.VMEM((1, 2 * channels), F32),
            pltpu.VMEM((most, 3 * channels), BF16),
            pltpu.VMEM((most, 3 * channels), BF16),
            pltpu.VMEM((more, 3 * channels), BF16),
            pltpu.VMEM((more, 3 * channels), BF16),
            pltpu.VMEM((more, 3 * channels), BF16),
            pltpu.VMEM((more, 3 * channels), BF16),
            pltpu.VMEM((2 * channels, own), BF16),
            pltpu.VMEM((12 * GN_GROUPS, channels), BF16),
            pltpu.VMEM((more, channels), F32),
            pltpu.VMEM((max(more, 2 * own), channels), F32),
            pltpu.VMEM((more, channels), F32),
            pltpu.VMEM((more, channels), F32),
            pltpu.VMEM((own, channels), F32),
            pltpu.VMEM((own, channels), F32),
            pltpu.VMEM((4, n, 2, channels), F32),
            pltpu.VMEM((m, 1, emb), F32),
            pltpu.VMEM((m, n, 2, channels), F32),
            pltpu.VMEM((n, GN_GROUPS, 4 * GN_GROUPS), F32),
            pltpu.VMEM((SPARE, 1, channels), F32),
            dma((11,)),
            dma((3, 2)),
            dma((3, 2)),
            dma((1,)),
            dma((4,)),
            dma((1,)),
            dma((2,)),
            dma((1,)),
        ],
        compiler_params=pltpu.CompilerParams(
            collective_id=0, has_side_effects=True, vmem_limit_bytes=GRANT
        ),
    )(
        timesteps, class_ids,
        *(
            pltpu.with_memory_space_constraint(operand, pltpu.HBM)
            for operand in (
                norm_gain[None], norm_bias[None], time_bias[None],
                adaptive_bias[None], images, cotangent, conv_first, conv_second, time_weight,
                class_table, adaptive_weight,
            )
        )
    )
    branch, igrad, wgrad, bgrad = pl.pallas_call(
        finish,
        out_shape=(
            jax.ShapeDtypeStruct(images.shape, BF16),
            jax.ShapeDtypeStruct(images.shape, BF16),
            jax.ShapeDtypeStruct((emb, 2 * channels), F32),
            jax.ShapeDtypeStruct((1, 2 * channels), F32),
        ),
        in_specs=[anywhere] * 2 + [vmem] * 2 + [anywhere],
        out_specs=(anywhere,) * 4,
        scratch_shapes=[pltpu.VMEM((emb, 2 * channels), F32), dma((3 + PARTS,))],
        compiler_params=pltpu.CompilerParams(vmem_limit_bytes=GRANT),
    )(*results)
    return branch, igrad, wgrad, bgrad[0]


def solution(mesh):
    return jax.shard_map(
        functools.partial(body, mesh.shape["tile"], mesh.shape["image"]),
        mesh=mesh,
        in_specs=(
            P(("groups", "image"), "tile", None, None),
            P(("groups", "image"), "tile", None, None),
            P(("groups", "image")),
            P(("groups", "image")),
            P(),
            P(),
            P(),
            P(),
            P(None, "tile"),
            P("tile"),
            P(None, "tile"),
            P("tile", None),
            P(),
        ),
        out_specs=(
            P(("groups", "image"), "tile", None, None),
            P(("groups", "image"), "tile", None, None),
            P(("groups", "tile"), None),
            P("groups"),
        ),
        check_vma=False,
    )
```

```python
import functools
import math

import jax
import jax.numpy as jnp
from jax import lax
from jax.experimental import pallas as pl
from jax.experimental.pallas import tpu as pltpu
from jax.sharding import PartitionSpec as P

GN_GROUPS = 32
EPSILON = 1e-05
MESH = pl.DeviceIdType.MESH
F32 = jnp.float32
BF16 = jnp.bfloat16
GRANT = 24 << 20
REACH = 2
PARTS = 2
SPARE = 128
HIGHEST = lax.Precision.HIGHEST


def group_spread(values, width):
    count = values.shape[-1]
    lane = lax.broadcasted_iota(jnp.int32, values.shape, values.ndim - 1)
    step = 1
    while step < width:
        up = pltpu.roll(values, step, values.ndim - 1)
        down = pltpu.roll(values, count - step, values.ndim - 1)
        values = values + jnp.where((lane & step) != 0, up, down)
        step *= 2
    return values


def silu_slope(pre, sigma):
    return sigma * (1.0 + pre * (1.0 - sigma))


def column_sums(first, second):
    return jnp.concatenate(
        [jnp.sum(first, axis=0, keepdims=True), jnp.sum(second, axis=0, keepdims=True)], axis=0
    )


def kernel(
    n, m,
    steps_ref, ids_ref, gain_hbm, bias_hbm, tbias_hbm, abias_hbm,
    images_hbm, cot_hbm, first_hbm, second_hbm, tweight_hbm, table_hbm, aweight_hbm,
    branch, igrad, left_out, right_out, bgrad,
    images, cot, first, second, tweight, table, aweight,
    gain_ref, bias_ref, tbias_ref, abias_ref,
    near_first, near_second, near_hidden, near_scaled, wide_plain, tall, table_of,
    hidden, gact, nsecond, gpre, nfirst, slope,
    slots, acts, pairs, maps, spare,
    load_sem, halo_send, halo_recv, send_sem, slot_recv, act_recv, pair_recv, map_recv,
):
    me = lax.axis_index("tile")
    mine = lax.axis_index("image")
    rows, cols, channels = images_hbm.shape[1:]
    width = channels // GN_GROUPS
    cells = float(rows * cols * n * width)
    own = rows * cols
    above, below = me > 0, me < n - 1

    def load(source, target, k):
        return pltpu.make_async_copy(source, target, load_sem.at[k])

    loads = [
        load(images_hbm.at[0], images.at[pl.ds(REACH, rows)], 0),
        load(cot_hbm.at[0], cot.at[pl.ds(REACH, rows)], 1),
        load(tweight_hbm, tweight, 2),
        load(table_hbm, table, 3),
        load(aweight_hbm, aweight, 4),
        load(first_hbm, first, 5),
        load(second_hbm, second, 6),
        load(gain_hbm, gain_ref, 7),
        load(bias_hbm, bias_ref, 8),
        load(tbias_hbm, tbias_ref, 9),
        load(abias_hbm, abias_ref, 10),
    ]
    loads[0].start()
    barrier = pltpu.get_barrier_semaphore()
    for k in reversed(range(1, n)):
        pl.semaphore_signal(
            barrier, inc=1, device_id={"tile": lax.rem(me + k, n)}, device_id_type=MESH
        )
    for k in range(1, m):
        pl.semaphore_signal(
            barrier, inc=1, device_id={"image": lax.rem(mine + k, m)}, device_id_type=MESH
        )
    for k in (7, 8, 5, 2, 3, 4, 9, 10, 1, 6):
        loads[k].start()

    def remote(buffer, slot, receive, device):
        return pltpu.make_async_remote_copy(
            src_ref=buffer.at[slot],
            dst_ref=buffer.at[slot],
            send_sem=send_sem.at[0],
            recv_sem=receive,
            device_id=device,
            device_id_type=MESH,
        )

    def settle(lines, receive):
        while lines:
            part = min(lines, spare.shape[0])
            block = spare.at[pl.ds(0, part)]
            copy = pltpu.make_async_remote_copy(
                src_ref=block,
                dst_ref=block,
                send_sem=send_sem.at[0],
                recv_sem=send_sem.at[0] if receive is None else receive,
                device_id={"tile": lax.rem(me + 1, n)},
                device_id_type=MESH,
            )
            if receive is None:
                copy.wait_send()
            else:
                copy.wait_recv()
            lines -= part

    def tile_peer(k):
        return {"tile": lax.rem(me + k, n)}

    def share(stage, value):
        slots[stage, me] = value
        for k in range(1, n):
            remote(slots.at[stage], me, slot_recv.at[stage], tile_peer(k)).start()

    def total(stage):
        settle(2 * (n - 1), slot_recv.at[stage])
        summed = slots[stage, 0]
        for k in range(1, n):
            summed = summed + slots[stage, k]
        return summed

    HALOS = ((REACH, rows + REACH, rows + REACH - 1, REACH - 1, 1),
             (REACH + 1, rows + REACH + 1, rows + REACH - 2, REACH - 2, 1),
             (REACH, rows + REACH, rows, 0, REACH))

    def halo_copy(which, buffer, up):
        up_from, up_to, down_from, down_to, count = HALOS[which]
        source, target = (up_from, up_to) if up else (down_from, down_to)
        return pltpu.make_async_remote_copy(
            src_ref=buffer.at[pl.ds(source, count)],
            dst_ref=buffer.at[pl.ds(target, count)],
            send_sem=halo_send.at[which, int(up)],
            recv_sem=halo_recv.at[which, int(up)],
            device_id={"tile": me - 1 if up else me + 1},
            device_id_type=MESH,
        )

    def halo_start(which, buffer):
        _, low, _, high, count = HALOS[which]

        @pl.when(above)
        def _():
            halo_copy(which, buffer, True).start()

        @pl.when(below)
        def _():
            halo_copy(which, buffer, False).start()

        @pl.when(jnp.logical_not(above))
        def _():
            buffer[pl.ds(high, count)] = jnp.zeros((count, cols, channels), BF16)

        @pl.when(jnp.logical_not(below))
        def _():
            buffer[pl.ds(low, count)] = jnp.zeros((count, cols, channels), BF16)

    def halo_wait(which, buffer):
        @pl.when(below)
        def _():
            halo_copy(which, buffer, True).wait_recv()

        @pl.when(above)
        def _():
            halo_copy(which, buffer, False).wait_recv()

    column = lax.broadcasted_iota(jnp.int32, (cols, channels), 0)

    def widen(wide, row, values):
        before = jnp.where(column == 0, 0.0, pltpu.roll(values, 1, 0))
        after = jnp.where(column == cols - 1, 0.0, pltpu.roll(values, cols - 1, 0))
        at = pl.ds(row * cols, cols)
        wide[at, 0:channels] = before.astype(BF16)
        wide[at, channels : 2 * channels] = values.astype(BF16)
        wide[at, 2 * channels : 3 * channels] = after.astype(BF16)

    edge = jnp.zeros((1, channels), F32)

    def shifted(parts, count):
        lines = []
        for p in range(count):
            before, at, after = [part[p * cols : (p + 1) * cols] for part in parts]
            before = jnp.concatenate([edge, before[: cols - 1]], axis=0)
            after = jnp.concatenate([after[1:], edge], axis=0)
            lines.append(at + (before + after))
        return lines

    def conv(near, starts, count, weight):
        parts = [None] * 3
        for j in (0, 2, 1):
            for i in range(3):
                lines = [near[pl.ds((start + i) * cols, count * cols), :] for start in starts]
                product = jnp.dot(
                    lines[0] if len(lines) == 1 else jnp.concatenate(lines, axis=0),
                    weight[i, j],
                    preferred_element_type=F32,
                )
                parts[j] = product if i == 0 else parts[j] + product
        return shifted(parts, count * len(starts))

    def conv_back(lines_of, count, weight):
        parts = [None] * 3
        for j in (0, 2, 1):
            for i in range(3):
                product = lax.dot_general(
                    lines_of(i),
                    weight[2 - i, 2 - j],
                    (((1,), (1,)), ((), ())),
                    preferred_element_type=F32,
                )
                parts[j] = product if i == 0 else parts[j] + product
        return shifted(parts, count)

    def window(near, count):
        return lambda i: near[pl.ds(i * cols, count * cols), :]

    def pieces(values):
        parts = []
        for _ in range(3):
            part = values.astype(BF16)
            parts.append(part)
            values = values - part.astype(F32)
        return parts

    def moments(summed):
        spread = group_spread(summed, width) / cells
        centre = spread[0:1]
        variance = jnp.maximum(spread[1:2] - centre * centre, 0.0)
        return centre, lax.rsqrt(variance + EPSILON)

    def add_up(parts):
        return functools.reduce(jnp.add, parts)

    def gathered_sums(lines):
        folded = [
            add_up([jnp.sum(line[q].reshape(cols // 8, 8, channels), axis=0) for line in lines])
            for q in range(2)
        ]
        return column_sums(*folded)

    loads[0].wait()
    sums = []
    for p in range(rows):
        line = images[REACH + p].astype(F32)
        sums.append((line, line * line))
    sums = gathered_sums(sums)
    pl.semaphore_wait(barrier, n - 1 + m - 1)
    share(0, sums)
    halo_start(0, images)
    halo_start(1, images)

    for k in (2, 3, 4, 7, 8, 9, 10):
        loads[k].wait()
    half = tweight.shape[0] // 2
    index = lax.broadcasted_iota(jnp.int32, (half, 1), 0).astype(F32)
    angles = steps_ref[0].astype(F32) * jnp.exp(-math.log(10000.0) * index / half)
    pre_time = (
        jnp.sum(jnp.cos(angles) * tweight[0:half].astype(F32), axis=0, keepdims=True)
        + jnp.sum(jnp.sin(angles) * tweight[half:].astype(F32), axis=0, keepdims=True)
        + tbias_ref[...]
    )
    entry = lax.broadcasted_iota(jnp.int32, table.shape, 0) == ids_ref[0]
    picked = jnp.sum(jnp.where(entry, table[...].astype(F32), 0.0), axis=0, keepdims=True)
    embedding = pre_time * jax.nn.sigmoid(pre_time) + picked
    activated = embedding * jax.nn.sigmoid(embedding)
    acts[mine] = activated
    for k in range(1, m):
        remote(acts, mine, act_recv.at[0], {"image": lax.rem(mine + k, m)}).start()
    partial = jnp.dot(
        jnp.broadcast_to(activated, (8, activated.shape[1])),
        aweight[...].astype(F32),
        precision=HIGHEST,
        preferred_element_type=F32,
    )[0:1]
    share(1, jnp.concatenate([partial[:, :channels], partial[:, channels:]], axis=0))

    loads[1].wait()
    halo_start(2, cot)

    loads[5].wait()
    halo_wait(0, images)
    gain, bias = gain_ref[...], bias_ref[...]
    centre, inverse_first = moments(total(0))
    stretch = 0.5 * inverse_first * gain
    offset = 0.5 * bias - centre * stretch

    def first_row(row, inside):
        lean = images[row].astype(F32) * stretch + offset
        value = lean * (1.0 + jnp.tanh(lean))
        if inside is not None:
            value = jnp.where(inside, value, 0.0)
        near_first[pl.ds(row * cols, cols)] = value.astype(BF16)

    first_row(REACH - 1, above)
    for p in range(rows):
        first_row(REACH + p, None)
    first_row(rows + REACH, below)
    centre_rows = [
        line.astype(BF16).astype(F32) for line in conv(near_first, (1,), rows, first)
    ]
    share(2, gathered_sums([(line, line * line) for line in centre_rows]))
    for p, line in enumerate(centre_rows):
        hidden[pl.ds((1 + p) * cols, cols)] = line

    halo_wait(1, images)
    first_row(0, above)
    first_row(rows + 2 * REACH - 1, below)
    for row, line in zip((0, rows + 1), conv(near_first, (0, rows + 1), 1, first)):
        hidden[pl.ds(row * cols, cols)] = line.astype(BF16).astype(F32)

    whole_rows, first_cells, last_cells = [[], []], [[], []], [[], []]
    for p in range(rows):
        at = pl.ds(p * cols, cols)
        line = images[REACH + p].astype(F32)
        lean = line * stretch + offset
        bend = jnp.tanh(lean)
        steep = (0.5 * gain) * ((1.0 + bend) * (1.0 + lean * (1.0 - bend)))
        line = (line - centre) * inverse_first
        nfirst[at] = line
        slope[at] = steep
        for part, lines in enumerate((steep, steep * line)):
            lines = lines.astype(BF16).astype(F32)
            gact[at if part == 0 else pl.ds((rows + p) * cols, cols)] = lines
            whole_rows[part].append(jnp.sum(lines, axis=0, keepdims=True))
            first_cells[part].append(lines[0:1])
            last_cells[part].append(lines[cols - 1 : cols])
    edges = []
    for part in range(2):
        tall[pl.ds(part * channels, channels), :] = gact[pl.ds(part * own, own)].T.astype(BF16)
        kept = [
            [a - b for a, b in zip(whole_rows[part], first_cells[part])],
            whole_rows[part],
            [a - b for a, b in zip(whole_rows[part], last_cells[part])],
        ]
        grid = []
        for i in range(3):
            for j in range(3):
                value = add_up(kept[j])
                if i == 0:
                    value = value - jnp.where(above, 0.0, kept[j][0])
                elif i == 2:
                    value = value - jnp.where(below, 0.0, kept[j][rows - 1])
                grid.append(value)
        edges.append(grid)
    for row in range(rows + 2):
        lines = hidden[pl.ds(row * cols, cols)]
        if row == 0:
            lines = jnp.where(above, lines, 0.0)
        elif row == rows + 1:
            lines = jnp.where(below, lines, 0.0)
        widen(wide_plain, row, lines)
    same = (
        lax.broadcasted_iota(jnp.int32, (GN_GROUPS, channels), 1) // width
        == lax.broadcasted_iota(jnp.int32, (GN_GROUPS, channels), 0)
    )
    products, constants = [None, None], None
    for i in range(3):
        for j in range(3):
            taps = first[2 - i, 2 - j]
            wide_taps = taps.astype(F32)
            near = wide_plain[pl.ds(i * cols, own), j * channels : (j + 1) * channels]
            for part in range(2):
                product = wide_taps * jnp.dot(
                    tall[pl.ds(part * channels, channels), :], near, preferred_element_type=F32
                )
                products[part] = product if i + j == 0 else products[part] + product
            spread_rows = [
                jnp.where(same, piece.astype(F32), 0.0)
                for part in range(2)
                for piece in pieces(edges[part][3 * i + j])
            ]
            product = jnp.dot(
                jnp.concatenate(spread_rows, axis=0).astype(BF16), taps, preferred_element_type=F32
            )
            constants = product if i + j == 0 else constants + product
    blocks = [
        jnp.sum(product.reshape(GN_GROUPS, width, channels), axis=1) for product in products
    ] + [
        add_up(
            [constants[(3 * part + q) * GN_GROUPS : (3 * part + q + 1) * GN_GROUPS] for q in range(3)]
        )
        for part in range(2)
    ]
    columns_of = [pieces(block) for block in blocks]
    lanes = 4 * GN_GROUPS
    gathered = None
    for quarter in range(4):
        row = lax.broadcasted_iota(jnp.int32, (channels, lanes), 0)
        lane = lax.broadcasted_iota(jnp.int32, (channels, lanes), 1)
        chosen = jnp.where(row // width + quarter * GN_GROUPS == lane, 1.0, 0.0).astype(BF16)
        product = jnp.dot(
            jnp.concatenate(columns_of[quarter], axis=0), chosen, preferred_element_type=F32
        )
        gathered = product if gathered is None else gathered + product
    maps[me] = add_up([gathered[q * GN_GROUPS : (q + 1) * GN_GROUPS] for q in range(3)])
    for k in range(1, n):
        remote(maps, me, map_recv.at[0], tile_peer(k)).start()

    halo_wait(2, cot)
    loads[6].wait()
    spans = lambda i: cot[pl.ds(i, rows + 2)].reshape((rows + 2) * cols, channels)
    for row, line in enumerate(conv_back(spans, rows + 2, second)):
        gact[pl.ds(row * cols, cols)] = line

    modulation = total(1)
    factor = 1.0 + (modulation[0:1] + abias_ref[:, :channels])
    shift = modulation[1:2] + abias_ref[:, channels:]
    centre, inverse_second = moments(total(2))

    def second_row(row):
        at = pl.ds(row * cols, cols)
        normed = (hidden[at] - centre) * inverse_second
        lean = normed * (0.5 * factor) + 0.5 * shift
        bend = jnp.tanh(lean)
        rise = 1.0 + bend
        back = gact[at] * (0.5 * rise * (1.0 + lean * (1.0 - bend)))
        nsecond[at] = normed
        gact[at] = lean * rise
        gpre[at] = back
        return back * normed, back

    pairs[mine, me] = gathered_sums([second_row(1 + p) for p in range(rows)])
    others = [(k, step) for step in range(m) for k in range(n) if k or step]
    for k, step in others:
        remote(
            pairs.at[mine], me, pair_recv.at[min(step, 1)],
            {"tile": lax.rem(me + k, n), "image": lax.rem(mine + step, m)},
        ).start()

    scale = factor * inverse_second
    second_row(0)
    second_row(rows + 1)

    def masked(row, values):
        if row == 0:
            return jnp.where(above, values, 0.0)
        if row == rows + 1:
            return jnp.where(below, values, 0.0)
        return values

    for row in range(rows + 2):
        at = pl.ds(row * cols, cols)
        back = gpre[at] * scale
        gpre[at] = back
        near_scaled[at] = masked(row, back).astype(BF16)
    gradient = conv_back(window(near_scaled, rows), rows, first)
    sums = []
    for p in range(rows):
        at = pl.ds(p * cols, cols)
        early = gradient[p] * slope[at]
        sums.append((early, early * nfirst[at]))
    share(3, gathered_sums(sums))

    for row in range(rows + 2):
        at = pl.ds(row * cols, cols)
        near_second[at] = masked(row, gact[at]).astype(BF16)
    for p, line in enumerate(conv(near_second, (0,), rows, second)):
        branch[0, p] = line.astype(BF16)

    settle(maps.shape[1] * maps.shape[2] // channels * (n - 1), map_recv.at[0])
    summed = add_up([maps[k] for k in range(n)])
    spread_of = jnp.where(same, 1.0, 0.0)
    for q, piece in enumerate(pieces(summed)):
        table_of[pl.ds(q * lanes, lanes), :] = lax.dot_general(
            piece.astype(F32), spread_of, (((0,), (0,)), ((), ())), preferred_element_type=F32
        ).astype(BF16)

    settle((m - 1) * acts.shape[2] // channels, act_recv.at[0])
    extra = (-6 * m) % 16

    def stacked(parts):
        if extra:
            parts = parts + [jnp.zeros((extra, parts[0].shape[1]), F32)]
        return jnp.concatenate(parts, axis=0).astype(BF16)

    thirds = [[piece.astype(F32) for piece in pieces(acts[k])] for k in range(m)]
    left_out[...] = stacked([thirds[k][q] for q in (0, 0, 1, 0, 1, 2) for k in range(m)])

    settle(2 * (n - 1), pair_recv.at[0])

    def whole(image):
        return add_up([pairs[image, k] for k in range(n)])

    spread = group_spread(whole(mine) * factor, width) / cells
    paired_mean, plain_mean = inverse_second * spread[0:1], inverse_second * spread[1:2]
    for row in range(rows + 2):
        at = pl.ds(row * cols, cols)
        back = gpre[at] - plain_mean - nsecond[at] * paired_mean
        near_hidden[at] = masked(row, back).astype(BF16)

    tilt = paired_mean * inverse_second
    level = plain_mean - tilt * centre
    row = lax.broadcasted_iota(jnp.int32, (channels, lanes), 0)
    lane = lax.broadcasted_iota(jnp.int32, (channels, lanes), 1)
    chosen = jnp.where(lax.rem(lane, GN_GROUPS) * width == row, 1.0, 0.0).astype(BF16)
    short = [piece.astype(F32) for piece in pieces(level) + pieces(tilt)]
    short = jnp.concatenate(short + [jnp.zeros((2, channels), F32)], axis=0).astype(BF16)
    short = jnp.dot(short, chosen, preferred_element_type=F32)
    quarter = lax.broadcasted_iota(jnp.int32, (1, lanes), 1) // GN_GROUPS
    nothing = jnp.zeros((1, lanes), F32)
    left = []
    for part in range(2):
        mixed = [
            jnp.where(quarter == part, short[3 + q : 4 + q], jnp.where(quarter == part + 2, short[q : q + 1], 0.0))
            for q in range(3)
        ]
        left += [
            jnp.concatenate([mixed[q]] * (3 - q) + [nothing] * q, axis=1) for q in range(3)
        ]
    left = jnp.concatenate(left + [jnp.zeros((2, 3 * lanes), F32)], axis=0).astype(BF16)
    moved = jnp.dot(left, table_of[...], preferred_element_type=F32)
    moved = jnp.concatenate(
        [jnp.sum(moved[3 * part : 3 * part + 3], axis=0, keepdims=True) for part in range(2)], axis=0
    )

    gradient = conv_back(window(near_hidden, rows), rows, first)

    spread = (group_spread(total(3), width) - moved) / cells
    for p in range(rows):
        at = pl.ds(p * cols, cols)
        back = gradient[p] * slope[at]
        result = inverse_first * (back - spread[0:1] - nfirst[at] * spread[1:2])
        igrad[0, p] = result.astype(BF16)

    settle(2 * n * (m - 1), pair_recv.at[1])
    sums = [whole(k) for k in range(m)]
    for part in range(2):
        lines = [value[part : part + 1] for value in sums]
        thirds = [[piece.astype(F32) for piece in pieces(line)] for line in lines]
        columns = slice(part * channels, (part + 1) * channels)
        right_out[:, columns] = stacked([thirds[k][q] for q in (0, 1, 0, 2, 1, 0) for k in range(m)])
        bgrad[:, columns] = add_up(lines)

    lines = 2 * (4 * (n - 1) + len(others)) + (m - 1) * acts.shape[2] // channels
    lines += maps.shape[1] * maps.shape[2] // channels * (n - 1)
    settle(lines, None)
    for which, buffer in enumerate((images, images, cot)):

        @pl.when(above)
        def _():
            halo_copy(which, buffer, True).wait_send()

        @pl.when(below)
        def _():
            halo_copy(which, buffer, False).wait_send()


def finish(branch, igrad, left, right, bgrad, branch_out, igrad_out, wgrad_out, bgrad_out, wgrad, sem):
    copies = [
        pltpu.make_async_copy(source, target, sem.at[k])
        for k, (source, target) in enumerate(
            [(igrad, igrad_out), (branch, branch_out), (bgrad, bgrad_out)]
        )
    ]
    for copy in copies:
        copy.start()
    height = wgrad.shape[0] // PARTS
    for k in range(PARTS):
        at = pl.ds(k * height, height)
        wgrad[at] = lax.dot_general(
            left[:, k * height : (k + 1) * height], right[...],
            (((0,), (0,)), ((), ())), preferred_element_type=F32,
        )
        copy = pltpu.make_async_copy(wgrad.at[at], wgrad_out.at[at], sem.at[3 + k])
        copy.start()
        copies.append(copy)
    for copy in copies:
        copy.wait()


def body(
    n, m,
    images, cotangent, timesteps, class_ids, norm_gain, norm_bias, conv_first, conv_second,
    time_weight, time_bias, class_table, adaptive_weight, adaptive_bias,
):
    count, rows, cols, channels = images.shape
    assert count == 1 and rows >= REACH
    emb = time_weight.shape[1]
    vmem = pl.BlockSpec(memory_space=pltpu.VMEM)
    anywhere = pl.BlockSpec(memory_space=pl.ANY)
    padded = rows + 2 * REACH
    stack = 6 * m + (-6 * m) % 16
    own, more, most = rows * cols, (rows + 2) * cols, padded * cols
    dma = pltpu.SemaphoreType.DMA
    results = pl.pallas_call(
        functools.partial(kernel, n, m),
        out_shape=(
            jax.ShapeDtypeStruct(images.shape, BF16),
            jax.ShapeDtypeStruct(images.shape, BF16),
            jax.ShapeDtypeStruct((stack, emb), BF16),
            jax.ShapeDtypeStruct((stack, 2 * channels), BF16),
            jax.ShapeDtypeStruct((1, 2 * channels), F32),
        ),
        in_specs=[pl.BlockSpec(memory_space=pltpu.SMEM)] * 2
        + [pl.BlockSpec(memory_space=pltpu.HBM)] * 11,
        out_specs=(vmem,) * 5,
        scratch_shapes=[
            pltpu.VMEM((padded, cols, channels), BF16),
            pltpu.VMEM((padded, cols, channels), BF16),
            pltpu.VMEM(conv_first.shape, BF16),
            pltpu.VMEM(conv_second.shape, BF16),
            pltpu.VMEM(time_weight.shape, BF16),
            pltpu.VMEM(class_table.shape, BF16),
            pltpu.VMEM(adaptive_weight.shape, BF16),
            pltpu.VMEM((1, channels), F32),
            pltpu.VMEM((1, channels), F32),
            pltpu.VMEM((1, emb), F32),
            pltpu.VMEM((1, 2 * channels), F32),
            pltpu.VMEM((most, channels), BF16),
            pltpu.VMEM((more, channels), BF16),
            pltpu.VMEM((more, channels), BF16),
            pltpu.VMEM((more, channels), BF16),
            pltpu.VMEM((more, 3 * channels), BF16),
            pltpu.VMEM((2 * channels, own), BF16),
            pltpu.VMEM((12 * GN_GROUPS, channels), BF16),
            pltpu.VMEM((more, channels), F32),
            pltpu.VMEM((max(more, 2 * own), channels), F32),
            pltpu.VMEM((more, channels), F32),
            pltpu.VMEM((more, channels), F32),
            pltpu.VMEM((own, channels), F32),
            pltpu.VMEM((own, channels), F32),
            pltpu.VMEM((4, n, 2, channels), F32),
            pltpu.VMEM((m, 1, emb), F32),
            pltpu.VMEM((m, n, 2, channels), F32),
            pltpu.VMEM((n, GN_GROUPS, 4 * GN_GROUPS), F32),
            pltpu.VMEM((SPARE, 1, channels), F32),
            dma((11,)),
            dma((3, 2)),
            dma((3, 2)),
            dma((1,)),
            dma((4,)),
            dma((1,)),
            dma((2,)),
            dma((1,)),
        ],
        compiler_params=pltpu.CompilerParams(
            collective_id=0, has_side_effects=True, vmem_limit_bytes=GRANT
        ),
    )(
        timesteps, class_ids,
        *(
            pltpu.with_memory_space_constraint(operand, pltpu.HBM)
            for operand in (
                norm_gain[None], norm_bias[None], time_bias[None],
                adaptive_bias[None], images, cotangent, conv_first, conv_second, time_weight,
                class_table, adaptive_weight,
            )
        )
    )
    branch, igrad, wgrad, bgrad = pl.pallas_call(
        finish,
        out_shape=(
            jax.ShapeDtypeStruct(images.shape, BF16),
            jax.ShapeDtypeStruct(images.shape, BF16),
            jax.ShapeDtypeStruct((emb, 2 * channels), F32),
            jax.ShapeDtypeStruct((1, 2 * channels), F32),
        ),
        in_specs=[anywhere] * 2 + [vmem] * 2 + [anywhere],
        out_specs=(anywhere,) * 4,
        scratch_shapes=[pltpu.VMEM((emb, 2 * channels), F32), dma((3 + PARTS,))],
        compiler_params=pltpu.CompilerParams(vmem_limit_bytes=GRANT),
    )(*results)
    return branch, igrad, wgrad, bgrad[0]


def solution(mesh):
    return jax.shard_map(
        functools.partial(body, mesh.shape["tile"], mesh.shape["image"]),
        mesh=mesh,
        in_specs=(
            P(("groups", "image"), "tile", None, None),
            P(("groups", "image"), "tile", None, None),
            P(("groups", "image")),
            P(("groups", "image")),
            P(),
            P(),
            P(),
            P(),
            P(None, "tile"),
            P("tile"),
            P(None, "tile"),
            P("tile", None),
            P(),
        ),
        out_specs=(
            P(("groups", "image"), "tile", None, None),
            P(("groups", "image"), "tile", None, None),
            P(("groups", "tile"), None),
            P("groups"),
        ),
        check_vma=False,
    )
```

```python
import functools
import math

import jax
import jax.numpy as jnp
from jax import lax
from jax.experimental import pallas as pl
from jax.experimental.pallas import tpu as pltpu
from jax.sharding import PartitionSpec as P

GN_GROUPS = 32
EPSILON = 1e-05
MESH = pl.DeviceIdType.MESH
F32 = jnp.float32
BF16 = jnp.bfloat16
GRANT = 24 << 20
REACH = 2
PARTS = 2
SPARE = 128
HIGHEST = lax.Precision.HIGHEST


def group_spread(values, width):
    count = values.shape[-1]
    lane = lax.broadcasted_iota(jnp.int32, values.shape, values.ndim - 1)
    step = 1
    while step < width:
        up = pltpu.roll(values, step, values.ndim - 1)
        down = pltpu.roll(values, count - step, values.ndim - 1)
        values = values + jnp.where((lane & step) != 0, up, down)
        step *= 2
    return values


def silu_slope(pre, sigma):
    return sigma * (1.0 + pre * (1.0 - sigma))


def column_sums(first, second):
    return jnp.concatenate(
        [jnp.sum(first, axis=0, keepdims=True), jnp.sum(second, axis=0, keepdims=True)], axis=0
    )


def kernel(
    n, m,
    steps_ref, ids_ref, gain_hbm, bias_hbm, tbias_hbm, abias_hbm,
    images_hbm, cot_hbm, first_hbm, second_hbm, tweight_hbm, table_hbm, aweight_hbm,
    branch, igrad, left_out, right_out, bgrad,
    images, cot, first, second, first_back, second_back, tweight, table, aweight,
    gain_ref, bias_ref, tbias_ref, abias_ref,
    near_first, near_second, near_hidden, near_scaled, wide_plain, tall, table_of,
    hidden, gact, nsecond, gpre, nfirst, slope,
    slots, acts, pairs, maps, spare,
    load_sem, halo_send, halo_recv, send_sem, slot_recv, act_recv, pair_recv, map_recv,
):
    me = lax.axis_index("tile")
    mine = lax.axis_index("image")
    rows, cols, channels = images_hbm.shape[1:]
    width = channels // GN_GROUPS
    cells = float(rows * cols * n * width)
    own = rows * cols
    above, below = me > 0, me < n - 1

    def load(source, target, k):
        return pltpu.make_async_copy(source, target, load_sem.at[k])

    loads = [
        load(images_hbm.at[0], images.at[pl.ds(REACH, rows)], 0),
        load(cot_hbm.at[0], cot.at[pl.ds(REACH, rows)], 1),
        load(tweight_hbm, tweight, 2),
        load(table_hbm, table, 3),
        load(aweight_hbm, aweight, 4),
        load(first_hbm, first, 5),
        load(second_hbm, second, 6),
        load(gain_hbm, gain_ref, 7),
        load(bias_hbm, bias_ref, 8),
        load(tbias_hbm, tbias_ref, 9),
        load(abias_hbm, abias_ref, 10),
    ]
    loads[0].start()
    barrier = pltpu.get_barrier_semaphore()
    for k in reversed(range(1, n)):
        pl.semaphore_signal(
            barrier, inc=1, device_id={"tile": lax.rem(me + k, n)}, device_id_type=MESH
        )
    for k in range(1, m):
        pl.semaphore_signal(
            barrier, inc=1, device_id={"image": lax.rem(mine + k, m)}, device_id_type=MESH
        )
    for k in (7, 8, 5, 2, 3, 4, 9, 10, 1, 6):
        loads[k].start()

    def remote(buffer, slot, receive, device):
        return pltpu.make_async_remote_copy(
            src_ref=buffer.at[slot],
            dst_ref=buffer.at[slot],
            send_sem=send_sem.at[0],
            recv_sem=receive,
            device_id=device,
            device_id_type=MESH,
        )

    def settle(lines, receive):
        while lines:
            part = min(lines, spare.shape[0])
            block = spare.at[pl.ds(0, part)]
            copy = pltpu.make_async_remote_copy(
                src_ref=block,
                dst_ref=block,
                send_sem=send_sem.at[0],
                recv_sem=send_sem.at[0] if receive is None else receive,
                device_id={"tile": lax.rem(me + 1, n)},
                device_id_type=MESH,
            )
            if receive is None:
                copy.wait_send()
            else:
                copy.wait_recv()
            lines -= part

    def tile_peer(k):
        return {"tile": lax.rem(me + k, n)}

    def share(stage, value):
        slots[stage, me] = value
        for k in range(1, n):
            remote(slots.at[stage], me, slot_recv.at[stage], tile_peer(k)).start()

    def total(stage):
        settle(2 * (n - 1), slot_recv.at[stage])
        summed = slots[stage, 0]
        for k in range(1, n):
            summed = summed + slots[stage, k]
        return summed

    HALOS = ((REACH, rows + REACH, rows + REACH - 1, REACH - 1, 1),
             (REACH + 1, rows + REACH + 1, rows + REACH - 2, REACH - 2, 1),
             (REACH, rows + REACH, rows, 0, REACH))

    def halo_copy(which, buffer, up):
        up_from, up_to, down_from, down_to, count = HALOS[which]
        source, target = (up_from, up_to) if up else (down_from, down_to)
        return pltpu.make_async_remote_copy(
            src_ref=buffer.at[pl.ds(source, count)],
            dst_ref=buffer.at[pl.ds(target, count)],
            send_sem=halo_send.at[which, int(up)],
            recv_sem=halo_recv.at[which, int(up)],
            device_id={"tile": me - 1 if up else me + 1},
            device_id_type=MESH,
        )

    def halo_start(which, buffer):
        _, low, _, high, count = HALOS[which]

        @pl.when(above)
        def _():
            halo_copy(which, buffer, True).start()

        @pl.when(below)
        def _():
            halo_copy(which, buffer, False).start()

        @pl.when(jnp.logical_not(above))
        def _():
            buffer[pl.ds(high, count)] = jnp.zeros((count, cols, channels), BF16)

        @pl.when(jnp.logical_not(below))
        def _():
            buffer[pl.ds(low, count)] = jnp.zeros((count, cols, channels), BF16)

    def halo_wait(which, buffer):
        @pl.when(below)
        def _():
            halo_copy(which, buffer, True).wait_recv()

        @pl.when(above)
        def _():
            halo_copy(which, buffer, False).wait_recv()

    column = lax.broadcasted_iota(jnp.int32, (cols, channels), 0)

    def widen(wide, row, values):
        before = jnp.where(column == 0, 0.0, pltpu.roll(values, 1, 0))
        after = jnp.where(column == cols - 1, 0.0, pltpu.roll(values, cols - 1, 0))
        at = pl.ds(row * cols, cols)
        wide[at, 0:channels] = before.astype(BF16)
        wide[at, channels : 2 * channels] = values.astype(BF16)
        wide[at, 2 * channels : 3 * channels] = after.astype(BF16)

    edge = jnp.zeros((1, channels), F32)

    def shifted(parts, count):
        lines = []
        for p in range(count):
            before, at, after = [part[p * cols : (p + 1) * cols] for part in parts]
            before = jnp.concatenate([edge, before[: cols - 1]], axis=0)
            after = jnp.concatenate([after[1:], edge], axis=0)
            lines.append(at + (before + after))
        return lines

    def conv(near, starts, count, weight):
        parts = [None] * 3
        for j in (0, 2, 1):
            for i in range(3):
                lines = [near[pl.ds((start + i) * cols, count * cols), :] for start in starts]
                product = jnp.dot(
                    lines[0] if len(lines) == 1 else jnp.concatenate(lines, axis=0),
                    weight[i, j],
                    preferred_element_type=F32,
                )
                parts[j] = product if i == 0 else parts[j] + product
        return shifted(parts, count * len(starts))

    def conv_back(lines_of, count, weight):
        parts = [None] * 3
        for j in (0, 2, 1):
            for i in range(3):
                product = jnp.dot(
                    lines_of(i), weight[2 - i, 2 - j], preferred_element_type=F32
                )
                parts[j] = product if i == 0 else parts[j] + product
        return shifted(parts, count)

    def window(near, start, count):
        return lambda i: near[pl.ds((start + i) * cols, count * cols), :]

    halves = [(0, rows // 2), (rows // 2, rows - rows // 2)]

    def pieces(values):
        parts = []
        for _ in range(3):
            part = values.astype(BF16)
            parts.append(part)
            values = values - part.astype(F32)
        return parts

    def moments(summed):
        spread = group_spread(summed, width) / cells
        centre = spread[0:1]
        variance = jnp.maximum(spread[1:2] - centre * centre, 0.0)
        return centre, lax.rsqrt(variance + EPSILON)

    def add_up(parts):
        return functools.reduce(jnp.add, parts)

    def gathered_sums(lines):
        folded = [
            add_up([jnp.sum(line[q].reshape(cols // 8, 8, channels), axis=0) for line in lines])
            for q in range(2)
        ]
        return column_sums(*folded)

    loads[0].wait()
    sums = []
    for p in range(rows):
        line = images[REACH + p].astype(F32)
        sums.append((line, line * line))
    sums = gathered_sums(sums)
    pl.semaphore_wait(barrier, n - 1 + m - 1)
    share(0, sums)
    halo_start(0, images)
    halo_start(1, images)

    for k in (2, 3, 4, 7, 8, 9, 10):
        loads[k].wait()
    half = tweight.shape[0] // 2
    index = lax.broadcasted_iota(jnp.int32, (half, 1), 0).astype(F32)
    angles = steps_ref[0].astype(F32) * jnp.exp(-math.log(10000.0) * index / half)
    pre_time = (
        jnp.sum(jnp.cos(angles) * tweight[0:half].astype(F32), axis=0, keepdims=True)
        + jnp.sum(jnp.sin(angles) * tweight[half:].astype(F32), axis=0, keepdims=True)
        + tbias_ref[...]
    )
    entry = lax.broadcasted_iota(jnp.int32, table.shape, 0) == ids_ref[0]
    picked = jnp.sum(jnp.where(entry, table[...].astype(F32), 0.0), axis=0, keepdims=True)
    embedding = pre_time * jax.nn.sigmoid(pre_time) + picked
    activated = embedding * jax.nn.sigmoid(embedding)
    acts[mine] = activated
    for k in range(1, m):
        remote(acts, mine, act_recv.at[0], {"image": lax.rem(mine + k, m)}).start()
    partial = jnp.dot(
        jnp.broadcast_to(activated, (8, activated.shape[1])),
        aweight[...].astype(F32),
        precision=HIGHEST,
        preferred_element_type=F32,
    )[0:1]
    share(1, jnp.concatenate([partial[:, :channels], partial[:, channels:]], axis=0))

    loads[1].wait()
    halo_start(2, cot)

    for k, weight, turned in ((5, first, first_back), (6, second, second_back)):
        loads[k].wait()
        for i in range(3):
            for j in range(3):
                turned[i, j] = weight[i, j].T
    halo_wait(0, images)
    gain, bias = gain_ref[...], bias_ref[...]
    centre, inverse_first = moments(total(0))
    stretch = 0.5 * inverse_first * gain
    offset = 0.5 * bias - centre * stretch

    def first_row(row, inside):
        lean = images[row].astype(F32) * stretch + offset
        value = lean * (1.0 + jnp.tanh(lean))
        if inside is not None:
            value = jnp.where(inside, value, 0.0)
        near_first[pl.ds(row * cols, cols)] = value.astype(BF16)

    centre_rows, done = [], 0
    for start, count in halves:
        while done < start + count + 2:
            row = REACH - 1 + done
            first_row(row, above if done == 0 else below if done == rows + 1 else None)
            done += 1
        centre_rows += [
            line.astype(BF16).astype(F32)
            for line in conv(near_first, (1 + start,), count, first)
        ]
    share(2, gathered_sums([(line, line * line) for line in centre_rows]))
    for p, line in enumerate(centre_rows):
        hidden[pl.ds((1 + p) * cols, cols)] = line

    halo_wait(1, images)
    first_row(0, above)
    first_row(rows + 2 * REACH - 1, below)
    for row, line in zip((0, rows + 1), conv(near_first, (0, rows + 1), 1, first)):
        hidden[pl.ds(row * cols, cols)] = line.astype(BF16).astype(F32)

    whole_rows, first_cells, last_cells = [[], []], [[], []], [[], []]
    for p in range(rows):
        at = pl.ds(p * cols, cols)
        line = images[REACH + p].astype(F32)
        lean = line * stretch + offset
        bend = jnp.tanh(lean)
        steep = (0.5 * gain) * ((1.0 + bend) * (1.0 + lean * (1.0 - bend)))
        line = (line - centre) * inverse_first
        nfirst[at] = line
        slope[at] = steep
        for part, lines in enumerate((steep, steep * line)):
            lines = lines.astype(BF16).astype(F32)
            gact[at if part == 0 else pl.ds((rows + p) * cols, cols)] = lines
            whole_rows[part].append(jnp.sum(lines, axis=0, keepdims=True))
            first_cells[part].append(lines[0:1])
            last_cells[part].append(lines[cols - 1 : cols])
    edges = []
    for part in range(2):
        tall[pl.ds(part * channels, channels), :] = gact[pl.ds(part * own, own)].T.astype(BF16)
        kept = [
            [a - b for a, b in zip(whole_rows[part], first_cells[part])],
            whole_rows[part],
            [a - b for a, b in zip(whole_rows[part], last_cells[part])],
        ]
        grid = []
        for i in range(3):
            for j in range(3):
                value = add_up(kept[j])
                if i == 0:
                    value = value - jnp.where(above, 0.0, kept[j][0])
                elif i == 2:
                    value = value - jnp.where(below, 0.0, kept[j][rows - 1])
                grid.append(value)
        edges.append(grid)
    for row in range(rows + 2):
        lines = hidden[pl.ds(row * cols, cols)]
        if row == 0:
            lines = jnp.where(above, lines, 0.0)
        elif row == rows + 1:
            lines = jnp.where(below, lines, 0.0)
        widen(wide_plain, row, lines)
    same = (
        lax.broadcasted_iota(jnp.int32, (GN_GROUPS, channels), 1) // width
        == lax.broadcasted_iota(jnp.int32, (GN_GROUPS, channels), 0)
    )
    products, constants = [None, None], None
    for i in range(3):
        for j in range(3):
            taps = first[2 - i, 2 - j]
            wide_taps = taps.astype(F32)
            near = wide_plain[pl.ds(i * cols, own), j * channels : (j + 1) * channels]
            for part in range(2):
                product = wide_taps * jnp.dot(
                    tall[pl.ds(part * channels, channels), :], near, preferred_element_type=F32
                )
                products[part] = product if i + j == 0 else products[part] + product
            spread_rows = [
                jnp.where(same, piece.astype(F32), 0.0)
                for part in range(2)
                for piece in pieces(edges[part][3 * i + j])
            ]
            product = jnp.dot(
                jnp.concatenate(spread_rows, axis=0).astype(BF16), taps, preferred_element_type=F32
            )
            constants = product if i + j == 0 else constants + product
    blocks = [
        jnp.sum(product.reshape(GN_GROUPS, width, channels), axis=1) for product in products
    ] + [
        add_up(
            [constants[(3 * part + q) * GN_GROUPS : (3 * part + q + 1) * GN_GROUPS] for q in range(3)]
        )
        for part in range(2)
    ]
    columns_of = [pieces(block) for block in blocks]
    lanes = 4 * GN_GROUPS
    gathered = None
    for quarter in range(4):
        row = lax.broadcasted_iota(jnp.int32, (channels, lanes), 0)
        lane = lax.broadcasted_iota(jnp.int32, (channels, lanes), 1)
        chosen = jnp.where(row // width + quarter * GN_GROUPS == lane, 1.0, 0.0).astype(BF16)
        product = jnp.dot(
            jnp.concatenate(columns_of[quarter], axis=0), chosen, preferred_element_type=F32
        )
        gathered = product if gathered is None else gathered + product
    maps[me] = add_up([gathered[q * GN_GROUPS : (q + 1) * GN_GROUPS] for q in range(3)])
    for k in range(1, n):
        remote(maps, me, map_recv.at[0], tile_peer(k)).start()

    halo_wait(2, cot)
    count = (rows + 2) // 2
    for start in (0, rows + 2 - count):
        spans = lambda i: cot[pl.ds(start + i, count)].reshape(count * cols, channels)
        for p, line in enumerate(conv_back(spans, count, second_back)):
            gact[pl.ds((start + p) * cols, cols)] = line

    modulation = total(1)
    factor = 1.0 + (modulation[0:1] + abias_ref[:, :channels])
    shift = modulation[1:2] + abias_ref[:, channels:]
    centre, inverse_second = moments(total(2))

    def second_row(row):
        at = pl.ds(row * cols, cols)
        normed = (hidden[at] - centre) * inverse_second
        lean = normed * (0.5 * factor) + 0.5 * shift
        bend = jnp.tanh(lean)
        rise = 1.0 + bend
        back = gact[at] * (0.5 * rise * (1.0 + lean * (1.0 - bend)))
        nsecond[at] = normed
        gact[at] = lean * rise
        gpre[at] = back
        return back * normed, back

    pairs[mine, me] = gathered_sums([second_row(1 + p) for p in range(rows)])
    others = [(k, step) for step in range(m) for k in range(n) if k or step]
    for k, step in others:
        remote(
            pairs.at[mine], me, pair_recv.at[min(step, 1)],
            {"tile": lax.rem(me + k, n), "image": lax.rem(mine + step, m)},
        ).start()

    scale = factor * inverse_second
    second_row(0)
    second_row(rows + 1)

    def masked(row, values):
        if row == 0:
            return jnp.where(above, values, 0.0)
        if row == rows + 1:
            return jnp.where(below, values, 0.0)
        return values

    sums, done = [], 0
    for start, count in halves:
        while done < start + count + 2:
            at = pl.ds(done * cols, cols)
            back = gpre[at] * scale
            gpre[at] = back
            near_scaled[at] = masked(done, back).astype(BF16)
            done += 1
        for p, line in enumerate(conv_back(window(near_scaled, start, count), count, first_back)):
            at = pl.ds((start + p) * cols, cols)
            early = line * slope[at]
            sums.append((early, early * nfirst[at]))
    share(3, gathered_sums(sums))

    for row in range(rows + 2):
        at = pl.ds(row * cols, cols)
        near_second[at] = masked(row, gact[at]).astype(BF16)
    for start, count in halves:
        for p, line in enumerate(conv(near_second, (start,), count, second)):
            branch[0, start + p] = line.astype(BF16)

    settle(maps.shape[1] * maps.shape[2] // channels * (n - 1), map_recv.at[0])
    summed = add_up([maps[k] for k in range(n)])
    spread_of = jnp.where(same, 1.0, 0.0)
    for q, piece in enumerate(pieces(summed)):
        table_of[pl.ds(q * lanes, lanes), :] = lax.dot_general(
            piece.astype(F32), spread_of, (((0,), (0,)), ((), ())), preferred_element_type=F32
        ).astype(BF16)

    settle((m - 1) * acts.shape[2] // channels, act_recv.at[0])
    extra = (-6 * m) % 16

    def stacked(parts):
        if extra:
            parts = parts + [jnp.zeros((extra, parts[0].shape[1]), F32)]
        return jnp.concatenate(parts, axis=0).astype(BF16)

    thirds = [[piece.astype(F32) for piece in pieces(acts[k])] for k in range(m)]
    left_out[...] = stacked([thirds[k][q] for q in (0, 0, 1, 0, 1, 2) for k in range(m)])

    settle(2 * (n - 1), pair_recv.at[0])

    def whole(image):
        return add_up([pairs[image, k] for k in range(n)])

    spread = group_spread(whole(mine) * factor, width) / cells
    paired_mean, plain_mean = inverse_second * spread[0:1], inverse_second * spread[1:2]
    gradient, done = [], 0
    for start, count in halves:
        while done < start + count + 2:
            at = pl.ds(done * cols, cols)
            back = gpre[at] - plain_mean - nsecond[at] * paired_mean
            near_hidden[at] = masked(done, back).astype(BF16)
            done += 1
        gradient += conv_back(window(near_hidden, start, count), count, first_back)

    tilt = paired_mean * inverse_second
    level = plain_mean - tilt * centre
    row = lax.broadcasted_iota(jnp.int32, (channels, lanes), 0)
    lane = lax.broadcasted_iota(jnp.int32, (channels, lanes), 1)
    chosen = jnp.where(lax.rem(lane, GN_GROUPS) * width == row, 1.0, 0.0).astype(BF16)
    short = [piece.astype(F32) for piece in pieces(level) + pieces(tilt)]
    short = jnp.concatenate(short + [jnp.zeros((2, channels), F32)], axis=0).astype(BF16)
    short = jnp.dot(short, chosen, preferred_element_type=F32)
    quarter = lax.broadcasted_iota(jnp.int32, (1, lanes), 1) // GN_GROUPS
    nothing = jnp.zeros((1, lanes), F32)
    left = []
    for part in range(2):
        mixed = [
            jnp.where(quarter == part, short[3 + q : 4 + q], jnp.where(quarter == part + 2, short[q : q + 1], 0.0))
            for q in range(3)
        ]
        left += [
            jnp.concatenate([mixed[q]] * (3 - q) + [nothing] * q, axis=1) for q in range(3)
        ]
    left = jnp.concatenate(left + [jnp.zeros((2, 3 * lanes), F32)], axis=0).astype(BF16)
    moved = jnp.dot(left, table_of[...], preferred_element_type=F32)
    moved = jnp.concatenate(
        [jnp.sum(moved[3 * part : 3 * part + 3], axis=0, keepdims=True) for part in range(2)], axis=0
    )

    spread = (group_spread(total(3), width) - moved) / cells
    for p in range(rows):
        at = pl.ds(p * cols, cols)
        back = gradient[p] * slope[at]
        result = inverse_first * (back - spread[0:1] - nfirst[at] * spread[1:2])
        igrad[0, p] = result.astype(BF16)

    settle(2 * n * (m - 1), pair_recv.at[1])
    sums = [whole(k) for k in range(m)]
    for part in range(2):
        lines = [value[part : part + 1] for value in sums]
        thirds = [[piece.astype(F32) for piece in pieces(line)] for line in lines]
        columns = slice(part * channels, (part + 1) * channels)
        right_out[:, columns] = stacked([thirds[k][q] for q in (0, 1, 0, 2, 1, 0) for k in range(m)])
        bgrad[:, columns] = add_up(lines)

    lines = 2 * (4 * (n - 1) + len(others)) + (m - 1) * acts.shape[2] // channels
    lines += maps.shape[1] * maps.shape[2] // channels * (n - 1)
    settle(lines, None)
    for which, buffer in enumerate((images, images, cot)):

        @pl.when(above)
        def _():
            halo_copy(which, buffer, True).wait_send()

        @pl.when(below)
        def _():
            halo_copy(which, buffer, False).wait_send()


def finish(branch, igrad, left, right, bgrad, branch_out, igrad_out, wgrad_out, bgrad_out, wgrad, sem):
    copies = [
        pltpu.make_async_copy(source, target, sem.at[k])
        for k, (source, target) in enumerate(
            [(igrad, igrad_out), (branch, branch_out), (bgrad, bgrad_out)]
        )
    ]
    for copy in copies:
        copy.start()
    height = wgrad.shape[0] // PARTS
    for k in range(PARTS):
        at = pl.ds(k * height, height)
        wgrad[at] = lax.dot_general(
            left[:, k * height : (k + 1) * height], right[...],
            (((0,), (0,)), ((), ())), preferred_element_type=F32,
        )
        copy = pltpu.make_async_copy(wgrad.at[at], wgrad_out.at[at], sem.at[3 + k])
        copy.start()
        copies.append(copy)
    for copy in copies:
        copy.wait()


def body(
    n, m,
    images, cotangent, timesteps, class_ids, norm_gain, norm_bias, conv_first, conv_second,
    time_weight, time_bias, class_table, adaptive_weight, adaptive_bias,
):
    count, rows, cols, channels = images.shape
    assert count == 1 and rows >= REACH
    emb = time_weight.shape[1]
    vmem = pl.BlockSpec(memory_space=pltpu.VMEM)
    anywhere = pl.BlockSpec(memory_space=pl.ANY)
    padded = rows + 2 * REACH
    stack = 6 * m + (-6 * m) % 16
    own, more, most = rows * cols, (rows + 2) * cols, padded * cols
    dma = pltpu.SemaphoreType.DMA
    results = pl.pallas_call(
        functools.partial(kernel, n, m),
        out_shape=(
            jax.ShapeDtypeStruct(images.shape, BF16),
            jax.ShapeDtypeStruct(images.shape, BF16),
            jax.ShapeDtypeStruct((stack, emb), BF16),
            jax.ShapeDtypeStruct((stack, 2 * channels), BF16),
            jax.ShapeDtypeStruct((1, 2 * channels), F32),
        ),
        in_specs=[pl.BlockSpec(memory_space=pltpu.SMEM)] * 2
        + [pl.BlockSpec(memory_space=pltpu.HBM)] * 11,
        out_specs=(vmem,) * 5,
        scratch_shapes=[
            pltpu.VMEM((padded, cols, channels), BF16),
            pltpu.VMEM((padded, cols, channels), BF16),
            pltpu.VMEM(conv_first.shape, BF16),
            pltpu.VMEM(conv_second.shape, BF16),
            pltpu.VMEM(conv_first.shape, BF16),
            pltpu.VMEM(conv_second.shape, BF16),
            pltpu.VMEM(time_weight.shape, BF16),
            pltpu.VMEM(class_table.shape, BF16),
            pltpu.VMEM(adaptive_weight.shape, BF16),
            pltpu.VMEM((1, channels), F32),
            pltpu.VMEM((1, channels), F32),
            pltpu.VMEM((1, emb), F32),
            pltpu.VMEM((1, 2 * channels), F32),
            pltpu.VMEM((most, channels), BF16),
            pltpu.VMEM((more, channels), BF16),
            pltpu.VMEM((more, channels), BF16),
            pltpu.VMEM((more, channels), BF16),
            pltpu.VMEM((more, 3 * channels), BF16),
            pltpu.VMEM((2 * channels, own), BF16),
            pltpu.VMEM((12 * GN_GROUPS, channels), BF16),
            pltpu.VMEM((more, channels), F32),
            pltpu.VMEM((max(more, 2 * own), channels), F32),
            pltpu.VMEM((more, channels), F32),
            pltpu.VMEM((more, channels), F32),
            pltpu.VMEM((own, channels), F32),
            pltpu.VMEM((own, channels), F32),
            pltpu.VMEM((4, n, 2, channels), F32),
            pltpu.VMEM((m, 1, emb), F32),
            pltpu.VMEM((m, n, 2, channels), F32),
            pltpu.VMEM((n, GN_GROUPS, 4 * GN_GROUPS), F32),
            pltpu.VMEM((SPARE, 1, channels), F32),
            dma((11,)),
            dma((3, 2)),
            dma((3, 2)),
            dma((1,)),
            dma((4,)),
            dma((1,)),
            dma((2,)),
            dma((1,)),
        ],
        compiler_params=pltpu.CompilerParams(
            collective_id=0, has_side_effects=True, vmem_limit_bytes=GRANT
        ),
    )(
        timesteps, class_ids,
        *(
            pltpu.with_memory_space_constraint(operand, pltpu.HBM)
            for operand in (
                norm_gain[None], norm_bias[None], time_bias[None],
                adaptive_bias[None], images, cotangent, conv_first, conv_second, time_weight,
                class_table, adaptive_weight,
            )
        )
    )
    branch, igrad, wgrad, bgrad = pl.pallas_call(
        finish,
        out_shape=(
            jax.ShapeDtypeStruct(images.shape, BF16),
            jax.ShapeDtypeStruct(images.shape, BF16),
            jax.ShapeDtypeStruct((emb, 2 * channels), F32),
            jax.ShapeDtypeStruct((1, 2 * channels), F32),
        ),
        in_specs=[anywhere] * 2 + [vmem] * 2 + [anywhere],
        out_specs=(anywhere,) * 4,
        scratch_shapes=[pltpu.VMEM((emb, 2 * channels), F32), dma((3 + PARTS,))],
        compiler_params=pltpu.CompilerParams(vmem_limit_bytes=GRANT),
    )(*results)
    return branch, igrad, wgrad, bgrad[0]


def solution(mesh):
    return jax.shard_map(
        functools.partial(body, mesh.shape["tile"], mesh.shape["image"]),
        mesh=mesh,
        in_specs=(
            P(("groups", "image"), "tile", None, None),
            P(("groups", "image"), "tile", None, None),
            P(("groups", "image")),
            P(("groups", "image")),
            P(),
            P(),
            P(),
            P(),
            P(None, "tile"),
            P("tile"),
            P(None, "tile"),
            P("tile", None),
            P(),
        ),
        out_specs=(
            P(("groups", "image"), "tile", None, None),
            P(("groups", "image"), "tile", None, None),
            P(("groups", "tile"), None),
            P("groups"),
        ),
        check_vma=False,
    )
```

```python
import functools
import math

import jax
import jax.numpy as jnp
from jax import lax
from jax.experimental import pallas as pl
from jax.experimental.pallas import tpu as pltpu
from jax.sharding import PartitionSpec as P

GN_GROUPS = 32
EPSILON = 1e-05
MESH = pl.DeviceIdType.MESH
F32 = jnp.float32
BF16 = jnp.bfloat16
GRANT = 24 << 20
REACH = 2
PARTS = 2
SPARE = 128
HIGHEST = lax.Precision.HIGHEST


def group_spread(values, width):
    count = values.shape[-1]
    place = lax.broadcasted_iota(jnp.int32, values.shape, values.ndim - 1) % width
    terms = [values]
    for step in range(1, width):
        ahead = pltpu.roll(values, count - step, values.ndim - 1)
        wrapped = pltpu.roll(values, width - step, values.ndim - 1)
        terms.append(jnp.where(place + step < width, ahead, wrapped))
    while len(terms) > 1:
        pairs = [left + right for left, right in zip(terms[::2], terms[1::2])]
        terms = pairs + terms[2 * len(pairs) :]
    return terms[0]


def silu_slope(pre, sigma):
    return sigma * (1.0 + pre * (1.0 - sigma))


def column_sums(first, second):
    return jnp.concatenate(
        [jnp.sum(first, axis=0, keepdims=True), jnp.sum(second, axis=0, keepdims=True)], axis=0
    )


def kernel(
    n, m,
    steps_ref, ids_ref, gain_hbm, bias_hbm, tbias_hbm, abias_hbm,
    images_hbm, cot_hbm, first_hbm, second_hbm, tweight_hbm, table_hbm, aweight_hbm,
    branch, igrad, left_out, right_out, bgrad,
    images, cot, first, second, first_back, second_back, tweight, table, aweight,
    gain_ref, bias_ref, tbias_ref, abias_ref,
    near_first, near_second, near_hidden, near_scaled, wide_plain, tall, table_of,
    hidden, gact, nsecond, gpre, nfirst, slope,
    slots, acts, pairs, maps, spare,
    load_sem, halo_send, halo_recv, send_sem, slot_recv, act_recv, pair_recv, map_recv,
):
    me = lax.axis_index("tile")
    mine = lax.axis_index("image")
    rows, cols, channels = images_hbm.shape[1:]
    width = channels // GN_GROUPS
    cells = float(rows * cols * n * width)
    own = rows * cols
    above, below = me > 0, me < n - 1

    def load(source, target, k):
        return pltpu.make_async_copy(source, target, load_sem.at[k])

    loads = [
        load(images_hbm.at[0], images.at[pl.ds(REACH, rows)], 0),
        load(cot_hbm.at[0], cot.at[pl.ds(REACH, rows)], 1),
        load(tweight_hbm, tweight, 2),
        load(table_hbm, table, 3),
        load(aweight_hbm, aweight, 4),
        load(first_hbm, first, 5),
        load(second_hbm, second, 6),
        load(gain_hbm, gain_ref, 7),
        load(bias_hbm, bias_ref, 8),
        load(tbias_hbm, tbias_ref, 9),
        load(abias_hbm, abias_ref, 10),
    ]
    loads[0].start()
    barrier = pltpu.get_barrier_semaphore()
    for k in reversed(range(1, n)):
        pl.semaphore_signal(
            barrier, inc=1, device_id={"tile": lax.rem(me + k, n)}, device_id_type=MESH
        )
    for k in range(1, m):
        pl.semaphore_signal(
            barrier, inc=1, device_id={"image": lax.rem(mine + k, m)}, device_id_type=MESH
        )
    for k in (7, 8, 5, 2, 3, 4, 9, 10, 1, 6):
        loads[k].start()

    def remote(buffer, slot, receive, device):
        return pltpu.make_async_remote_copy(
            src_ref=buffer.at[slot],
            dst_ref=buffer.at[slot],
            send_sem=send_sem.at[0],
            recv_sem=receive,
            device_id=device,
            device_id_type=MESH,
        )

    def settle(lines, receive):
        while lines:
            part = min(lines, spare.shape[0])
            block = spare.at[pl.ds(0, part)]
            copy = pltpu.make_async_remote_copy(
                src_ref=block,
                dst_ref=block,
                send_sem=send_sem.at[0],
                recv_sem=send_sem.at[0] if receive is None else receive,
                device_id={"tile": lax.rem(me + 1, n)},
                device_id_type=MESH,
            )
            if receive is None:
                copy.wait_send()
            else:
                copy.wait_recv()
            lines -= part

    def tile_peer(k):
        return {"tile": lax.rem(me + k, n)}

    def share(stage, value):
        slots[stage, me] = value
        for k in range(1, n):
            remote(slots.at[stage], me, slot_recv.at[stage], tile_peer(k)).start()

    def total(stage):
        settle(2 * (n - 1), slot_recv.at[stage])
        summed = slots[stage, 0]
        for k in range(1, n):
            summed = summed + slots[stage, k]
        return summed

    HALOS = ((REACH, rows + REACH, rows + REACH - 1, REACH - 1, 1),
             (REACH + 1, rows + REACH + 1, rows + REACH - 2, REACH - 2, 1),
             (REACH, rows + REACH, rows, 0, REACH))

    def halo_copy(which, buffer, up):
        up_from, up_to, down_from, down_to, count = HALOS[which]
        source, target = (up_from, up_to) if up else (down_from, down_to)
        return pltpu.make_async_remote_copy(
            src_ref=buffer.at[pl.ds(source, count)],
            dst_ref=buffer.at[pl.ds(target, count)],
            send_sem=halo_send.at[which, int(up)],
            recv_sem=halo_recv.at[which, int(up)],
            device_id={"tile": me - 1 if up else me + 1},
            device_id_type=MESH,
        )

    def halo_start(which, buffer):
        _, low, _, high, count = HALOS[which]

        @pl.when(above)
        def _():
            halo_copy(which, buffer, True).start()

        @pl.when(below)
        def _():
            halo_copy(which, buffer, False).start()

        @pl.when(jnp.logical_not(above))
        def _():
            buffer[pl.ds(high, count)] = jnp.zeros((count, cols, channels), BF16)

        @pl.when(jnp.logical_not(below))
        def _():
            buffer[pl.ds(low, count)] = jnp.zeros((count, cols, channels), BF16)

    def halo_wait(which, buffer):
        @pl.when(below)
        def _():
            halo_copy(which, buffer, True).wait_recv()

        @pl.when(above)
        def _():
            halo_copy(which, buffer, False).wait_recv()

    column = lax.broadcasted_iota(jnp.int32, (cols, channels), 0)

    def widen(wide, row, values):
        before = jnp.where(column == 0, 0.0, pltpu.roll(values, 1, 0))
        after = jnp.where(column == cols - 1, 0.0, pltpu.roll(values, cols - 1, 0))
        at = pl.ds(row * cols, cols)
        wide[at, 0:channels] = before.astype(BF16)
        wide[at, channels : 2 * channels] = values.astype(BF16)
        wide[at, 2 * channels : 3 * channels] = after.astype(BF16)

    edge = jnp.zeros((1, channels), F32)

    def shifted(parts, count):
        lines = []
        for p in range(count):
            before, at, after = [part[p * cols : (p + 1) * cols] for part in parts]
            before = jnp.concatenate([edge, before[: cols - 1]], axis=0)
            after = jnp.concatenate([after[1:], edge], axis=0)
            lines.append(at + (before + after))
        return lines

    def conv(near, starts, count, weight):
        parts = [None] * 3
        for j in (0, 2, 1):
            for i in range(3):
                lines = [near[pl.ds((start + i) * cols, count * cols), :] for start in starts]
                product = jnp.dot(
                    lines[0] if len(lines) == 1 else jnp.concatenate(lines, axis=0),
                    weight[i, j],
                    preferred_element_type=F32,
                )
                parts[j] = product if i == 0 else parts[j] + product
        return shifted(parts, count * len(starts))

    def conv_back(lines_of, count, weight):
        parts = [None] * 3
        for j in (0, 2, 1):
            for i in range(3):
                product = jnp.dot(
                    lines_of(i), weight[2 - i, 2 - j], preferred_element_type=F32
                )
                parts[j] = product if i == 0 else parts[j] + product
        return shifted(parts, count)

    def window(near, start, count):
        return lambda i: near[pl.ds((start + i) * cols, count * cols), :]

    halves = [(0, rows // 2), (rows // 2, rows - rows // 2)]

    def pieces(values):
        parts = []
        for _ in range(3):
            part = values.astype(BF16)
            parts.append(part)
            values = values - part.astype(F32)
        return parts

    def moments(summed):
        spread = summed / cells
        centre = spread[0:1]
        variance = jnp.maximum(spread[1:2] - centre * centre, 0.0)
        return centre, lax.rsqrt(variance + EPSILON)

    def add_up(parts):
        return functools.reduce(jnp.add, parts)

    def gathered_sums(lines):
        folded = [
            add_up([jnp.sum(line[q].reshape(cols // 8, 8, channels), axis=0) for line in lines])
            for q in range(2)
        ]
        return column_sums(*folded)

    loads[0].wait()
    sums = []
    for p in range(rows):
        line = images[REACH + p].astype(F32)
        sums.append((line, line * line))
    sums = group_spread(gathered_sums(sums), width)
    pl.semaphore_wait(barrier, n - 1 + m - 1)
    share(0, sums)
    halo_start(0, images)
    halo_start(1, images)

    for k in (2, 3, 4, 7, 8, 9, 10):
        loads[k].wait()
    half = tweight.shape[0] // 2
    index = lax.broadcasted_iota(jnp.int32, (half, 1), 0).astype(F32)
    angles = steps_ref[0].astype(F32) * jnp.exp(-math.log(10000.0) * index / half)
    pre_time = (
        jnp.sum(jnp.cos(angles) * tweight[0:half].astype(F32), axis=0, keepdims=True)
        + jnp.sum(jnp.sin(angles) * tweight[half:].astype(F32), axis=0, keepdims=True)
        + tbias_ref[...]
    )
    entry = lax.broadcasted_iota(jnp.int32, table.shape, 0) == ids_ref[0]
    picked = jnp.sum(jnp.where(entry, table[...].astype(F32), 0.0), axis=0, keepdims=True)
    embedding = pre_time * jax.nn.sigmoid(pre_time) + picked
    activated = embedding * jax.nn.sigmoid(embedding)
    acts[mine] = activated
    for k in range(1, m):
        remote(acts, mine, act_recv.at[0], {"image": lax.rem(mine + k, m)}).start()
    partial = jnp.dot(
        jnp.broadcast_to(activated, (8, activated.shape[1])),
        aweight[...].astype(F32),
        precision=HIGHEST,
        preferred_element_type=F32,
    )[0:1]
    share(1, jnp.concatenate([partial[:, :channels], partial[:, channels:]], axis=0))

    loads[1].wait()
    halo_start(2, cot)

    for k, weight, turned in ((5, first, first_back), (6, second, second_back)):
        loads[k].wait()
        for i in range(3):
            for j in range(3):
                turned[i, j] = weight[i, j].T
    halo_wait(0, images)
    gain, bias = gain_ref[...], bias_ref[...]
    centre, inverse_first = moments(total(0))
    stretch = 0.5 * inverse_first * gain
    offset = 0.5 * bias - centre * stretch

    def first_row(row, inside):
        lean = images[row].astype(F32) * stretch + offset
        value = lean * (1.0 + jnp.tanh(lean))
        if inside is not None:
            value = jnp.where(inside, value, 0.0)
        near_first[pl.ds(row * cols, cols)] = value.astype(BF16)

    centre_rows, done = [], 0
    for start, count in halves:
        while done < start + count + 2:
            row = REACH - 1 + done
            first_row(row, above if done == 0 else below if done == rows + 1 else None)
            done += 1
        centre_rows += [
            line.astype(BF16).astype(F32)
            for line in conv(near_first, (1 + start,), count, first)
        ]
    share(2, gathered_sums([(line, line * line) for line in centre_rows]))
    for p, line in enumerate(centre_rows):
        hidden[pl.ds((1 + p) * cols, cols)] = line

    halo_wait(1, images)
    first_row(0, above)
    first_row(rows + 2 * REACH - 1, below)
    for row, line in zip((0, rows + 1), conv(near_first, (0, rows + 1), 1, first)):
        hidden[pl.ds(row * cols, cols)] = line.astype(BF16).astype(F32)

    whole_rows, first_cells, last_cells = [[], []], [[], []], [[], []]
    for p in range(rows):
        at = pl.ds(p * cols, cols)
        line = images[REACH + p].astype(F32)
        lean = line * stretch + offset
        bend = jnp.tanh(lean)
        steep = (0.5 * gain) * ((1.0 + bend) * (1.0 + lean * (1.0 - bend)))
        line = (line - centre) * inverse_first
        nfirst[at] = line
        slope[at] = steep
        for part, lines in enumerate((steep, steep * line)):
            lines = lines.astype(BF16).astype(F32)
            gact[at if part == 0 else pl.ds((rows + p) * cols, cols)] = lines
            whole_rows[part].append(jnp.sum(lines, axis=0, keepdims=True))
            first_cells[part].append(lines[0:1])
            last_cells[part].append(lines[cols - 1 : cols])
    edges = []
    for part in range(2):
        tall[pl.ds(part * channels, channels), :] = gact[pl.ds(part * own, own)].T.astype(BF16)
        kept = [
            [a - b for a, b in zip(whole_rows[part], first_cells[part])],
            whole_rows[part],
            [a - b for a, b in zip(whole_rows[part], last_cells[part])],
        ]
        grid = []
        for i in range(3):
            for j in range(3):
                value = add_up(kept[j])
                if i == 0:
                    value = value - jnp.where(above, 0.0, kept[j][0])
                elif i == 2:
                    value = value - jnp.where(below, 0.0, kept[j][rows - 1])
                grid.append(value)
        edges.append(grid)
    for row in range(rows + 2):
        lines = hidden[pl.ds(row * cols, cols)]
        if row == 0:
            lines = jnp.where(above, lines, 0.0)
        elif row == rows + 1:
            lines = jnp.where(below, lines, 0.0)
        widen(wide_plain, row, lines)
    same = (
        lax.broadcasted_iota(jnp.int32, (GN_GROUPS, channels), 1) // width
        == lax.broadcasted_iota(jnp.int32, (GN_GROUPS, channels), 0)
    )
    products, constants = [None, None], None
    for i in range(3):
        for j in range(3):
            taps = first[2 - i, 2 - j]
            wide_taps = taps.astype(F32)
            near = wide_plain[pl.ds(i * cols, own), j * channels : (j + 1) * channels]
            for part in range(2):
                product = wide_taps * jnp.dot(
                    tall[pl.ds(part * channels, channels), :], near, preferred_element_type=F32
                )
                products[part] = product if i + j == 0 else products[part] + product
            spread_rows = [
                jnp.where(same, piece.astype(F32), 0.0)
                for part in range(2)
                for piece in pieces(edges[part][3 * i + j])
            ]
            product = jnp.dot(
                jnp.concatenate(spread_rows, axis=0).astype(BF16), taps, preferred_element_type=F32
            )
            constants = product if i + j == 0 else constants + product
    blocks = [
        jnp.sum(product.reshape(GN_GROUPS, width, channels), axis=1) for product in products
    ] + [
        add_up(
            [constants[(3 * part + q) * GN_GROUPS : (3 * part + q + 1) * GN_GROUPS] for q in range(3)]
        )
        for part in range(2)
    ]
    columns_of = [pieces(block) for block in blocks]
    lanes = 4 * GN_GROUPS
    gathered = None
    for quarter in range(4):
        row = lax.broadcasted_iota(jnp.int32, (channels, lanes), 0)
        lane = lax.broadcasted_iota(jnp.int32, (channels, lanes), 1)
        chosen = jnp.where(row // width + quarter * GN_GROUPS == lane, 1.0, 0.0).astype(BF16)
        product = jnp.dot(
            jnp.concatenate(columns_of[quarter], axis=0), chosen, preferred_element_type=F32
        )
        gathered = product if gathered is None else gathered + product
    maps[me] = add_up([gathered[q * GN_GROUPS : (q + 1) * GN_GROUPS] for q in range(3)])
    for k in range(1, n):
        remote(maps, me, map_recv.at[0], tile_peer(k)).start()

    halo_wait(2, cot)
    count = (rows + 2) // 2
    for start in (0, rows + 2 - count):
        spans = lambda i: cot[pl.ds(start + i, count)].reshape(count * cols, channels)
        for p, line in enumerate(conv_back(spans, count, second_back)):
            gact[pl.ds((start + p) * cols, cols)] = line

    modulation = total(1)
    factor = 1.0 + (modulation[0:1] + abias_ref[:, :channels])
    shift = modulation[1:2] + abias_ref[:, channels:]
    centre, inverse_second = moments(group_spread(total(2), width))

    def second_row(row):
        at = pl.ds(row * cols, cols)
        normed = (hidden[at] - centre) * inverse_second
        lean = normed * (0.5 * factor) + 0.5 * shift
        bend = jnp.tanh(lean)
        rise = 1.0 + bend
        back = gact[at] * (0.5 * rise * (1.0 + lean * (1.0 - bend)))
        nsecond[at] = normed
        gact[at] = lean * rise
        gpre[at] = back
        return back * normed, back

    pairs[mine, me] = gathered_sums([second_row(1 + p) for p in range(rows)])
    others = [(k, step) for step in range(m) for k in range(n) if k or step]
    for k, step in others:
        remote(
            pairs.at[mine], me, pair_recv.at[min(step, 1)],
            {"tile": lax.rem(me + k, n), "image": lax.rem(mine + step, m)},
        ).start()

    scale = factor * inverse_second
    second_row(0)
    second_row(rows + 1)

    def masked(row, values):
        if row == 0:
            return jnp.where(above, values, 0.0)
        if row == rows + 1:
            return jnp.where(below, values, 0.0)
        return values

    sums, done = [], 0
    for start, count in halves:
        while done < start + count + 2:
            at = pl.ds(done * cols, cols)
            back = gpre[at] * scale
            gpre[at] = back
            near_scaled[at] = masked(done, back).astype(BF16)
            done += 1
        for p, line in enumerate(conv_back(window(near_scaled, start, count), count, first_back)):
            at = pl.ds((start + p) * cols, cols)
            early = line * slope[at]
            sums.append((early, early * nfirst[at]))
    share(3, group_spread(gathered_sums(sums), width))

    for row in range(rows + 2):
        at = pl.ds(row * cols, cols)
        near_second[at] = masked(row, gact[at]).astype(BF16)
    for start, count in halves:
        for p, line in enumerate(conv(near_second, (start,), count, second)):
            branch[0, start + p] = line.astype(BF16)

    settle(maps.shape[1] * maps.shape[2] // channels * (n - 1), map_recv.at[0])
    summed = add_up([maps[k] for k in range(n)])
    spread_of = jnp.where(same, 1.0, 0.0)
    for q, piece in enumerate(pieces(summed)):
        table_of[pl.ds(q * lanes, lanes), :] = lax.dot_general(
            piece.astype(F32), spread_of, (((0,), (0,)), ((), ())), preferred_element_type=F32
        ).astype(BF16)

    settle((m - 1) * acts.shape[2] // channels, act_recv.at[0])
    extra = (-6 * m) % 16

    def stacked(parts):
        if extra:
            parts = parts + [jnp.zeros((extra, parts[0].shape[1]), F32)]
        return jnp.concatenate(parts, axis=0).astype(BF16)

    thirds = [[piece.astype(F32) for piece in pieces(acts[k])] for k in range(m)]
    left_out[...] = stacked([thirds[k][q] for q in (0, 0, 1, 0, 1, 2) for k in range(m)])

    settle(2 * (n - 1), pair_recv.at[0])

    def whole(image):
        return add_up([pairs[image, k] for k in range(n)])

    spread = group_spread(whole(mine) * factor, width) / cells
    paired_mean, plain_mean = inverse_second * spread[0:1], inverse_second * spread[1:2]
    gradient, done = [], 0
    for start, count in halves:
        while done < start + count + 2:
            at = pl.ds(done * cols, cols)
            back = gpre[at] - plain_mean - nsecond[at] * paired_mean
            near_hidden[at] = masked(done, back).astype(BF16)
            done += 1
        gradient += conv_back(window(near_hidden, start, count), count, first_back)

    tilt = paired_mean * inverse_second
    level = plain_mean - tilt * centre
    row = lax.broadcasted_iota(jnp.int32, (channels, lanes), 0)
    lane = lax.broadcasted_iota(jnp.int32, (channels, lanes), 1)
    chosen = jnp.where(lax.rem(lane, GN_GROUPS) * width == row, 1.0, 0.0).astype(BF16)
    short = [piece.astype(F32) for piece in pieces(level) + pieces(tilt)]
    short = jnp.concatenate(short + [jnp.zeros((2, channels), F32)], axis=0).astype(BF16)
    short = jnp.dot(short, chosen, preferred_element_type=F32)
    quarter = lax.broadcasted_iota(jnp.int32, (1, lanes), 1) // GN_GROUPS
    nothing = jnp.zeros((1, lanes), F32)
    left = []
    for part in range(2):
        mixed = [
            jnp.where(quarter == part, short[3 + q : 4 + q], jnp.where(quarter == part + 2, short[q : q + 1], 0.0))
            for q in range(3)
        ]
        left += [
            jnp.concatenate([mixed[q]] * (3 - q) + [nothing] * q, axis=1) for q in range(3)
        ]
    left = jnp.concatenate(left + [jnp.zeros((2, 3 * lanes), F32)], axis=0).astype(BF16)
    moved = jnp.dot(left, table_of[...], preferred_element_type=F32)
    moved = jnp.concatenate(
        [jnp.sum(moved[3 * part : 3 * part + 3], axis=0, keepdims=True) for part in range(2)], axis=0
    )

    spread = (total(3) - moved) / cells
    for p in range(rows):
        at = pl.ds(p * cols, cols)
        back = gradient[p] * slope[at]
        result = inverse_first * (back - spread[0:1] - nfirst[at] * spread[1:2])
        igrad[0, p] = result.astype(BF16)

    settle(2 * n * (m - 1), pair_recv.at[1])
    sums = [whole(k) for k in range(m)]
    for part in range(2):
        lines = [value[part : part + 1] for value in sums]
        thirds = [[piece.astype(F32) for piece in pieces(line)] for line in lines]
        columns = slice(part * channels, (part + 1) * channels)
        right_out[:, columns] = stacked([thirds[k][q] for q in (0, 1, 0, 2, 1, 0) for k in range(m)])
        bgrad[:, columns] = add_up(lines)

    lines = 2 * (4 * (n - 1) + len(others)) + (m - 1) * acts.shape[2] // channels
    lines += maps.shape[1] * maps.shape[2] // channels * (n - 1)
    settle(lines, None)
    for which, buffer in enumerate((images, images, cot)):

        @pl.when(above)
        def _():
            halo_copy(which, buffer, True).wait_send()

        @pl.when(below)
        def _():
            halo_copy(which, buffer, False).wait_send()


def finish(branch, igrad, left, right, bgrad, branch_out, igrad_out, wgrad_out, bgrad_out, wgrad, sem):
    copies = [
        pltpu.make_async_copy(source, target, sem.at[k])
        for k, (source, target) in enumerate(
            [(igrad, igrad_out), (branch, branch_out), (bgrad, bgrad_out)]
        )
    ]
    for copy in copies:
        copy.start()
    height = wgrad.shape[0] // PARTS
    for k in range(PARTS):
        at = pl.ds(k * height, height)
        wgrad[at] = lax.dot_general(
            left[:, k * height : (k + 1) * height], right[...],
            (((0,), (0,)), ((), ())), preferred_element_type=F32,
        )
        copy = pltpu.make_async_copy(wgrad.at[at], wgrad_out.at[at], sem.at[3 + k])
        copy.start()
        copies.append(copy)
    for copy in copies:
        copy.wait()


def body(
    n, m,
    images, cotangent, timesteps, class_ids, norm_gain, norm_bias, conv_first, conv_second,
    time_weight, time_bias, class_table, adaptive_weight, adaptive_bias,
):
    count, rows, cols, channels = images.shape
    assert count == 1 and rows >= REACH
    emb = time_weight.shape[1]
    vmem = pl.BlockSpec(memory_space=pltpu.VMEM)
    anywhere = pl.BlockSpec(memory_space=pl.ANY)
    padded = rows + 2 * REACH
    stack = 6 * m + (-6 * m) % 16
    own, more, most = rows * cols, (rows + 2) * cols, padded * cols
    dma = pltpu.SemaphoreType.DMA
    results = pl.pallas_call(
        functools.partial(kernel, n, m),
        out_shape=(
            jax.ShapeDtypeStruct(images.shape, BF16),
            jax.ShapeDtypeStruct(images.shape, BF16),
            jax.ShapeDtypeStruct((stack, emb), BF16),
            jax.ShapeDtypeStruct((stack, 2 * channels), BF16),
            jax.ShapeDtypeStruct((1, 2 * channels), F32),
        ),
        in_specs=[pl.BlockSpec(memory_space=pltpu.SMEM)] * 2
        + [pl.BlockSpec(memory_space=pltpu.HBM)] * 11,
        out_specs=(vmem,) * 5,
        scratch_shapes=[
            pltpu.VMEM((padded, cols, channels), BF16),
            pltpu.VMEM((padded, cols, channels), BF16),
            pltpu.VMEM(conv_first.shape, BF16),
            pltpu.VMEM(conv_second.shape, BF16),
            pltpu.VMEM(conv_first.shape, BF16),
            pltpu.VMEM(conv_second.shape, BF16),
            pltpu.VMEM(time_weight.shape, BF16),
            pltpu.VMEM(class_table.shape, BF16),
            pltpu.VMEM(adaptive_weight.shape, BF16),
            pltpu.VMEM((1, channels), F32),
            pltpu.VMEM((1, channels), F32),
            pltpu.VMEM((1, emb), F32),
            pltpu.VMEM((1, 2 * channels), F32),
            pltpu.VMEM((most, channels), BF16),
            pltpu.VMEM((more, channels), BF16),
            pltpu.VMEM((more, channels), BF16),
            pltpu.VMEM((more, channels), BF16),
            pltpu.VMEM((more, 3 * channels), BF16),
            pltpu.VMEM((2 * channels, own), BF16),
            pltpu.VMEM((12 * GN_GROUPS, channels), BF16),
            pltpu.VMEM((more, channels), F32),
            pltpu.VMEM((max(more, 2 * own), channels), F32),
            pltpu.VMEM((more, channels), F32),
            pltpu.VMEM((more, channels), F32),
            pltpu.VMEM((own, channels), F32),
            pltpu.VMEM((own, channels), F32),
            pltpu.VMEM((4, n, 2, channels), F32),
            pltpu.VMEM((m, 1, emb), F32),
            pltpu.VMEM((m, n, 2, channels), F32),
            pltpu.VMEM((n, GN_GROUPS, 4 * GN_GROUPS), F32),
            pltpu.VMEM((SPARE, 1, channels), F32),
            dma((11,)),
            dma((3, 2)),
            dma((3, 2)),
            dma((1,)),
            dma((4,)),
            dma((1,)),
            dma((2,)),
            dma((1,)),
        ],
        compiler_params=pltpu.CompilerParams(
            collective_id=0, has_side_effects=True, vmem_limit_bytes=GRANT
        ),
    )(
        timesteps, class_ids,
        *(
            pltpu.with_memory_space_constraint(operand, pltpu.HBM)
            for operand in (
                norm_gain[None], norm_bias[None], time_bias[None],
                adaptive_bias[None], images, cotangent, conv_first, conv_second, time_weight,
                class_table, adaptive_weight,
            )
        )
    )
    branch, igrad, wgrad, bgrad = pl.pallas_call(
        finish,
        out_shape=(
            jax.ShapeDtypeStruct(images.shape, BF16),
            jax.ShapeDtypeStruct(images.shape, BF16),
            jax.ShapeDtypeStruct((emb, 2 * channels), F32),
            jax.ShapeDtypeStruct((1, 2 * channels), F32),
        ),
        in_specs=[anywhere] * 2 + [vmem] * 2 + [anywhere],
        out_specs=(anywhere,) * 4,
        scratch_shapes=[pltpu.VMEM((emb, 2 * channels), F32), dma((3 + PARTS,))],
        compiler_params=pltpu.CompilerParams(vmem_limit_bytes=GRANT),
    )(*results)
    return branch, igrad, wgrad, bgrad[0]


def solution(mesh):
    return jax.shard_map(
        functools.partial(body, mesh.shape["tile"], mesh.shape["image"]),
        mesh=mesh,
        in_specs=(
            P(("groups", "image"), "tile", None, None),
            P(("groups", "image"), "tile", None, None),
            P(("groups", "image")),
            P(("groups", "image")),
            P(),
            P(),
            P(),
            P(),
            P(None, "tile"),
            P("tile"),
            P(None, "tile"),
            P("tile", None),
            P(),
        ),
        out_specs=(
            P(("groups", "image"), "tile", None, None),
            P(("groups", "image"), "tile", None, None),
            P(("groups", "tile"), None),
            P("groups"),
        ),
        check_vma=False,
    )
```

```python
import functools
import math

import jax
import jax.numpy as jnp
from jax import lax
from jax.experimental import pallas as pl
from jax.experimental.pallas import tpu as pltpu
from jax.sharding import PartitionSpec as P

GN_GROUPS = 32
EPSILON = 1e-05
MESH = pl.DeviceIdType.MESH
F32 = jnp.float32
BF16 = jnp.bfloat16
GRANT = 24 << 20
REACH = 2
PARTS = 2
SPARE = 128
HIGHEST = lax.Precision.HIGHEST


def group_spread(values, width):
    count = values.shape[-1]
    place = lax.broadcasted_iota(jnp.int32, values.shape, values.ndim - 1) % width
    terms = [values]
    for step in range(1, width):
        ahead = pltpu.roll(values, count - step, values.ndim - 1)
        wrapped = pltpu.roll(values, width - step, values.ndim - 1)
        terms.append(jnp.where(place + step < width, ahead, wrapped))
    while len(terms) > 1:
        pairs = [left + right for left, right in zip(terms[::2], terms[1::2])]
        terms = pairs + terms[2 * len(pairs) :]
    return terms[0]


def silu_slope(pre, sigma):
    return sigma * (1.0 + pre * (1.0 - sigma))


def column_sums(first, second):
    return jnp.concatenate(
        [jnp.sum(first, axis=0, keepdims=True), jnp.sum(second, axis=0, keepdims=True)], axis=0
    )


def kernel(
    n, m,
    steps_ref, ids_ref, gain_hbm, bias_hbm, tbias_hbm, abias_hbm,
    images_hbm, cot_hbm, first_hbm, second_hbm, tweight_hbm, table_hbm, aweight_hbm,
    branch, igrad, left_out, right_out, bgrad,
    images, cot, first, second, first_back, second_back, tweight, table, aweight,
    gain_ref, bias_ref, tbias_ref, abias_ref,
    near_first, near_second, near_hidden, near_scaled, wide_plain, tall, table_of,
    hidden, gact, nsecond, gpre, nfirst, slope,
    slots, acts, pairs, maps, spare,
    load_sem, halo_send, halo_recv, send_sem, slot_recv, act_recv, pair_recv, map_recv,
):
    me = lax.axis_index("tile")
    mine = lax.axis_index("image")
    rows, cols, channels = images_hbm.shape[1:]
    width = channels // GN_GROUPS
    cells = float(rows * cols * n * width)
    own = rows * cols
    above, below = me > 0, me < n - 1

    def load(source, target, k):
        return pltpu.make_async_copy(source, target, load_sem.at[k])

    loads = [
        load(images_hbm.at[0], images.at[pl.ds(REACH, rows)], 0),
        load(cot_hbm.at[0], cot.at[pl.ds(REACH, rows)], 1),
        load(tweight_hbm, tweight, 2),
        load(table_hbm, table, 3),
        load(aweight_hbm, aweight, 4),
        load(first_hbm, first, 5),
        load(second_hbm, second, 6),
        load(gain_hbm, gain_ref, 7),
        load(bias_hbm, bias_ref, 8),
        load(tbias_hbm, tbias_ref, 9),
        load(abias_hbm, abias_ref, 10),
    ]
    loads[0].start()
    barrier = pltpu.get_barrier_semaphore()
    for k in reversed(range(1, n)):
        pl.semaphore_signal(
            barrier, inc=1, device_id={"tile": lax.rem(me + k, n)}, device_id_type=MESH
        )
    for k in range(1, m):
        pl.semaphore_signal(
            barrier, inc=1, device_id={"image": lax.rem(mine + k, m)}, device_id_type=MESH
        )
    for k in (7, 8, 5, 2, 3, 4, 9, 10, 1, 6):
        loads[k].start()

    def remote(buffer, slot, receive, device):
        return pltpu.make_async_remote_copy(
            src_ref=buffer.at[slot],
            dst_ref=buffer.at[slot],
            send_sem=send_sem.at[0],
            recv_sem=receive,
            device_id=device,
            device_id_type=MESH,
        )

    def settle(lines, receive):
        while lines:
            part = min(lines, spare.shape[0])
            block = spare.at[pl.ds(0, part)]
            copy = pltpu.make_async_remote_copy(
                src_ref=block,
                dst_ref=block,
                send_sem=send_sem.at[0],
                recv_sem=send_sem.at[0] if receive is None else receive,
                device_id={"tile": lax.rem(me + 1, n)},
                device_id_type=MESH,
            )
            if receive is None:
                copy.wait_send()
            else:
                copy.wait_recv()
            lines -= part

    def tile_peer(k):
        return {"tile": lax.rem(me + k, n)}

    def share(stage, value):
        slots[stage, me] = value
        for k in range(1, n):
            remote(slots.at[stage], me, slot_recv.at[stage], tile_peer(k)).start()

    def total(stage):
        settle(2 * (n - 1), slot_recv.at[stage])
        summed = slots[stage, 0]
        for k in range(1, n):
            summed = summed + slots[stage, k]
        return summed

    HALOS = ((REACH, rows + REACH, rows + REACH - 1, REACH - 1, 1),
             (REACH + 1, rows + REACH + 1, rows + REACH - 2, REACH - 2, 1),
             (REACH, rows + REACH, rows, 0, REACH))

    def halo_copy(which, buffer, up):
        up_from, up_to, down_from, down_to, count = HALOS[which]
        source, target = (up_from, up_to) if up else (down_from, down_to)
        return pltpu.make_async_remote_copy(
            src_ref=buffer.at[pl.ds(source, count)],
            dst_ref=buffer.at[pl.ds(target, count)],
            send_sem=halo_send.at[which, int(up)],
            recv_sem=halo_recv.at[which, int(up)],
            device_id={"tile": me - 1 if up else me + 1},
            device_id_type=MESH,
        )

    def halo_start(which, buffer):
        _, low, _, high, count = HALOS[which]

        @pl.when(above)
        def _():
            halo_copy(which, buffer, True).start()

        @pl.when(below)
        def _():
            halo_copy(which, buffer, False).start()

        @pl.when(jnp.logical_not(above))
        def _():
            buffer[pl.ds(high, count)] = jnp.zeros((count, cols, channels), BF16)

        @pl.when(jnp.logical_not(below))
        def _():
            buffer[pl.ds(low, count)] = jnp.zeros((count, cols, channels), BF16)

    def halo_wait(which, buffer):
        @pl.when(below)
        def _():
            halo_copy(which, buffer, True).wait_recv()

        @pl.when(above)
        def _():
            halo_copy(which, buffer, False).wait_recv()

    column = lax.broadcasted_iota(jnp.int32, (cols, channels), 0)

    def widen(wide, row, values):
        before = jnp.where(column == 0, 0.0, pltpu.roll(values, 1, 0))
        after = jnp.where(column == cols - 1, 0.0, pltpu.roll(values, cols - 1, 0))
        at = pl.ds(row * cols, cols)
        wide[at, 0:channels] = before.astype(BF16)
        wide[at, channels : 2 * channels] = values.astype(BF16)
        wide[at, 2 * channels : 3 * channels] = after.astype(BF16)

    edge = jnp.zeros((1, channels), F32)

    def shifted(parts, count):
        lines = []
        for p in range(count):
            before, at, after = [part[p * cols : (p + 1) * cols] for part in parts]
            before = jnp.concatenate([edge, before[: cols - 1]], axis=0)
            after = jnp.concatenate([after[1:], edge], axis=0)
            lines.append(at + (before + after))
        return lines

    def conv(near, starts, count, weight):
        parts = [None] * 3
        for j in (0, 2, 1):
            for i in range(3):
                lines = [near[pl.ds((start + i) * cols, count * cols), :] for start in starts]
                product = jnp.dot(
                    lines[0] if len(lines) == 1 else jnp.concatenate(lines, axis=0),
                    weight[i, j],
                    preferred_element_type=F32,
                )
                parts[j] = product if i == 0 else parts[j] + product
        return shifted(parts, count * len(starts))

    def conv_back(lines_of, count, weight):
        parts = [None] * 3
        for j in (0, 2, 1):
            for i in range(3):
                product = jnp.dot(
                    lines_of(i), weight[2 - i, 2 - j], preferred_element_type=F32
                )
                parts[j] = product if i == 0 else parts[j] + product
        return shifted(parts, count)

    def window(near, start, count):
        return lambda i: near[pl.ds((start + i) * cols, count * cols), :]

    halves = [(0, rows // 2), (rows // 2, rows - rows // 2)]

    def pieces(values):
        parts = []
        for _ in range(3):
            part = values.astype(BF16)
            parts.append(part)
            values = values - part.astype(F32)
        return parts

    def moments(summed):
        spread = summed / cells
        centre = spread[0:1]
        variance = jnp.maximum(spread[1:2] - centre * centre, 0.0)
        return centre, lax.rsqrt(variance + EPSILON)

    def add_up(parts):
        return functools.reduce(jnp.add, parts)

    def gathered_sums(lines):
        folded = [
            add_up([jnp.sum(line[q].reshape(cols // 8, 8, channels), axis=0) for line in lines])
            for q in range(2)
        ]
        return column_sums(*folded)

    loads[0].wait()
    sums = []
    for p in range(rows):
        line = images[REACH + p].astype(F32)
        sums.append((line, line * line))
    sums = group_spread(gathered_sums(sums), width)
    pl.semaphore_wait(barrier, n - 1 + m - 1)
    share(0, sums)
    halo_start(0, images)
    halo_start(1, images)

    for k in (2, 3, 4, 7, 8, 9, 10):
        loads[k].wait()
    half = tweight.shape[0] // 2
    index = lax.broadcasted_iota(jnp.int32, (half, 1), 0).astype(F32)
    angles = steps_ref[0].astype(F32) * jnp.exp(-math.log(10000.0) * index / half)
    pre_time = (
        jnp.sum(jnp.cos(angles) * tweight[0:half].astype(F32), axis=0, keepdims=True)
        + jnp.sum(jnp.sin(angles) * tweight[half:].astype(F32), axis=0, keepdims=True)
        + tbias_ref[...]
    )
    entry = lax.broadcasted_iota(jnp.int32, table.shape, 0) == ids_ref[0]
    picked = jnp.sum(jnp.where(entry, table[...].astype(F32), 0.0), axis=0, keepdims=True)
    embedding = pre_time * jax.nn.sigmoid(pre_time) + picked
    activated = embedding * jax.nn.sigmoid(embedding)
    acts[mine] = activated
    for k in range(1, m):
        remote(acts, mine, act_recv.at[0], {"image": lax.rem(mine + k, m)}).start()
    partial = jnp.dot(
        jnp.broadcast_to(activated, (8, activated.shape[1])),
        aweight[...].astype(F32),
        precision=HIGHEST,
        preferred_element_type=F32,
    )[0:1]
    share(1, jnp.concatenate([partial[:, :channels], partial[:, channels:]], axis=0))

    loads[1].wait()
    halo_start(2, cot)

    for k, weight, turned in ((5, first, first_back), (6, second, second_back)):
        loads[k].wait()
        for i in range(3):
            for j in range(3):
                turned[i, j] = weight[i, j].T
    halo_wait(0, images)
    gain, bias = gain_ref[...], bias_ref[...]
    centre, inverse_first = moments(total(0))
    stretch = 0.5 * inverse_first * gain
    offset = 0.5 * bias - centre * stretch

    def first_row(row, inside):
        lean = images[row].astype(F32) * stretch + offset
        value = lean * (1.0 + jnp.tanh(lean))
        if inside is not None:
            value = jnp.where(inside, value, 0.0)
        near_first[pl.ds(row * cols, cols)] = value.astype(BF16)

    centre_rows, done = [], 0
    for start, count in halves:
        while done < start + count + 2:
            row = REACH - 1 + done
            first_row(row, above if done == 0 else below if done == rows + 1 else None)
            done += 1
        centre_rows += [
            line.astype(BF16).astype(F32)
            for line in conv(near_first, (1 + start,), count, first)
        ]
    share(2, gathered_sums([(line, line * line) for line in centre_rows]))
    for p, line in enumerate(centre_rows):
        hidden[pl.ds((1 + p) * cols, cols)] = line

    halo_wait(1, images)
    first_row(0, above)
    first_row(rows + 2 * REACH - 1, below)
    for row, line in zip((0, rows + 1), conv(near_first, (0, rows + 1), 1, first)):
        hidden[pl.ds(row * cols, cols)] = line.astype(BF16).astype(F32)

    whole_rows, first_cells, last_cells = [[], []], [[], []], [[], []]
    for p in range(rows):
        at = pl.ds(p * cols, cols)
        line = images[REACH + p].astype(F32)
        lean = line * stretch + offset
        bend = jnp.tanh(lean)
        steep = (0.5 * gain) * ((1.0 + bend) * (1.0 + lean * (1.0 - bend)))
        line = (line - centre) * inverse_first
        nfirst[at] = line
        slope[at] = steep
        for part, lines in enumerate((steep, steep * line)):
            lines = lines.astype(BF16).astype(F32)
            gact[at if part == 0 else pl.ds((rows + p) * cols, cols)] = lines
            whole_rows[part].append(jnp.sum(lines, axis=0, keepdims=True))
            first_cells[part].append(lines[0:1])
            last_cells[part].append(lines[cols - 1 : cols])
    edges = []
    for part in range(2):
        tall[pl.ds(part * channels, channels), :] = gact[pl.ds(part * own, own)].T.astype(BF16)
        kept = [
            [a - b for a, b in zip(whole_rows[part], first_cells[part])],
            whole_rows[part],
            [a - b for a, b in zip(whole_rows[part], last_cells[part])],
        ]
        grid = []
        for i in range(3):
            for j in range(3):
                value = add_up(kept[j])
                if i == 0:
                    value = value - jnp.where(above, 0.0, kept[j][0])
                elif i == 2:
                    value = value - jnp.where(below, 0.0, kept[j][rows - 1])
                grid.append(value)
        edges.append(grid)
    for row in range(rows + 2):
        lines = hidden[pl.ds(row * cols, cols)]
        if row == 0:
            lines = jnp.where(above, lines, 0.0)
        elif row == rows + 1:
            lines = jnp.where(below, lines, 0.0)
        widen(wide_plain, row, lines)
    same = (
        lax.broadcasted_iota(jnp.int32, (GN_GROUPS, channels), 1) // width
        == lax.broadcasted_iota(jnp.int32, (GN_GROUPS, channels), 0)
    )
    products, constants = [None, None], None
    for i in range(3):
        for j in range(3):
            taps = first[2 - i, 2 - j]
            wide_taps = taps.astype(F32)
            near = wide_plain[pl.ds(i * cols, own), j * channels : (j + 1) * channels]
            for part in range(2):
                product = wide_taps * jnp.dot(
                    tall[pl.ds(part * channels, channels), :], near, preferred_element_type=F32
                )
                products[part] = product if i + j == 0 else products[part] + product
            spread_rows = [
                jnp.where(same, piece.astype(F32), 0.0)
                for part in range(2)
                for piece in pieces(edges[part][3 * i + j])
            ]
            product = jnp.dot(
                jnp.concatenate(spread_rows, axis=0).astype(BF16), taps, preferred_element_type=F32
            )
            constants = product if i + j == 0 else constants + product
    blocks = [
        jnp.sum(product.reshape(GN_GROUPS, width, channels), axis=1) for product in products
    ] + [
        add_up(
            [constants[(3 * part + q) * GN_GROUPS : (3 * part + q + 1) * GN_GROUPS] for q in range(3)]
        )
        for part in range(2)
    ]
    columns_of = [pieces(block) for block in blocks]
    lanes = 4 * GN_GROUPS
    gathered = None
    for quarter in range(4):
        row = lax.broadcasted_iota(jnp.int32, (channels, lanes), 0)
        lane = lax.broadcasted_iota(jnp.int32, (channels, lanes), 1)
        chosen = jnp.where(row // width + quarter * GN_GROUPS == lane, 1.0, 0.0).astype(BF16)
        product = jnp.dot(
            jnp.concatenate(columns_of[quarter], axis=0), chosen, preferred_element_type=F32
        )
        gathered = product if gathered is None else gathered + product
    maps[me] = add_up([gathered[q * GN_GROUPS : (q + 1) * GN_GROUPS] for q in range(3)])
    for k in range(1, n):
        remote(maps, me, map_recv.at[0], tile_peer(k)).start()

    halo_wait(2, cot)
    count = (rows + 2) // 2
    for start in (0, rows + 2 - count):
        spans = lambda i: cot[pl.ds(start + i, count)].reshape(count * cols, channels)
        for p, line in enumerate(conv_back(spans, count, second_back)):
            gact[pl.ds((start + p) * cols, cols)] = line

    modulation = total(1)
    factor = 1.0 + (modulation[0:1] + abias_ref[:, :channels])
    shift = modulation[1:2] + abias_ref[:, channels:]
    centre, inverse_second = moments(group_spread(total(2), width))

    def second_row(row):
        at = pl.ds(row * cols, cols)
        normed = (hidden[at] - centre) * inverse_second
        lean = normed * (0.5 * factor) + 0.5 * shift
        bend = jnp.tanh(lean)
        rise = 1.0 + bend
        back = gact[at] * (0.5 * rise * (1.0 + lean * (1.0 - bend)))
        nsecond[at] = normed
        gact[at] = lean * rise
        gpre[at] = back
        return back * normed, back

    pairs[mine, me] = gathered_sums([second_row(1 + p) for p in range(rows)])
    others = [(k, step) for step in range(m) for k in range(n) if k or step]
    for k, step in others:
        remote(
            pairs.at[mine], me, pair_recv.at[min(step, 1)],
            {"tile": lax.rem(me + k, n), "image": lax.rem(mine + step, m)},
        ).start()

    scale = factor * inverse_second
    second_row(0)
    second_row(rows + 1)

    def masked(row, values):
        if row == 0:
            return jnp.where(above, values, 0.0)
        if row == rows + 1:
            return jnp.where(below, values, 0.0)
        return values

    sums, done = [], 0
    for start, count in halves:
        while done < start + count + 2:
            at = pl.ds(done * cols, cols)
            back = gpre[at] * scale
            gpre[at] = back
            near_scaled[at] = masked(done, back).astype(BF16)
            done += 1
        for p, line in enumerate(conv_back(window(near_scaled, start, count), count, first_back)):
            at = pl.ds((start + p) * cols, cols)
            early = line * slope[at]
            sums.append((early, early * nfirst[at]))
    share(3, group_spread(gathered_sums(sums), width))

    for row in range(rows + 2):
        at = pl.ds(row * cols, cols)
        near_second[at] = masked(row, gact[at]).astype(BF16)
    for start, count in halves:
        for p, line in enumerate(conv(near_second, (start,), count, second)):
            branch[0, start + p] = line.astype(BF16)

    settle(maps.shape[1] * maps.shape[2] // channels * (n - 1), map_recv.at[0])
    summed = add_up([maps[k] for k in range(n)])
    spread_of = jnp.where(same, 1.0, 0.0)
    for q, piece in enumerate(pieces(summed)):
        table_of[pl.ds(q * lanes, lanes), :] = lax.dot_general(
            piece.astype(F32), spread_of, (((0,), (0,)), ((), ())), preferred_element_type=F32
        ).astype(BF16)

    settle((m - 1) * acts.shape[2] // channels, act_recv.at[0])
    extra = (-6 * m) % 16

    def stacked(parts):
        if extra:
            parts = parts + [jnp.zeros((extra, parts[0].shape[1]), F32)]
        return jnp.concatenate(parts, axis=0)

    thirds = [[piece.astype(F32) for piece in pieces(acts[k])] for k in range(m)]
    left_out[...] = stacked(
        [thirds[k][q] for q in (0, 0, 1, 0, 1, 2) for k in range(m)]
    ).T.astype(BF16)

    settle(2 * (n - 1), pair_recv.at[0])

    def whole(image):
        return add_up([pairs[image, k] for k in range(n)])

    spread = group_spread(whole(mine) * factor, width) / cells
    paired_mean, plain_mean = inverse_second * spread[0:1], inverse_second * spread[1:2]
    gradient, done = [], 0
    for start, count in halves:
        while done < start + count + 2:
            at = pl.ds(done * cols, cols)
            back = gpre[at] - plain_mean - nsecond[at] * paired_mean
            near_hidden[at] = masked(done, back).astype(BF16)
            done += 1
        gradient += conv_back(window(near_hidden, start, count), count, first_back)

    tilt = paired_mean * inverse_second
    level = plain_mean - tilt * centre
    row = lax.broadcasted_iota(jnp.int32, (channels, lanes), 0)
    lane = lax.broadcasted_iota(jnp.int32, (channels, lanes), 1)
    chosen = jnp.where(lax.rem(lane, GN_GROUPS) * width == row, 1.0, 0.0).astype(BF16)
    short = [piece.astype(F32) for piece in pieces(level) + pieces(tilt)]
    short = jnp.concatenate(short + [jnp.zeros((2, channels), F32)], axis=0).astype(BF16)
    short = jnp.dot(short, chosen, preferred_element_type=F32)
    quarter = lax.broadcasted_iota(jnp.int32, (1, lanes), 1) // GN_GROUPS
    nothing = jnp.zeros((1, lanes), F32)
    left = []
    for part in range(2):
        mixed = [
            jnp.where(quarter == part, short[3 + q : 4 + q], jnp.where(quarter == part + 2, short[q : q + 1], 0.0))
            for q in range(3)
        ]
        left += [
            jnp.concatenate([mixed[q]] * (3 - q) + [nothing] * q, axis=1) for q in range(3)
        ]
    left = jnp.concatenate(left + [jnp.zeros((2, 3 * lanes), F32)], axis=0).astype(BF16)
    moved = jnp.dot(left, table_of[...], preferred_element_type=F32)
    moved = jnp.concatenate(
        [jnp.sum(moved[3 * part : 3 * part + 3], axis=0, keepdims=True) for part in range(2)], axis=0
    )

    spread = (total(3) - moved) / cells
    for p in range(rows):
        at = pl.ds(p * cols, cols)
        back = gradient[p] * slope[at]
        result = inverse_first * (back - spread[0:1] - nfirst[at] * spread[1:2])
        igrad[0, p] = result.astype(BF16)

    settle(2 * n * (m - 1), pair_recv.at[1])
    sums = [whole(k) for k in range(m)]
    for part in range(2):
        lines = [value[part : part + 1] for value in sums]
        thirds = [[piece.astype(F32) for piece in pieces(line)] for line in lines]
        columns = slice(part * channels, (part + 1) * channels)
        right_out[:, columns] = stacked(
            [thirds[k][q] for q in (0, 1, 0, 2, 1, 0) for k in range(m)]
        ).astype(BF16)
        bgrad[:, columns] = add_up(lines)

    lines = 2 * (4 * (n - 1) + len(others)) + (m - 1) * acts.shape[2] // channels
    lines += maps.shape[1] * maps.shape[2] // channels * (n - 1)
    settle(lines, None)
    for which, buffer in enumerate((images, images, cot)):

        @pl.when(above)
        def _():
            halo_copy(which, buffer, True).wait_send()

        @pl.when(below)
        def _():
            halo_copy(which, buffer, False).wait_send()


def finish(branch, igrad, left, right, bgrad, branch_out, igrad_out, wgrad_out, bgrad_out, wgrad, sem):
    copies = [
        pltpu.make_async_copy(source, target, sem.at[k])
        for k, (source, target) in enumerate(
            [(igrad, igrad_out), (branch, branch_out), (bgrad, bgrad_out)]
        )
    ]
    for copy in copies:
        copy.start()
    height = wgrad.shape[0] // PARTS
    for k in range(PARTS):
        at = pl.ds(k * height, height)
        wgrad[at] = jnp.dot(left[at], right[...], preferred_element_type=F32)
        copy = pltpu.make_async_copy(wgrad.at[at], wgrad_out.at[at], sem.at[3 + k])
        copy.start()
        copies.append(copy)
    for copy in copies:
        copy.wait()


def body(
    n, m,
    images, cotangent, timesteps, class_ids, norm_gain, norm_bias, conv_first, conv_second,
    time_weight, time_bias, class_table, adaptive_weight, adaptive_bias,
):
    count, rows, cols, channels = images.shape
    assert count == 1 and rows >= REACH
    emb = time_weight.shape[1]
    vmem = pl.BlockSpec(memory_space=pltpu.VMEM)
    anywhere = pl.BlockSpec(memory_space=pl.ANY)
    padded = rows + 2 * REACH
    stack = 6 * m + (-6 * m) % 16
    own, more, most = rows * cols, (rows + 2) * cols, padded * cols
    dma = pltpu.SemaphoreType.DMA
    results = pl.pallas_call(
        functools.partial(kernel, n, m),
        out_shape=(
            jax.ShapeDtypeStruct(images.shape, BF16),
            jax.ShapeDtypeStruct(images.shape, BF16),
            jax.ShapeDtypeStruct((emb, stack), BF16),
            jax.ShapeDtypeStruct((stack, 2 * channels), BF16),
            jax.ShapeDtypeStruct((1, 2 * channels), F32),
        ),
        in_specs=[pl.BlockSpec(memory_space=pltpu.SMEM)] * 2
        + [pl.BlockSpec(memory_space=pltpu.HBM)] * 11,
        out_specs=(vmem,) * 5,
        scratch_shapes=[
            pltpu.VMEM((padded, cols, channels), BF16),
            pltpu.VMEM((padded, cols, channels), BF16),
            pltpu.VMEM(conv_first.shape, BF16),
            pltpu.VMEM(conv_second.shape, BF16),
            pltpu.VMEM(conv_first.shape, BF16),
            pltpu.VMEM(conv_second.shape, BF16),
            pltpu.VMEM(time_weight.shape, BF16),
            pltpu.VMEM(class_table.shape, BF16),
            pltpu.VMEM(adaptive_weight.shape, BF16),
            pltpu.VMEM((1, channels), F32),
            pltpu.VMEM((1, channels), F32),
            pltpu.VMEM((1, emb), F32),
            pltpu.VMEM((1, 2 * channels), F32),
            pltpu.VMEM((most, channels), BF16),
            pltpu.VMEM((more, channels), BF16),
            pltpu.VMEM((more, channels), BF16),
            pltpu.VMEM((more, channels), BF16),
            pltpu.VMEM((more, 3 * channels), BF16),
            pltpu.VMEM((2 * channels, own), BF16),
            pltpu.VMEM((12 * GN_GROUPS, channels), BF16),
            pltpu.VMEM((more, channels), F32),
            pltpu.VMEM((max(more, 2 * own), channels), F32),
            pltpu.VMEM((more, channels), F32),
            pltpu.VMEM((more, channels), F32),
            pltpu.VMEM((own, channels), F32),
            pltpu.VMEM((own, channels), F32),
            pltpu.VMEM((4, n, 2, channels), F32),
            pltpu.VMEM((m, 1, emb), F32),
            pltpu.VMEM((m, n, 2, channels), F32),
            pltpu.VMEM((n, GN_GROUPS, 4 * GN_GROUPS), F32),
            pltpu.VMEM((SPARE, 1, channels), F32),
            dma((11,)),
            dma((3, 2)),
            dma((3, 2)),
            dma((1,)),
            dma((4,)),
            dma((1,)),
            dma((2,)),
            dma((1,)),
        ],
        compiler_params=pltpu.CompilerParams(
            collective_id=0, has_side_effects=True, vmem_limit_bytes=GRANT
        ),
    )(
        timesteps, class_ids,
        *(
            pltpu.with_memory_space_constraint(operand, pltpu.HBM)
            for operand in (
                norm_gain[None], norm_bias[None], time_bias[None],
                adaptive_bias[None], images, cotangent, conv_first, conv_second, time_weight,
                class_table, adaptive_weight,
            )
        )
    )
    branch, igrad, wgrad, bgrad = pl.pallas_call(
        finish,
        out_shape=(
            jax.ShapeDtypeStruct(images.shape, BF16),
            jax.ShapeDtypeStruct(images.shape, BF16),
            jax.ShapeDtypeStruct((emb, 2 * channels), F32),
            jax.ShapeDtypeStruct((1, 2 * channels), F32),
        ),
        in_specs=[anywhere] * 2 + [vmem] * 2 + [anywhere],
        out_specs=(anywhere,) * 4,
        scratch_shapes=[pltpu.VMEM((emb, 2 * channels), F32), dma((3 + PARTS,))],
        compiler_params=pltpu.CompilerParams(vmem_limit_bytes=GRANT),
    )(*results)
    return branch, igrad, wgrad, bgrad[0]


def solution(mesh):
    return jax.shard_map(
        functools.partial(body, mesh.shape["tile"], mesh.shape["image"]),
        mesh=mesh,
        in_specs=(
            P(("groups", "image"), "tile", None, None),
            P(("groups", "image"), "tile", None, None),
            P(("groups", "image")),
            P(("groups", "image")),
            P(),
            P(),
            P(),
            P(),
            P(None, "tile"),
            P("tile"),
            P(None, "tile"),
            P("tile", None),
            P(),
        ),
        out_specs=(
            P(("groups", "image"), "tile", None, None),
            P(("groups", "image"), "tile", None, None),
            P(("groups", "tile"), None),
            P("groups"),
        ),
        check_vma=False,
    )
```

```python
import functools
import math

import jax
import jax.numpy as jnp
from jax import lax
from jax.experimental import pallas as pl
from jax.experimental.pallas import tpu as pltpu
from jax.sharding import PartitionSpec as P

GN_GROUPS = 32
EPSILON = 1e-05
MESH = pl.DeviceIdType.MESH
F32 = jnp.float32
BF16 = jnp.bfloat16
GRANT = 24 << 20
REACH = 2
PARTS = 2
SPARE = 128
HIGHEST = lax.Precision.HIGHEST


def group_spread(values, width):
    count = values.shape[-1]
    place = lax.broadcasted_iota(jnp.int32, values.shape, values.ndim - 1) % width
    terms = [values]
    for step in range(1, width):
        ahead = pltpu.roll(values, count - step, values.ndim - 1)
        wrapped = pltpu.roll(values, width - step, values.ndim - 1)
        terms.append(jnp.where(place + step < width, ahead, wrapped))
    while len(terms) > 1:
        pairs = [left + right for left, right in zip(terms[::2], terms[1::2])]
        terms = pairs + terms[2 * len(pairs) :]
    return terms[0]


def silu_slope(pre, sigma):
    return sigma * (1.0 + pre * (1.0 - sigma))


def column_sums(first, second):
    return jnp.concatenate(
        [jnp.sum(first, axis=0, keepdims=True), jnp.sum(second, axis=0, keepdims=True)], axis=0
    )


def kernel(
    n, m,
    steps_ref, ids_ref, gain_hbm, bias_hbm, tbias_hbm, abias_hbm,
    images_hbm, cot_hbm, first_hbm, second_hbm, tweight_hbm, table_hbm, aweight_hbm,
    branch, igrad, left_out, right_out, bgrad,
    images, cot, first, second, first_back, second_back, tweight, table, aweight,
    gain_ref, bias_ref, tbias_ref, abias_ref,
    near_first, near_second, near_hidden, near_scaled, wide_plain, tall, table_of,
    hidden, gact, nsecond, gpre, nfirst, slope,
    slots, acts, pairs, maps, spare,
    load_sem, halo_send, halo_recv, send_sem, slot_recv, act_recv, pair_recv, map_recv,
):
    me = lax.axis_index("tile")
    mine = lax.axis_index("image")
    rows, cols, channels = images_hbm.shape[1:]
    width = channels // GN_GROUPS
    cells = float(rows * cols * n * width)
    own = rows * cols
    above, below = me > 0, me < n - 1

    def load(source, target, k):
        return pltpu.make_async_copy(source, target, load_sem.at[k])

    loads = [
        load(images_hbm.at[0], images.at[pl.ds(REACH, rows)], 0),
        load(cot_hbm.at[0], cot.at[pl.ds(REACH, rows)], 1),
        load(tweight_hbm, tweight, 2),
        load(table_hbm, table, 3),
        load(aweight_hbm, aweight, 4),
        load(first_hbm, first, 5),
        load(second_hbm, second, 6),
        load(gain_hbm, gain_ref, 7),
        load(bias_hbm, bias_ref, 8),
        load(tbias_hbm, tbias_ref, 9),
        load(abias_hbm, abias_ref, 10),
    ]
    loads[0].start()
    barrier = pltpu.get_barrier_semaphore()
    for k in reversed(range(1, n)):
        pl.semaphore_signal(
            barrier, inc=1, device_id={"tile": lax.rem(me + k, n)}, device_id_type=MESH
        )
    for k in range(1, m):
        pl.semaphore_signal(
            barrier, inc=1, device_id={"image": lax.rem(mine + k, m)}, device_id_type=MESH
        )
    for k in (7, 8, 5, 2, 3, 4, 9, 10, 1, 6):
        loads[k].start()

    def remote(buffer, slot, receive, device):
        return pltpu.make_async_remote_copy(
            src_ref=buffer.at[slot],
            dst_ref=buffer.at[slot],
            send_sem=send_sem.at[0],
            recv_sem=receive,
            device_id=device,
            device_id_type=MESH,
        )

    def settle(lines, receive):
        while lines:
            part = min(lines, spare.shape[0])
            block = spare.at[pl.ds(0, part)]
            copy = pltpu.make_async_remote_copy(
                src_ref=block,
                dst_ref=block,
                send_sem=send_sem.at[0],
                recv_sem=send_sem.at[0] if receive is None else receive,
                device_id={"tile": lax.rem(me + 1, n)},
                device_id_type=MESH,
            )
            if receive is None:
                copy.wait_send()
            else:
                copy.wait_recv()
            lines -= part

    def tile_peer(k):
        return {"tile": lax.rem(me + k, n)}

    def share(stage, value):
        slots[stage, me] = value
        for k in range(1, n):
            remote(slots.at[stage], me, slot_recv.at[stage], tile_peer(k)).start()

    def total(stage):
        settle(2 * (n - 1), slot_recv.at[stage])
        summed = slots[stage, 0]
        for k in range(1, n):
            summed = summed + slots[stage, k]
        return summed

    HALOS = ((REACH, rows + REACH, rows + REACH - 1, REACH - 1, 1),
             (REACH + 1, rows + REACH + 1, rows + REACH - 2, REACH - 2, 1),
             (REACH, rows + REACH, rows, 0, REACH))

    def halo_copy(which, buffer, up):
        up_from, up_to, down_from, down_to, count = HALOS[which]
        source, target = (up_from, up_to) if up else (down_from, down_to)
        return pltpu.make_async_remote_copy(
            src_ref=buffer.at[pl.ds(source, count)],
            dst_ref=buffer.at[pl.ds(target, count)],
            send_sem=halo_send.at[which, int(up)],
            recv_sem=halo_recv.at[which, int(up)],
            device_id={"tile": me - 1 if up else me + 1},
            device_id_type=MESH,
        )

    def halo_start(which, buffer):
        _, low, _, high, count = HALOS[which]

        @pl.when(above)
        def _():
            halo_copy(which, buffer, True).start()

        @pl.when(below)
        def _():
            halo_copy(which, buffer, False).start()

        @pl.when(jnp.logical_not(above))
        def _():
            buffer[pl.ds(high, count)] = jnp.zeros((count, cols, channels), BF16)

        @pl.when(jnp.logical_not(below))
        def _():
            buffer[pl.ds(low, count)] = jnp.zeros((count, cols, channels), BF16)

    def halo_wait(which, buffer):
        @pl.when(below)
        def _():
            halo_copy(which, buffer, True).wait_recv()

        @pl.when(above)
        def _():
            halo_copy(which, buffer, False).wait_recv()

    column = lax.broadcasted_iota(jnp.int32, (cols, channels), 0)

    def widen(wide, row, values):
        before = jnp.where(column == 0, 0.0, pltpu.roll(values, 1, 0))
        after = jnp.where(column == cols - 1, 0.0, pltpu.roll(values, cols - 1, 0))
        at = pl.ds(row * cols, cols)
        wide[at, 0:channels] = before.astype(BF16)
        wide[at, channels : 2 * channels] = values.astype(BF16)
        wide[at, 2 * channels : 3 * channels] = after.astype(BF16)

    edge = jnp.zeros((1, channels), F32)

    def shifted(parts, count):
        lines = []
        for p in range(count):
            before, at, after = [part[p * cols : (p + 1) * cols] for part in parts]
            before = jnp.concatenate([edge, before[: cols - 1]], axis=0)
            after = jnp.concatenate([after[1:], edge], axis=0)
            lines.append(at + (before + after))
        return lines

    def conv(near, starts, count, weight):
        parts = [None] * 3
        for j in (0, 2, 1):
            for i in range(3):
                lines = [near[pl.ds((start + i) * cols, count * cols), :] for start in starts]
                product = jnp.dot(
                    lines[0] if len(lines) == 1 else jnp.concatenate(lines, axis=0),
                    weight[i, j],
                    preferred_element_type=F32,
                )
                parts[j] = product if i == 0 else parts[j] + product
        return shifted(parts, count * len(starts))

    def conv_back(lines_of, count, weight):
        parts = [None] * 3
        for j in (0, 2, 1):
            for i in range(3):
                product = jnp.dot(
                    lines_of(i), weight[2 - i, 2 - j], preferred_element_type=F32
                )
                parts[j] = product if i == 0 else parts[j] + product
        return shifted(parts, count)

    def window(near, start, count):
        return lambda i: near[pl.ds((start + i) * cols, count * cols), :]

    halves = [(0, rows // 2), (rows // 2, rows - rows // 2)]

    def pieces(values):
        parts = []
        for _ in range(3):
            part = values.astype(BF16)
            parts.append(part)
            values = values - part.astype(F32)
        return parts

    def moments(summed):
        spread = summed / cells
        centre = spread[0:1]
        variance = jnp.maximum(spread[1:2] - centre * centre, 0.0)
        return centre, lax.rsqrt(variance + EPSILON)

    def add_up(parts):
        return functools.reduce(jnp.add, parts)

    def gathered_sums(lines):
        folded = [
            add_up([jnp.sum(line[q].reshape(cols // 8, 8, channels), axis=0) for line in lines])
            for q in range(2)
        ]
        return column_sums(*folded)

    loads[0].wait()
    sums = []
    for p in range(rows):
        line = images[REACH + p].astype(F32)
        sums.append((line, line * line))
    sums = group_spread(gathered_sums(sums), width)
    pl.semaphore_wait(barrier, n - 1 + m - 1)
    share(0, sums)
    halo_start(0, images)
    halo_start(1, images)

    for k in (2, 3, 4, 7, 8, 9, 10):
        loads[k].wait()
    half = tweight.shape[0] // 2
    index = lax.broadcasted_iota(jnp.int32, (half, 1), 0).astype(F32)
    angles = steps_ref[0].astype(F32) * jnp.exp(-math.log(10000.0) * index / half)
    pre_time = (
        jnp.sum(jnp.cos(angles) * tweight[0:half].astype(F32), axis=0, keepdims=True)
        + jnp.sum(jnp.sin(angles) * tweight[half:].astype(F32), axis=0, keepdims=True)
        + tbias_ref[...]
    )
    entry = lax.broadcasted_iota(jnp.int32, table.shape, 0) == ids_ref[0]
    picked = jnp.sum(jnp.where(entry, table[...].astype(F32), 0.0), axis=0, keepdims=True)
    embedding = pre_time * jax.nn.sigmoid(pre_time) + picked
    activated = embedding * jax.nn.sigmoid(embedding)
    acts[mine] = activated
    for k in range(1, m):
        remote(acts, mine, act_recv.at[0], {"image": lax.rem(mine + k, m)}).start()
    partial = jnp.dot(
        jnp.broadcast_to(activated, (8, activated.shape[1])),
        aweight[...].astype(F32),
        precision=HIGHEST,
        preferred_element_type=F32,
    )[0:1]
    share(1, jnp.concatenate([partial[:, :channels], partial[:, channels:]], axis=0))

    loads[1].wait()
    halo_start(2, cot)

    for k, weight, turned in ((5, first, first_back), (6, second, second_back)):
        loads[k].wait()
        for i in range(3):
            for j in range(3):
                turned[i, j] = weight[i, j].T
    halo_wait(0, images)
    gain, bias = gain_ref[...], bias_ref[...]
    centre, inverse_first = moments(total(0))
    stretch = 0.5 * inverse_first * gain
    offset = 0.5 * bias - centre * stretch

    def first_row(row, inside):
        lean = images[row].astype(F32) * stretch + offset
        value = lean * (1.0 + jnp.tanh(lean))
        if inside is not None:
            value = jnp.where(inside, value, 0.0)
        near_first[pl.ds(row * cols, cols)] = value.astype(BF16)

    centre_rows, done = [], 0
    for start, count in halves:
        while done < start + count + 2:
            row = REACH - 1 + done
            first_row(row, above if done == 0 else below if done == rows + 1 else None)
            done += 1
        centre_rows += [
            line.astype(BF16).astype(F32)
            for line in conv(near_first, (1 + start,), count, first)
        ]
    share(2, gathered_sums([(line, line * line) for line in centre_rows]))
    for p, line in enumerate(centre_rows):
        hidden[pl.ds((1 + p) * cols, cols)] = line

    halo_wait(1, images)
    first_row(0, above)
    first_row(rows + 2 * REACH - 1, below)
    for row, line in zip((0, rows + 1), conv(near_first, (0, rows + 1), 1, first)):
        hidden[pl.ds(row * cols, cols)] = line.astype(BF16).astype(F32)

    whole_rows, first_cells, last_cells = [[], []], [[], []], [[], []]
    for p in range(rows):
        at = pl.ds(p * cols, cols)
        line = images[REACH + p].astype(F32)
        lean = line * stretch + offset
        bend = jnp.tanh(lean)
        steep = (0.5 * gain) * ((1.0 + bend) * (1.0 + lean * (1.0 - bend)))
        line = (line - centre) * inverse_first
        nfirst[at] = line
        slope[at] = steep
        for part, lines in enumerate((steep, steep * line)):
            lines = lines.astype(BF16).astype(F32)
            gact[at if part == 0 else pl.ds((rows + p) * cols, cols)] = lines
            whole_rows[part].append(jnp.sum(lines, axis=0, keepdims=True))
            first_cells[part].append(lines[0:1])
            last_cells[part].append(lines[cols - 1 : cols])
    edges = []
    for part in range(2):
        tall[pl.ds(part * channels, channels), :] = gact[pl.ds(part * own, own)].T.astype(BF16)
        kept = [
            [a - b for a, b in zip(whole_rows[part], first_cells[part])],
            whole_rows[part],
            [a - b for a, b in zip(whole_rows[part], last_cells[part])],
        ]
        grid = []
        for i in range(3):
            for j in range(3):
                value = add_up(kept[j])
                if i == 0:
                    value = value - jnp.where(above, 0.0, kept[j][0])
                elif i == 2:
                    value = value - jnp.where(below, 0.0, kept[j][rows - 1])
                grid.append(value)
        edges.append(grid)
    for row in range(rows + 2):
        lines = hidden[pl.ds(row * cols, cols)]
        if row == 0:
            lines = jnp.where(above, lines, 0.0)
        elif row == rows + 1:
            lines = jnp.where(below, lines, 0.0)
        widen(wide_plain, row, lines)
    same = (
        lax.broadcasted_iota(jnp.int32, (GN_GROUPS, channels), 1) // width
        == lax.broadcasted_iota(jnp.int32, (GN_GROUPS, channels), 0)
    )
    products, constants = [None, None], None
    for i in range(3):
        for j in range(3):
            taps = first[2 - i, 2 - j]
            wide_taps = taps.astype(F32)
            near = wide_plain[pl.ds(i * cols, own), j * channels : (j + 1) * channels]
            for part in range(2):
                product = wide_taps * jnp.dot(
                    tall[pl.ds(part * channels, channels), :], near, preferred_element_type=F32
                )
                products[part] = product if i + j == 0 else products[part] + product
            spread_rows = [
                jnp.where(same, piece.astype(F32), 0.0)
                for part in range(2)
                for piece in pieces(edges[part][3 * i + j])
            ]
            product = jnp.dot(
                jnp.concatenate(spread_rows, axis=0).astype(BF16), taps, preferred_element_type=F32
            )
            constants = product if i + j == 0 else constants + product
    blocks = [
        jnp.sum(product.reshape(GN_GROUPS, width, channels), axis=1) for product in products
    ] + [
        add_up(
            [constants[(3 * part + q) * GN_GROUPS : (3 * part + q + 1) * GN_GROUPS] for q in range(3)]
        )
        for part in range(2)
    ]
    columns_of = [pieces(block) for block in blocks]
    lanes = 4 * GN_GROUPS
    gathered = None
    for quarter in range(4):
        row = lax.broadcasted_iota(jnp.int32, (channels, lanes), 0)
        lane = lax.broadcasted_iota(jnp.int32, (channels, lanes), 1)
        chosen = jnp.where(row // width + quarter * GN_GROUPS == lane, 1.0, 0.0).astype(BF16)
        product = jnp.dot(
            jnp.concatenate(columns_of[quarter], axis=0), chosen, preferred_element_type=F32
        )
        gathered = product if gathered is None else gathered + product
    maps[me] = add_up([gathered[q * GN_GROUPS : (q + 1) * GN_GROUPS] for q in range(3)])
    for k in range(1, n):
        remote(maps, me, map_recv.at[0], tile_peer(k)).start()

    halo_wait(2, cot)
    count = (rows + 2) // 2
    for start in (0, rows + 2 - count):
        spans = lambda i: cot[pl.ds(start + i, count)].reshape(count * cols, channels)
        for p, line in enumerate(conv_back(spans, count, second_back)):
            gact[pl.ds((start + p) * cols, cols)] = line

    modulation = total(1)
    factor = 1.0 + (modulation[0:1] + abias_ref[:, :channels])
    shift = modulation[1:2] + abias_ref[:, channels:]
    centre, inverse_second = moments(group_spread(total(2), width))

    def second_row(row):
        at = pl.ds(row * cols, cols)
        normed = (hidden[at] - centre) * inverse_second
        lean = normed * (0.5 * factor) + 0.5 * shift
        bend = jnp.tanh(lean)
        rise = 1.0 + bend
        back = gact[at] * (0.5 * rise * (1.0 + lean * (1.0 - bend)))
        nsecond[at] = normed
        gact[at] = lean * rise
        gpre[at] = back
        return back * normed, back

    pairs[mine, me] = gathered_sums([second_row(1 + p) for p in range(rows)])
    others = [(k, step) for step in range(m) for k in range(n) if k or step]
    for k, step in others:
        remote(
            pairs.at[mine], me, pair_recv.at[min(step, 1)],
            {"tile": lax.rem(me + k, n), "image": lax.rem(mine + step, m)},
        ).start()

    scale = factor * inverse_second
    second_row(0)
    second_row(rows + 1)

    def masked(row, values):
        if row == 0:
            return jnp.where(above, values, 0.0)
        if row == rows + 1:
            return jnp.where(below, values, 0.0)
        return values

    sums, done = [], 0
    for start, count in halves:
        while done < start + count + 2:
            at = pl.ds(done * cols, cols)
            back = gpre[at] * scale
            gpre[at] = back
            near_scaled[at] = masked(done, back).astype(BF16)
            done += 1
        for p, line in enumerate(conv_back(window(near_scaled, start, count), count, first_back)):
            at = pl.ds((start + p) * cols, cols)
            early = line * slope[at]
            sums.append((early, early * nfirst[at]))
    share(3, group_spread(gathered_sums(sums), width))

    for row in range(rows + 2):
        at = pl.ds(row * cols, cols)
        near_second[at] = masked(row, gact[at]).astype(BF16)
    for start, count in halves:
        for p, line in enumerate(conv(near_second, (start,), count, second)):
            branch[0, start + p] = line.astype(BF16)

    settle(maps.shape[1] * maps.shape[2] // channels * (n - 1), map_recv.at[0])
    summed = add_up([maps[k] for k in range(n)])
    spread_of = jnp.where(same, 1.0, 0.0)
    for q, piece in enumerate(pieces(summed)):
        table_of[pl.ds(q * lanes, lanes), :] = lax.dot_general(
            piece.astype(F32), spread_of, (((0,), (0,)), ((), ())), preferred_element_type=F32
        ).astype(BF16)

    settle((m - 1) * acts.shape[2] // channels, act_recv.at[0])
    extra = (-2 * m) % 8

    def stacked(parts):
        if extra:
            parts = parts + [jnp.zeros((extra, parts[0].shape[1]), F32)]
        return jnp.concatenate(parts, axis=0)

    blank = jnp.zeros((1, acts.shape[2]), F32)
    for part in range(2):
        lines = [acts[k] if q == part else blank for k in range(m) for q in range(2)]
        thirds = [piece.astype(F32) for piece in pieces(stacked(lines))]
        left_out[part] = jnp.concatenate(
            [thirds[q] for q in (0, 0, 1, 0, 1, 2)], axis=0
        ).T.astype(BF16)

    settle(2 * (n - 1), pair_recv.at[0])

    def whole(image):
        return add_up([pairs[image, k] for k in range(n)])

    spread = group_spread(whole(mine) * factor, width) / cells
    paired_mean, plain_mean = inverse_second * spread[0:1], inverse_second * spread[1:2]
    gradient, done = [], 0
    for start, count in halves:
        while done < start + count + 2:
            at = pl.ds(done * cols, cols)
            back = gpre[at] - plain_mean - nsecond[at] * paired_mean
            near_hidden[at] = masked(done, back).astype(BF16)
            done += 1
        gradient += conv_back(window(near_hidden, start, count), count, first_back)

    tilt = paired_mean * inverse_second
    level = plain_mean - tilt * centre
    row = lax.broadcasted_iota(jnp.int32, (channels, lanes), 0)
    lane = lax.broadcasted_iota(jnp.int32, (channels, lanes), 1)
    chosen = jnp.where(lax.rem(lane, GN_GROUPS) * width == row, 1.0, 0.0).astype(BF16)
    short = [piece.astype(F32) for piece in pieces(level) + pieces(tilt)]
    short = jnp.concatenate(short + [jnp.zeros((2, channels), F32)], axis=0).astype(BF16)
    short = jnp.dot(short, chosen, preferred_element_type=F32)
    quarter = lax.broadcasted_iota(jnp.int32, (1, lanes), 1) // GN_GROUPS
    nothing = jnp.zeros((1, lanes), F32)
    left = []
    for part in range(2):
        mixed = [
            jnp.where(quarter == part, short[3 + q : 4 + q], jnp.where(quarter == part + 2, short[q : q + 1], 0.0))
            for q in range(3)
        ]
        left += [
            jnp.concatenate([mixed[q]] * (3 - q) + [nothing] * q, axis=1) for q in range(3)
        ]
    left = jnp.concatenate(left + [jnp.zeros((2, 3 * lanes), F32)], axis=0).astype(BF16)
    moved = jnp.dot(left, table_of[...], preferred_element_type=F32)
    moved = jnp.concatenate(
        [jnp.sum(moved[3 * part : 3 * part + 3], axis=0, keepdims=True) for part in range(2)], axis=0
    )

    spread = (total(3) - moved) / cells
    for p in range(rows):
        at = pl.ds(p * cols, cols)
        back = gradient[p] * slope[at]
        result = inverse_first * (back - spread[0:1] - nfirst[at] * spread[1:2])
        igrad[0, p] = result.astype(BF16)

    settle(2 * n * (m - 1), pair_recv.at[1])
    sums = [whole(k) for k in range(m)]
    thirds = [piece.astype(F32) for piece in pieces(stacked(sums))]
    right_out[...] = jnp.concatenate([thirds[q] for q in (0, 1, 0, 2, 1, 0)], axis=0).astype(BF16)
    everything = add_up(sums)
    for part in range(2):
        bgrad[:, part * channels : (part + 1) * channels] = everything[part : part + 1]

    lines = 2 * (4 * (n - 1) + len(others)) + (m - 1) * acts.shape[2] // channels
    lines += maps.shape[1] * maps.shape[2] // channels * (n - 1)
    settle(lines, None)
    for which, buffer in enumerate((images, images, cot)):

        @pl.when(above)
        def _():
            halo_copy(which, buffer, True).wait_send()

        @pl.when(below)
        def _():
            halo_copy(which, buffer, False).wait_send()


def finish(branch, igrad, left, right, bgrad, branch_out, igrad_out, wgrad_out, bgrad_out, wgrad, sem):
    copies = [
        pltpu.make_async_copy(source, target, sem.at[k])
        for k, (source, target) in enumerate(
            [(igrad, igrad_out), (branch, branch_out), (bgrad, bgrad_out)]
        )
    ]
    for copy in copies:
        copy.start()
    height, width = wgrad.shape[0] // PARTS, right.shape[1]
    for k in range(PARTS):
        at = pl.ds(k * height, height)
        for part in range(2):
            wgrad[at, part * width : (part + 1) * width] = jnp.dot(
                left[part, at], right[...], preferred_element_type=F32
            )
        copy = pltpu.make_async_copy(wgrad.at[at], wgrad_out.at[at], sem.at[3 + k])
        copy.start()
        copies.append(copy)
    for copy in copies:
        copy.wait()


def body(
    n, m,
    images, cotangent, timesteps, class_ids, norm_gain, norm_bias, conv_first, conv_second,
    time_weight, time_bias, class_table, adaptive_weight, adaptive_bias,
):
    count, rows, cols, channels = images.shape
    assert count == 1 and rows >= REACH
    emb = time_weight.shape[1]
    vmem = pl.BlockSpec(memory_space=pltpu.VMEM)
    anywhere = pl.BlockSpec(memory_space=pl.ANY)
    padded = rows + 2 * REACH
    stack = 6 * (2 * m + (-2 * m) % 8)
    own, more, most = rows * cols, (rows + 2) * cols, padded * cols
    dma = pltpu.SemaphoreType.DMA
    results = pl.pallas_call(
        functools.partial(kernel, n, m),
        out_shape=(
            jax.ShapeDtypeStruct(images.shape, BF16),
            jax.ShapeDtypeStruct(images.shape, BF16),
            jax.ShapeDtypeStruct((2, emb, stack), BF16),
            jax.ShapeDtypeStruct((stack, channels), BF16),
            jax.ShapeDtypeStruct((1, 2 * channels), F32),
        ),
        in_specs=[pl.BlockSpec(memory_space=pltpu.SMEM)] * 2
        + [pl.BlockSpec(memory_space=pltpu.HBM)] * 11,
        out_specs=(vmem,) * 5,
        scratch_shapes=[
            pltpu.VMEM((padded, cols, channels), BF16),
            pltpu.VMEM((padded, cols, channels), BF16),
            pltpu.VMEM(conv_first.shape, BF16),
            pltpu.VMEM(conv_second.shape, BF16),
            pltpu.VMEM(conv_first.shape, BF16),
            pltpu.VMEM(conv_second.shape, BF16),
            pltpu.VMEM(time_weight.shape, BF16),
            pltpu.VMEM(class_table.shape, BF16),
            pltpu.VMEM(adaptive_weight.shape, BF16),
            pltpu.VMEM((1, channels), F32),
            pltpu.VMEM((1, channels), F32),
            pltpu.VMEM((1, emb), F32),
            pltpu.VMEM((1, 2 * channels), F32),
            pltpu.VMEM((most, channels), BF16),
            pltpu.VMEM((more, channels), BF16),
            pltpu.VMEM((more, channels), BF16),
            pltpu.VMEM((more, channels), BF16),
            pltpu.VMEM((more, 3 * channels), BF16),
            pltpu.VMEM((2 * channels, own), BF16),
            pltpu.VMEM((12 * GN_GROUPS, channels), BF16),
            pltpu.VMEM((more, channels), F32),
            pltpu.VMEM((max(more, 2 * own), channels), F32),
            pltpu.VMEM((more, channels), F32),
            pltpu.VMEM((more, channels), F32),
            pltpu.VMEM((own, channels), F32),
            pltpu.VMEM((own, channels), F32),
            pltpu.VMEM((4, n, 2, channels), F32),
            pltpu.VMEM((m, 1, emb), F32),
            pltpu.VMEM((m, n, 2, channels), F32),
            pltpu.VMEM((n, GN_GROUPS, 4 * GN_GROUPS), F32),
            pltpu.VMEM((SPARE, 1, channels), F32),
            dma((11,)),
            dma((3, 2)),
            dma((3, 2)),
            dma((1,)),
            dma((4,)),
            dma((1,)),
            dma((2,)),
            dma((1,)),
        ],
        compiler_params=pltpu.CompilerParams(
            collective_id=0, has_side_effects=True, vmem_limit_bytes=GRANT
        ),
    )(
        timesteps, class_ids,
        *(
            pltpu.with_memory_space_constraint(operand, pltpu.HBM)
            for operand in (
                norm_gain[None], norm_bias[None], time_bias[None],
                adaptive_bias[None], images, cotangent, conv_first, conv_second, time_weight,
                class_table, adaptive_weight,
            )
        )
    )
    branch, igrad, wgrad, bgrad = pl.pallas_call(
        finish,
        out_shape=(
            jax.ShapeDtypeStruct(images.shape, BF16),
            jax.ShapeDtypeStruct(images.shape, BF16),
            jax.ShapeDtypeStruct((emb, 2 * channels), F32),
            jax.ShapeDtypeStruct((1, 2 * channels), F32),
        ),
        in_specs=[anywhere] * 2 + [vmem] * 2 + [anywhere],
        out_specs=(anywhere,) * 4,
        scratch_shapes=[pltpu.VMEM((emb, 2 * channels), F32), dma((3 + PARTS,))],
        compiler_params=pltpu.CompilerParams(vmem_limit_bytes=GRANT),
    )(*results)
    return branch, igrad, wgrad, bgrad[0]


def solution(mesh):
    return jax.shard_map(
        functools.partial(body, mesh.shape["tile"], mesh.shape["image"]),
        mesh=mesh,
        in_specs=(
            P(("groups", "image"), "tile", None, None),
            P(("groups", "image"), "tile", None, None),
            P(("groups", "image")),
            P(("groups", "image")),
            P(),
            P(),
            P(),
            P(),
            P(None, "tile"),
            P("tile"),
            P(None, "tile"),
            P("tile", None),
            P(),
        ),
        out_specs=(
            P(("groups", "image"), "tile", None, None),
            P(("groups", "image"), "tile", None, None),
            P(("groups", "tile"), None),
            P("groups"),
        ),
        check_vma=False,
    )
```
